256 devices in a mesh: tok: 64 (over z, y, core), kv: 4 (over x).
Axes of the slice: x: 4, y: 4, z: 8, core: 2. Of those that a mesh axis runs over, the one named last changes fastest.
Arguments:
- tokens: bfloat16 [16384, 8192], P('tok', 'kv'), may hold values from -6 to 6
- frozen_query: bfloat16 [16384, 8192], P('tok', 'kv')
- trained_keys: bfloat16 [16384, 1024], P('tok', 'kv')
- trained_values: bfloat16 [16384, 1024], P('tok', 'kv'), may hold values from -6 to 6
- frozen_output: bfloat16 [16384, 8192], P('tok', 'kv'), may hold values from -3 to 3
- prompt_key_cache: bfloat16 [2, 256, 1024], P(None, 'kv'), may hold values from -6 to 6
- prompt_value_cache: bfloat16 [2, 256, 1024], P(None, 'kv'), may hold values from -6 to 6
- adapter_down: bfloat16 [256, 64, 8192], P('tok', None, 'kv'), may hold values from -0.0625 to 0.0625
- adapter_up: bfloat16 [256, 64, 8192], P('tok', None, 'kv'), may hold values from -0.75 to 0.75
- row_adapter_index: int32 [2048], replicated, may hold values from 0 to 255, as said below
- row_forget_flag: int32 [2048], replicated, may hold values 0 or 1
- row_prompt_index: int32 [2048], replicated, may hold values from 0 to 1
- row_prompt_length: int32 [2048], replicated, may hold values from 32 to 256, as said below
Outputs:
- grad_down: bfloat16 [256, 64, 8192], P('tok', None, 'kv')
- grad_up: bfloat16 [256, 64, 8192], P('tok', None, 'kv')
The draws below stay inside these ranges and needn't reach their ends.
Inputs may be any that keep to these rules, and one draw needn't show every extreme that they name: `row_adapter_index`: adapter a is held by index a // 4 of tok, its owner. Among the rows of one index of tok (rows i * 32 to i * 32 + 31) at most 2 name adapters of one owner, and this bound is reached. `row_prompt_length`: every index of tok holds a row of length 256.
All inputs are finite; a program needn't handle non-finite values.
Results may differ from the reference program's by a relative error of at most 0.03.
Values may be sent and summed in bfloat16 or wider, within the bound.
No kernel may reach another device: no remote copies, remote signals or barrier semaphores. Data moves between devices by JAX's collectives and lax.ppermute only.
A program may use at most 128 MiB of HBM per device.

```python
import math
import jax
import jax.numpy as jnp
from jax import lax

MODEL_WIDTH = 8192
QUERY_HEADS = 64
KEY_HEADS = 8
HEAD_WIDTH = 128
ADAPTER_RANK = 64
ADP_DEV = 4
ROWS_DEV = 32
QUERY_LENGTH = 8
PROMPT_LENGTH = 256
PROMPT_COUNT = 2
ADAPTER_TOTAL = 256
CAP = 2
SLOTS = 128
ROW_TOTAL = 2048
TOKEN_TOTAL = 16384
N_TOK = 64


def draw_row_adapter_index(key, part):
    key_hot, key_score, key_order, key_local = jax.random.split(key, 4)
    hot_owners = jax.random.permutation(key_hot, N_TOK)[:2].astype(jnp.int32)
    slot_owner = jnp.arange(SLOTS, dtype=jnp.int32) // CAP
    is_hot = jnp.any(slot_owner[:, None] == hot_owners[None, :], axis=1)
    scores = jax.random.randint(key_score, (N_TOK, SLOTS), 0, 4096) + jnp.where(is_hot, 4096, 0)[None, :]
    ranked = scores * SLOTS + jnp.arange(SLOTS, dtype=jnp.int32)[None, :]
    chosen = lax.top_k(ranked, ROWS_DEV)[1]
    owners = chosen // CAP
    shuffle = jax.random.randint(key_order, (N_TOK, ROWS_DEV), 0, 1 << 20) * ROWS_DEV + jnp.arange(ROWS_DEV, dtype=jnp.int32)[None, :]
    order = jnp.argsort(shuffle, axis=1, stable=True)
    owners = jnp.take_along_axis(owners, order, axis=1)
    local_ids = jax.random.randint(key_local, (N_TOK, ROWS_DEV), 0, ADP_DEV)
    return (owners * ADP_DEV + local_ids).reshape(ROW_TOTAL).astype(jnp.int32)


def draw_row_prompt_length(key, part):
    key_len, key_pick = jax.random.split(key, 2)
    lowest = max(1, PROMPT_LENGTH // 8)
    lengths = jax.random.randint(key_len, (N_TOK, ROWS_DEV), lowest, PROMPT_LENGTH + 1)
    longest = jax.random.randint(key_pick, (N_TOK, 1), 0, ROWS_DEV)
    lengths = jnp.where(jnp.arange(ROWS_DEV, dtype=jnp.int32)[None, :] == longest, PROMPT_LENGTH, lengths)
    return lengths.reshape(ROW_TOTAL).astype(jnp.int32)


def drawn_pair(key):
    key_query, random_key_keys = jax.random.split(jax.random.fold_in(key, 11), 2)
    query_rows = jnp.clip(jax.random.normal(key_query, (ROW_TOTAL, QUERY_LENGTH, QUERY_HEADS, HEAD_WIDTH), jnp.float32), -6.0, 6.0)
    random_key_values = 2.0 * jnp.clip(jax.random.normal(random_key_keys, (ROW_TOTAL, QUERY_LENGTH, KEY_HEADS, HEAD_WIDTH), jnp.float32), -6.0, 6.0)
    return (query_rows.reshape(TOKEN_TOTAL, QUERY_HEADS * HEAD_WIDTH), random_key_values.reshape(TOKEN_TOTAL, KEY_HEADS * HEAD_WIDTH))


def draw_frozen_query(key, part):
    return drawn_pair(key)[0].astype(jnp.bfloat16)


def draw_trained_keys(key, part):
    return drawn_pair(key)[1].astype(jnp.bfloat16)


def place_ends(drawn, rng, least, largest):
    dims = drawn.shape
    index_at = [jax.random.randint(jax.random.fold_in(rng, axis), (), 0, dims[axis]) for axis in range(len(dims))]
    drawn = drawn.at[tuple(index_at)].set(least)
    longest = dims.index(max(dims))
    index_at[longest] = (index_at[longest] + 1) % dims[longest]
    return drawn.at[tuple(index_at)].set(largest)


def block_scale(rng, dims, cuts, least, top_value):
    gain, own = 1.0, jax.random.fold_in(rng, 6)
    for dim, parts in cuts:
        steps = jnp.exp(jax.random.uniform(jax.random.fold_in(own, dim), (parts,), jnp.float32, least / len(cuts), top_value / len(cuts)))
        gain = gain * jnp.repeat(steps, dims[dim] // parts).reshape([-1 if axis == dim else 1 for axis in range(len(dims))])
    return gain


def gaussian(key, dims, width, bound, shards=(), kind=jnp.bfloat16):
    gain = block_scale(key, dims, shards, -0.22, 0.18) if shards else 1.0
    values = jax.random.normal(key, dims, jnp.float32) * width * gain
    return jnp.minimum(jnp.maximum(values, -bound), bound).astype(kind)


def setup_inputs(seed: int = 0) -> dict:
    seeds = jax.random.split(jax.random.key(seed), 14)
    tokens = gaussian(seeds[0], (TOKEN_TOTAL, MODEL_WIDTH), 1.0, 6.0, ((0, 64), (1, 4)))
    frozen_query = draw_frozen_query(jax.random.fold_in(seeds[13], 71), 0)
    trained_keys = draw_trained_keys(jax.random.fold_in(seeds[13], 71), 0)
    trained_values = gaussian(seeds[3], (TOKEN_TOTAL, KEY_HEADS * HEAD_WIDTH), 1.0, 6.0, ((0, 64), (1, 4)))
    frozen_output = gaussian(seeds[4], (TOKEN_TOTAL, QUERY_HEADS * HEAD_WIDTH), 0.5, 3.0, ((0, 64), (1, 4)))
    prompt_key_cache = gaussian(seeds[5], (PROMPT_COUNT, PROMPT_LENGTH, KEY_HEADS * HEAD_WIDTH), 1.0, 6.0, ((1, 4),))
    prompt_value_cache = gaussian(seeds[6], (PROMPT_COUNT, PROMPT_LENGTH, KEY_HEADS * HEAD_WIDTH), 1.0, 6.0, ((1, 4),))
    adapter_down = gaussian(seeds[7], (ADAPTER_TOTAL, ADAPTER_RANK, MODEL_WIDTH), MODEL_WIDTH ** -0.5, 0.0625, ((0, 64), (2, 4)))
    adapter_up = gaussian(seeds[8], (ADAPTER_TOTAL, ADAPTER_RANK, QUERY_HEADS * HEAD_WIDTH), ADAPTER_RANK ** -0.5, 0.75, ((0, 64), (2, 4)))
    row_adapter_index = draw_row_adapter_index(jax.random.fold_in(seeds[13], 71), 0)
    row_forget_flag = place_ends((jax.random.randint(seeds[10], (ROW_TOTAL,), 0, 3) < 1).astype(jnp.int32), jax.random.fold_in(seeds[10], 1), 0, 1)
    row_prompt_index = place_ends(jax.random.randint(seeds[11], (ROW_TOTAL,), 0, PROMPT_COUNT), jax.random.fold_in(seeds[11], 1), 0, PROMPT_COUNT - 1).astype(jnp.int32)
    row_prompt_length = draw_row_prompt_length(jax.random.fold_in(seeds[13], 71), 0)
    return dict(tokens=tokens, frozen_query=frozen_query, trained_keys=trained_keys, trained_values=trained_values, frozen_output=frozen_output, prompt_key_cache=prompt_key_cache, prompt_value_cache=prompt_value_cache, adapter_down=adapter_down, adapter_up=adapter_up, row_adapter_index=row_adapter_index, row_forget_flag=row_forget_flag, row_prompt_index=row_prompt_index, row_prompt_length=row_prompt_length)


ADAPTER_SCALE = 0.5

def attend_layer(query_rows, random_key_rows, value_matrix_rows, base_rows, row_loss_weight, row_len):
    answer_len = query_rows.shape[1]
    prompt_len = random_key_rows.shape[1] - answer_len
    inv_root = 1.0 / math.sqrt(query_rows.shape[-1])
    scores = jnp.einsum('rqkgd,rpkd->rkgqp', query_rows.astype(jnp.float32), random_key_rows.astype(jnp.float32)) * inv_root
    places = jnp.arange(prompt_len + answer_len, dtype=jnp.int32)
    answer_pos = jnp.arange(answer_len, dtype=jnp.int32)
    in_prompt = places[None, None, :] < row_len[:, None, None]
    in_answer = places[None, None, :] - prompt_len <= answer_pos[None, :, None]
    visible = jnp.where(places[None, None, :] < prompt_len, in_prompt, in_answer)[:, None, None, :, :]
    masked = jnp.where(visible, scores, -1e+30)
    row_max = lax.optimization_barrier(jnp.max(masked, axis=-1, keepdims=True))
    exp_terms = jnp.where(visible, jnp.exp(masked - row_max), 0.0)
    row_total = lax.optimization_barrier(jnp.sum(exp_terms, axis=-1, keepdims=True))
    probs_f32 = exp_terms / row_total
    probs_low = probs_f32.astype(jnp.bfloat16)
    attn_out = jnp.einsum('rkgqp,rpkd->rqkgd', probs_low.astype(jnp.float32), value_matrix_rows.astype(jnp.float32))
    grad_out = (row_loss_weight[:, None, None, None, None] * (attn_out - base_rows.astype(jnp.float32))).astype(jnp.bfloat16)
    grad_probs = jnp.einsum('rqkgd,rpkd->rkgqp', grad_out.astype(jnp.float32), value_matrix_rows.astype(jnp.float32))
    inner_sum = lax.optimization_barrier(jnp.sum(probs_f32 * grad_probs, axis=-1, keepdims=True))
    grad_scores = (probs_f32 * (grad_probs - inner_sum) * inv_root).astype(jnp.bfloat16)
    query_gradient = jnp.einsum('rkgqp,rpkd->rqkgd', grad_scores.astype(jnp.float32), random_key_rows.astype(jnp.float32))
    return query_gradient.astype(jnp.bfloat16)

def reference(tokens, frozen_query, trained_keys, trained_values, frozen_output, prompt_key_cache, prompt_value_cache, adapter_down, adapter_up, row_adapter_index, row_forget_flag, row_prompt_index, row_prompt_length):
    block_of_rows = math.gcd(ROW_TOTAL, 16)
    head_groups = QUERY_HEADS // KEY_HEADS

    def one_block(carry, block_index):
        down_total, up_total = carry
        first_row = block_index * block_of_rows
        first_token = first_row * QUERY_LENGTH

        def token_row_index(array):
            return lax.dynamic_slice_in_dim(array, first_token, block_of_rows * QUERY_LENGTH, 0).reshape(block_of_rows, QUERY_LENGTH, -1)
        adapter_index = lax.dynamic_slice_in_dim(row_adapter_index, first_row, block_of_rows, 0)
        prompt_index = lax.dynamic_slice_in_dim(row_prompt_index, first_row, block_of_rows, 0)
        forget_ids = lax.dynamic_slice_in_dim(row_forget_flag, first_row, block_of_rows, 0)
        length_index = lax.dynamic_slice_in_dim(row_prompt_length, first_row, block_of_rows, 0)
        token_block = token_row_index(tokens)
        down_weight_rows = adapter_down[adapter_index]
        up_weight_rows = adapter_up[adapter_index]
        rank_projection = jnp.einsum('rqd,rkd->rqk', token_block.astype(jnp.float32), down_weight_rows.astype(jnp.float32)).astype(jnp.bfloat16)
        adapter_delta = (ADAPTER_SCALE * jnp.einsum('sgx,sxl->sgl', rank_projection.astype(jnp.float32), up_weight_rows.astype(jnp.float32))).astype(jnp.bfloat16)
        query_rows = (token_row_index(frozen_query).astype(jnp.float32) + adapter_delta.astype(jnp.float32)).astype(jnp.bfloat16)
        random_key_rows = jnp.concatenate([prompt_key_cache[prompt_index], token_row_index(trained_keys)], axis=1).reshape(block_of_rows, PROMPT_LENGTH + QUERY_LENGTH, KEY_HEADS, HEAD_WIDTH)
        value_matrix_rows = jnp.concatenate([prompt_value_cache[prompt_index], token_row_index(trained_values)], axis=1).reshape(block_of_rows, PROMPT_LENGTH + QUERY_LENGTH, KEY_HEADS, HEAD_WIDTH)
        row_loss_weight = 1.0 - 2.0 * forget_ids.astype(jnp.float32)
        query_gradient = attend_layer(query_rows.reshape(block_of_rows, QUERY_LENGTH, KEY_HEADS, head_groups, HEAD_WIDTH), random_key_rows, value_matrix_rows, token_row_index(frozen_output).reshape(block_of_rows, QUERY_LENGTH, KEY_HEADS, head_groups, HEAD_WIDTH), row_loss_weight, length_index)
        query_gradient = query_gradient.reshape(block_of_rows, QUERY_LENGTH, QUERY_HEADS * HEAD_WIDTH)
        up_weight_part = ADAPTER_SCALE * jnp.einsum('xcz,xco->xzo', rank_projection.astype(jnp.float32), query_gradient.astype(jnp.float32))
        rank_gradient = (ADAPTER_SCALE * jnp.einsum('ylf,yif->yli', query_gradient.astype(jnp.float32), up_weight_rows.astype(jnp.float32))).astype(jnp.bfloat16)
        down_part = jnp.einsum('rqk,rqd->rkd', rank_gradient.astype(jnp.float32), token_block.astype(jnp.float32))
        down_total = down_total.at[adapter_index].add(down_part)
        up_total = up_total.at[adapter_index].add(up_weight_part)
        return ((down_total, up_total), None)
    start = (jnp.zeros((ADAPTER_TOTAL, ADAPTER_RANK, MODEL_WIDTH), jnp.float32), jnp.zeros((ADAPTER_TOTAL, ADAPTER_RANK, QUERY_HEADS * HEAD_WIDTH), jnp.float32))
    (down_total, up_total), _ = lax.scan(one_block, start, jnp.arange(ROW_TOTAL // block_of_rows, dtype=jnp.int32))
    return (down_total.astype(jnp.bfloat16), up_total.astype(jnp.bfloat16))
```

```python
import functools
import math

import jax
import jax.numpy as jnp
from jax import lax
from jax.experimental import pallas as pl
from jax.experimental.pallas import tpu as pltpu
from jax.sharding import PartitionSpec as P

QUERY_HEADS = 64
KEY_HEADS = 8
HEAD_WIDTH = 128
ADAPTER_RANK = 64
QUERY_LENGTH = 8
ADAPTER_SCALE = 0.5
CAP = 2
ROW_BLOCK = 16
VMEM_LIMIT = 56 * 1024 * 1024

_VMEM = pl.BlockSpec(memory_space=pltpu.VMEM)
_SMEM = pl.BlockSpec(memory_space=pltpu.SMEM)
_ANY = pl.BlockSpec(memory_space=pl.ANY)


def params():
    return pltpu.CompilerParams(vmem_limit_bytes=VMEM_LIMIT)


def route_kernel(source_ref, rows_ref, out_ref):
    first = pl.program_id(0) * out_ref.shape[0]
    for j in range(out_ref.shape[0]):
        row = source_ref[first + j]

        @pl.when(row >= 0)
        def _():
            out_ref[j] = rows_ref[row]

        @pl.when(row < 0)
        def _():
            out_ref[j] = jnp.zeros_like(out_ref[j])


def route_rows(source, rows, slots):
    row_count, length, width = rows.shape
    step = 16
    return pl.pallas_call(
        route_kernel,
        grid_spec=pltpu.PrefetchScalarGridSpec(
            num_scalar_prefetch=1,
            grid=(slots // step,),
            in_specs=[pl.BlockSpec((row_count, length, width), lambda i, s: (0, 0, 0))],
            out_specs=pl.BlockSpec((step, length, width), lambda i, s: (i, 0, 0)),
        ),
        out_shape=jax.ShapeDtypeStruct((slots, length, width), rows.dtype),
        compiler_params=params(),
        name="route_rows",
    )(source, rows)


def fold(products, mask):
    kept = products * mask.astype(jnp.float32)
    half = kept[:, :128] + kept[:, 128:]
    return half + pltpu.roll(half, 64, 1)


def low_half(shape):
    return lax.broadcasted_iota(jnp.int32, shape, 1) < 64


def project_kernel(xa_ref, xb_ref, ma_ref, mb_ref, weight_ref, out_ref):
    dims = (((1,), (1,)), ((), ()))
    weight = weight_ref[...]
    first = lax.dot_general(xa_ref[...], weight, dims, preferred_element_type=jnp.float32)
    second = lax.dot_general(xb_ref[...], weight, dims, preferred_element_type=jnp.float32)
    both = jnp.where(
        low_half(out_ref.shape), fold(first, ma_ref[...]), fold(second, mb_ref[...])
    )
    out_ref[...] = both.astype(out_ref.dtype)


def project(x, mask, weight, out_type):
    tokens, width = x.shape
    ranks = weight.shape[0]
    half = tokens // 2
    block = 128
    steps = half // block
    return pl.pallas_call(
        project_kernel,
        grid=(steps,),
        in_specs=[
            pl.BlockSpec((block, width), lambda i: (i, 0)),
            pl.BlockSpec((block, width), lambda i: (i + steps, 0)),
            pl.BlockSpec((block, ranks), lambda i: (i, 0)),
            pl.BlockSpec((block, ranks), lambda i: (i + steps, 0)),
            pl.BlockSpec((ranks, width), lambda i: (0, 0)),
        ],
        out_specs=pl.BlockSpec((block, 128), lambda i: (i, 0)),
        out_shape=jax.ShapeDtypeStruct((half, 128), out_type),
        compiler_params=params(),
        name="project",
    )(x, x, mask, mask, weight)


def spread_of(packed, mask, is_low):
    low = low_half(packed.shape)
    turned = pltpu.roll(packed, 64, 1)
    twice = jnp.where(low, packed, turned) if is_low else jnp.where(low, turned, packed)
    return (jnp.concatenate([twice, twice], axis=1) * mask.astype(jnp.float32)).astype(
        jnp.bfloat16
    )


def delta_kernel(p0, p1, p2, p3, mask_ref, weight_ref, out_ref, spread_ref, *, steps):
    total = (p0[...] + p1[...]) + (p2[...] + p3[...])
    low_rank = total.astype(jnp.bfloat16).astype(jnp.float32)

    def finish(is_low):
        spread = spread_of(low_rank, mask_ref[...], is_low)
        spread_ref[...] = spread
        out_ref[...] = (
            ADAPTER_SCALE
            * jnp.dot(spread, weight_ref[...], preferred_element_type=jnp.float32)
        ).astype(out_ref.dtype)

    pl.when(pl.program_id(0) < steps)(lambda: finish(True))
    pl.when(pl.program_id(0) >= steps)(lambda: finish(False))


def make_delta(parts, mask, weight):
    half = parts[0].shape[0]
    ranks, width = weight.shape
    block = 128
    steps = half // block
    packed = pl.BlockSpec((block, 128), lambda i: (i % steps, 0))
    return pl.pallas_call(
        functools.partial(delta_kernel, steps=steps),
        grid=(2 * steps,),
        in_specs=[packed] * 4
        + [
            pl.BlockSpec((block, ranks), lambda i: (i, 0)),
            pl.BlockSpec((ranks, width), lambda i: (0, 0)),
        ],
        out_specs=[
            pl.BlockSpec((block, width), lambda i: (i, 0)),
            pl.BlockSpec((block, ranks), lambda i: (i, 0)),
        ],
        out_shape=[
            jax.ShapeDtypeStruct((2 * half, width), jnp.bfloat16),
            jax.ShapeDtypeStruct((2 * half, ranks), jnp.bfloat16),
        ],
        compiler_params=params(),
        name="make_delta",
    )(*parts, mask, weight)


def grad_up_kernel(spread_ref, gradient_ref, out_ref):
    out_ref[...] = (
        ADAPTER_SCALE
        * lax.dot_general(
            spread_ref[...],
            gradient_ref[...],
            (((0,), (0,)), ((), ())),
            preferred_element_type=jnp.float32,
        )
    ).astype(out_ref.dtype)


def grad_up(spread, gradient):
    tokens, ranks = spread.shape
    width = gradient.shape[1]
    block = 512
    return pl.pallas_call(
        grad_up_kernel,
        grid=(width // block,),
        in_specs=[
            pl.BlockSpec((tokens, ranks), lambda i: (0, 0)),
            pl.BlockSpec((tokens, block), lambda i: (0, i)),
        ],
        out_specs=pl.BlockSpec((ranks, block), lambda i: (0, i)),
        out_shape=jax.ShapeDtypeStruct((ranks, width), jnp.bfloat16),
        compiler_params=params(),
        name="grad_up",
    )(spread, gradient)


def grad_down_kernel(p0, p1, p2, p3, mask_ref, tokens_ref, out_ref, spread_ref):
    half = p0.shape[0]

    @pl.when(pl.program_id(0) == 0)
    def _():
        total = (p0[...].astype(jnp.float32) + p1[...].astype(jnp.float32)) + (
            p2[...].astype(jnp.float32) + p3[...].astype(jnp.float32)
        )
        low_grad = (ADAPTER_SCALE * total).astype(jnp.bfloat16).astype(jnp.float32)
        spread_ref[:half] = spread_of(low_grad, mask_ref[:half], True)
        spread_ref[half:] = spread_of(low_grad, mask_ref[half:], False)

    out_ref[...] = lax.dot_general(
        spread_ref[...],
        tokens_ref[...],
        (((0,), (0,)), ((), ())),
        preferred_element_type=jnp.float32,
    ).astype(out_ref.dtype)


def grad_down(parts, mask, x):
    half = parts[0].shape[0]
    ranks = mask.shape[1]
    tokens, width = x.shape
    block = 512
    return pl.pallas_call(
        grad_down_kernel,
        grid=(width // block,),
        in_specs=[pl.BlockSpec((half, 128), lambda i: (0, 0))] * 4
        + [
            pl.BlockSpec((tokens, ranks), lambda i: (0, 0)),
            pl.BlockSpec((tokens, block), lambda i: (0, i)),
        ],
        out_specs=pl.BlockSpec((ranks, block), lambda i: (0, i)),
        out_shape=jax.ShapeDtypeStruct((ranks, width), jnp.bfloat16),
        scratch_shapes=[pltpu.VMEM((tokens, ranks), jnp.bfloat16)],
        compiler_params=params(),
        name="grad_down",
    )(*parts, mask, x)


def attend_kernel(
    target_ref,
    query_ref,
    base_ref,
    own_key_ref,
    own_value_ref,
    key_ref,
    value_ref,
    row_len_ref,
    row_prompt_ref,
    row_weight_ref,
    key_prompt_ref,
    key_place_ref,
    delta_hbm,
    out_hbm,
    delta_ref,
    grad_ref,
    in_sem,
    out_sem,
):
    rows, length, width = query_ref.shape
    head_group = QUERY_HEADS // KEY_HEADS
    kv_local = key_ref.shape[1] // HEAD_WIDTH
    group_width = head_group * HEAD_WIDTH
    block_tokens = ROW_BLOCK * length
    inv_root = 1.0 / math.sqrt(HEAD_WIDTH)
    queries = head_group * block_tokens
    contract = (((1,), (1,)), ((), ()))

    def fetch(r):
        return pltpu.make_async_copy(delta_hbm.at[target_ref[r]], delta_ref.at[r], in_sem.at[r])

    def send(r):
        return pltpu.make_async_copy(grad_ref.at[r], out_hbm.at[target_ref[r]], out_sem.at[r])

    for r in range(rows):
        fetch(r).start()
    for r in range(rows):
        fetch(r).wait()

    def heads(x):
        return jnp.concatenate(
            [x[:, h * HEAD_WIDTH : (h + 1) * HEAD_WIDTH] for h in range(head_group)], axis=0
        )

    def one_block(b, carry):
        block = pl.ds(b * ROW_BLOCK, ROW_BLOCK)
        tokens = pl.ds(b * block_tokens, block_tokens)
        shared_seen = (row_prompt_ref[tokens, :] == key_prompt_ref[...]) & (
            key_place_ref[...] < row_len_ref[tokens, :]
        )
        own_shape = (block_tokens, block_tokens)
        q_at = lax.broadcasted_iota(jnp.int32, own_shape, 0)
        k_at = lax.broadcasted_iota(jnp.int32, own_shape, 1)
        own_seen = (q_at // length == k_at // length) & (k_at <= q_at)
        weight = row_weight_ref[tokens, :]

        def group(x):
            return x.reshape(head_group, block_tokens, x.shape[-1])

        def flat(x):
            return x.reshape(queries, x.shape[-1])

        for g in range(kv_local):
            columns = slice(g * group_width, (g + 1) * group_width)
            keys_at = slice(g * HEAD_WIDTH, (g + 1) * HEAD_WIDTH)
            query = query_ref[block, :, columns].astype(jnp.float32) + delta_ref[
                block, :, columns
            ].astype(jnp.float32)
            query = heads(query.reshape(block_tokens, group_width)).astype(jnp.bfloat16)
            base = heads(
                base_ref[block, :, columns].astype(jnp.float32).reshape(block_tokens, group_width)
            )
            keys = key_ref[:, keys_at]
            values = value_ref[:, keys_at]
            own_keys = (
                own_key_ref[block, :, keys_at]
                .astype(jnp.float32)
                .reshape(block_tokens, HEAD_WIDTH)
                .astype(jnp.bfloat16)
            )
            own_values = (
                own_value_ref[block, :, keys_at]
                .astype(jnp.float32)
                .reshape(block_tokens, HEAD_WIDTH)
                .astype(jnp.bfloat16)
            )

            def by_rows(a, b):
                return lax.dot_general(a, b, contract, preferred_element_type=jnp.float32)

            def times(a, b):
                return jnp.dot(a, b, preferred_element_type=jnp.float32)

            shared = jnp.where(shared_seen[None], group(by_rows(query, keys) * inv_root), -1e30)
            own = jnp.where(own_seen[None], group(by_rows(query, own_keys) * inv_root), -1e30)
            top = jnp.maximum(
                jnp.max(shared, axis=-1, keepdims=True), jnp.max(own, axis=-1, keepdims=True)
            )
            shared = jnp.exp(shared - top)
            own = jnp.exp(own - top)
            total = jnp.sum(shared, axis=-1, keepdims=True) + jnp.sum(own, axis=-1, keepdims=True)
            scale = 1.0 / total
            shared = flat(shared * scale)
            own = flat(own * scale)
            attn_out = times(shared.astype(jnp.bfloat16), values) + times(
                own.astype(jnp.bfloat16), own_values
            )
            grad_out = flat(group(attn_out - base) * weight[None]).astype(jnp.bfloat16)
            shared_grad = by_rows(grad_out, values)
            own_grad = by_rows(grad_out, own_values)
            inner = jnp.sum(shared * shared_grad, axis=-1, keepdims=True) + jnp.sum(
                own * own_grad, axis=-1, keepdims=True
            )
            shared_gs = (shared * (shared_grad - inner) * inv_root).astype(jnp.bfloat16)
            own_gs = (own * (own_grad - inner) * inv_root).astype(jnp.bfloat16)
            gradient = times(shared_gs, keys) + times(own_gs, own_keys)
            for h in range(head_group):
                piece = gradient[h * block_tokens : (h + 1) * block_tokens]
                at = g * group_width + h * HEAD_WIDTH
                grad_ref[block, :, at : at + HEAD_WIDTH] = piece.reshape(
                    ROW_BLOCK, length, HEAD_WIDTH
                ).astype(jnp.bfloat16)
        return carry

    lax.fori_loop(0, rows // ROW_BLOCK, one_block, 0)
    for r in range(rows):
        send(r).start()
    for r in range(rows):
        send(r).wait()


def attend(target, query, base, own_key, own_value, keys, values, per_token, per_key, delta):
    rows, length, width = query.shape
    row_vectors = [v.reshape(rows * length, 1) for v in per_token]
    key_vectors = [v.reshape(1, -1) for v in per_key]
    return pl.pallas_call(
        attend_kernel,
        in_specs=[_SMEM] + [_VMEM] * 11 + [_ANY],
        out_specs=_ANY,
        out_shape=jax.ShapeDtypeStruct(delta.shape, delta.dtype),
        scratch_shapes=[
            pltpu.VMEM((rows, length, width), jnp.bfloat16),
            pltpu.VMEM((rows, length, width), jnp.bfloat16),
            pltpu.SemaphoreType.DMA((rows,)),
            pltpu.SemaphoreType.DMA((rows,)),
        ],
        input_output_aliases={12: 0},
        compiler_params=params(),
        name="attend",
    )(
        target,
        query,
        base,
        own_key,
        own_value,
        keys,
        values,
        *row_vectors,
        *key_vectors,
        delta,
    )


def shifted(block_for, count):
    return [
        lax.ppermute(block_for(k), "kv", [(i, (i + k) % count) for i in range(count)])
        for k in range(1, count)
    ]


def per_device(
    tokens,
    frozen_query,
    trained_keys,
    trained_values,
    frozen_output,
    prompt_key_cache,
    prompt_value_cache,
    adapter_down,
    adapter_up,
    row_adapter_index,
    row_forget_flag,
    row_prompt_index,
    row_prompt_length,
):
    tok_count = lax.axis_size("tok")
    kv_count = lax.axis_size("kv")
    me = lax.axis_index("tok")
    kv = lax.axis_index("kv")
    rows = tokens.shape[0] // QUERY_LENGTH
    width = tokens.shape[1]
    adapters = adapter_down.shape[0]
    slots = tok_count * CAP
    down_flat = adapter_down.reshape(adapters * ADAPTER_RANK, width)
    up_flat = adapter_up.reshape(adapters * ADAPTER_RANK, width)

    def as_rows(x):
        return x.reshape(rows, QUERY_LENGTH, x.shape[1])

    mine = lax.dynamic_slice_in_dim(row_adapter_index, me * rows, rows) // adapters
    row_at = jnp.arange(rows, dtype=jnp.int32)
    my_rank = jnp.sum(
        ((mine[:, None] == mine[None, :]) & (row_at[:, None] > row_at[None, :])).astype(jnp.int32),
        axis=1,
    )
    target = mine * CAP + my_rank
    slot_at = jnp.arange(slots, dtype=jnp.int32)
    source = (
        jnp.sum(jnp.where(slot_at[:, None] == target[None, :], row_at[None, :] + 1, 0), axis=1) - 1
    )

    sent = route_rows(source, as_rows(tokens), slots)
    arrived = lax.all_to_all(sent, "tok", split_axis=0, concat_axis=0, tiled=True)
    flat_tokens = arrived.reshape(slots * QUERY_LENGTH, width)

    all_owners = (row_adapter_index // adapters).reshape(tok_count, rows)
    hit = all_owners == me
    earlier = (
        jnp.sum(
            jnp.where((row_at[:, None] > row_at[None, :])[None], hit[:, None, :], False).astype(
                jnp.int32
            ),
            axis=2,
        )
    )
    local_adapter = (row_adapter_index % adapters).reshape(tok_count, rows)
    slot_adapter = jnp.sum(
        jnp.where(
            hit[:, None, :]
            & (earlier[:, None, :] == jnp.arange(CAP, dtype=jnp.int32)[None, :, None]),
            local_adapter[:, None, :] + 1,
            0,
        ),
        axis=2,
    ).reshape(slots)
    lane_adapter = jnp.arange(adapters * ADAPTER_RANK, dtype=jnp.int32) // ADAPTER_RANK + 1
    mask = jnp.broadcast_to(
        (slot_adapter[:, None] == lane_adapter[None, :]).astype(jnp.bfloat16)[:, None, :],
        (slots, QUERY_LENGTH, lane_adapter.shape[0]),
    ).reshape(slots * QUERY_LENGTH, lane_adapter.shape[0])

    prompts, place_local = prompt_key_cache.shape[:2]
    head_columns = prompt_key_cache.shape[2] // kv_count
    both = jnp.stack([prompt_key_cache, prompt_value_cache]).reshape(
        2 * prompts * place_local, kv_count, head_columns
    )

    def cache_block(k):
        return lax.dynamic_index_in_dim(both, (kv + k) % kv_count, 1, keepdims=False)

    cache = jnp.stack([cache_block(0)] + shifted(cache_block, kv_count)).reshape(
        kv_count, 2, prompts * place_local, head_columns
    )
    cache_keys = cache[:, 0].reshape(-1, head_columns)
    cache_values = cache[:, 1].reshape(-1, head_columns)
    key_at = jnp.arange(cache_keys.shape[0], dtype=jnp.int32)
    key_from = (kv - key_at // (prompts * place_local) + kv_count) % kv_count
    key_prompt = key_at // place_local % prompts
    key_place = key_from * place_local + key_at % place_local

    def of_my_tokens(x):
        return jnp.repeat(lax.dynamic_slice_in_dim(x, me * rows, rows), QUERY_LENGTH)

    row_weight = 1.0 - 2.0 * of_my_tokens(row_forget_flag).astype(jnp.float32)

    part = project(flat_tokens, mask, down_flat, jnp.float32)
    delta, spread = make_delta([part] + shifted(lambda k: part, kv_count), mask, up_flat)
    delta = lax.all_to_all(
        delta.reshape(slots, QUERY_LENGTH, width), "tok", split_axis=0, concat_axis=0, tiled=True
    )

    gradient = attend(
        target,
        as_rows(frozen_query),
        as_rows(frozen_output),
        as_rows(trained_keys),
        as_rows(trained_values),
        cache_keys,
        cache_values,
        (of_my_tokens(row_prompt_length), of_my_tokens(row_prompt_index), row_weight),
        (key_prompt, key_place),
        delta,
    )
    gradient = lax.all_to_all(gradient, "tok", split_axis=0, concat_axis=0, tiled=True).reshape(
        slots * QUERY_LENGTH, width
    )

    part = project(gradient, mask, up_flat, jnp.bfloat16)
    parts = [part] + shifted(lambda k: part, kv_count)
    up_grad = grad_up(spread, gradient)
    down_grad = grad_down(parts, mask, flat_tokens)
    return (
        down_grad.reshape(adapters, ADAPTER_RANK, width),
        up_grad.reshape(adapters, ADAPTER_RANK, width),
    )


def solution(mesh):
    return jax.shard_map(
        per_device,
        mesh=mesh,
        in_specs=(
            P("tok", "kv"),
            P("tok", "kv"),
            P("tok", "kv"),
            P("tok", "kv"),
            P("tok", "kv"),
            P(None, "kv", None),
            P(None, "kv", None),
            P("tok", None, "kv"),
            P("tok", None, "kv"),
            P(),
            P(),
            P(),
            P(),
        ),
        out_specs=(P("tok", None, "kv"), P("tok", None, "kv")),
        check_vma=False,
    )
```

```python
import functools
import math

import jax
import jax.numpy as jnp
from jax import lax
from jax.experimental import pallas as pl
from jax.experimental.pallas import tpu as pltpu
from jax.sharding import Mesh
from jax.sharding import PartitionSpec as P

QUERY_HEADS = 64
KEY_HEADS = 8
HEAD_WIDTH = 128
ADAPTER_RANK = 64
QUERY_LENGTH = 8
ADAPTER_SCALE = 0.5
CAP = 2
PLANES = 8
HOP_CAP = 10
TOK = ("z", "p")
ROW_BLOCK = 16
LOG2_E = math.log2(math.e)
VMEM_LIMIT = 56 * 1024 * 1024

_VMEM = pl.BlockSpec(memory_space=pltpu.VMEM)
_SMEM = pl.BlockSpec(memory_space=pltpu.SMEM)
_ANY = pl.BlockSpec(memory_space=pl.ANY)


def params():
    return pltpu.CompilerParams(vmem_limit_bytes=VMEM_LIMIT)


def route_kernel(source_ref, rows_ref, out_ref):
    first = pl.program_id(0) * out_ref.shape[0]
    for j in range(out_ref.shape[0]):
        row = source_ref[first + j]

        @pl.when(row >= 0)
        def _():
            out_ref[j] = rows_ref[row]

        @pl.when(row < 0)
        def _():
            out_ref[j] = jnp.zeros_like(out_ref[j])


def route_rows(source, rows, slots):
    row_count, length, width = rows.shape
    step = 16
    return pl.pallas_call(
        route_kernel,
        grid_spec=pltpu.PrefetchScalarGridSpec(
            num_scalar_prefetch=1,
            grid=(slots // step,),
            in_specs=[pl.BlockSpec((row_count, length, width), lambda i, s: (0, 0, 0))],
            out_specs=pl.BlockSpec((step, length, width), lambda i, s: (i, 0, 0)),
        ),
        out_shape=jax.ShapeDtypeStruct((slots, length, width), rows.dtype),
        compiler_params=params(),
        name="route_rows",
    )(source, rows)


def fold(products, mask):
    kept = products * mask.astype(jnp.float32)
    half = kept[:, :128] + kept[:, 128:]
    return half + pltpu.roll(half, 64, 1)


def low_half(shape):
    return lax.broadcasted_iota(jnp.int32, shape, 1) < 64


def project_kernel(x_ref, weight_ref, mask_ref, out_ref, total_ref):
    step = pl.program_id(0)
    product = lax.dot_general(
        x_ref[...],
        weight_ref[...],
        (((1,), (1,)), ((), ())),
        preferred_element_type=jnp.float32,
    )

    @pl.when(step == 0)
    def _():
        total_ref[...] = product

    @pl.when(step > 0)
    def _():
        total_ref[...] += product

    @pl.when(step == pl.num_programs(0) - 1)
    def _():
        half = out_ref.shape[0]
        both = jnp.where(
            low_half(out_ref.shape),
            fold(total_ref[:half], mask_ref[:half]),
            fold(total_ref[half:], mask_ref[half:]),
        )
        out_ref[...] = both.astype(out_ref.dtype)


def project(x, mask, weight, out_type):
    tokens, width = x.shape
    ranks = weight.shape[0]
    block = 512
    return pl.pallas_call(
        project_kernel,
        grid=(width // block,),
        in_specs=[
            pl.BlockSpec((tokens, block), lambda i: (0, i)),
            pl.BlockSpec((ranks, block), lambda i: (0, i)),
            pl.BlockSpec((tokens, ranks), lambda i: (0, 0)),
        ],
        out_specs=pl.BlockSpec((tokens // 2, 128), lambda i: (0, 0)),
        out_shape=jax.ShapeDtypeStruct((tokens // 2, 128), out_type),
        scratch_shapes=[pltpu.VMEM((tokens, ranks), jnp.float32)],
        compiler_params=params(),
        name="project",
    )(x, weight, mask)


def spread_of(packed, mask, is_low):
    low = low_half(packed.shape)
    turned = pltpu.roll(packed, 64, 1)
    twice = jnp.where(low, packed, turned) if is_low else jnp.where(low, turned, packed)
    return (jnp.concatenate([twice, twice], axis=1) * mask.astype(jnp.float32)).astype(
        jnp.bfloat16
    )


def delta_kernel(p0, p1, p2, p3, mask_ref, weight_ref, out_ref, spread_ref):
    half = p0.shape[0]

    @pl.when(pl.program_id(0) == 0)
    def _():
        total = (p0[...] + p1[...]) + (p2[...] + p3[...])
        low_rank = total.astype(jnp.bfloat16).astype(jnp.float32)
        spread_ref[:half] = spread_of(low_rank, mask_ref[:half], True)
        spread_ref[half:] = spread_of(low_rank, mask_ref[half:], False)

    out_ref[...] = (
        ADAPTER_SCALE
        * jnp.dot(spread_ref[...], weight_ref[...], preferred_element_type=jnp.float32)
    ).astype(out_ref.dtype)


def make_delta(parts, mask, weight):
    half = parts[0].shape[0]
    tokens = 2 * half
    ranks, width = weight.shape
    block = 512
    return pl.pallas_call(
        delta_kernel,
        grid=(width // block,),
        in_specs=[pl.BlockSpec((half, 128), lambda i: (0, 0))] * 4
        + [
            pl.BlockSpec((tokens, ranks), lambda i: (0, 0)),
            pl.BlockSpec((ranks, block), lambda i: (0, i)),
        ],
        out_specs=[
            pl.BlockSpec((tokens, block), lambda i: (0, i)),
            pl.BlockSpec((tokens, ranks), lambda i: (0, 0)),
        ],
        out_shape=[
            jax.ShapeDtypeStruct((tokens, width), jnp.bfloat16),
            jax.ShapeDtypeStruct((tokens, ranks), jnp.bfloat16),
        ],
        compiler_params=params(),
        name="make_delta",
    )(*parts, mask, weight)


def grad_up_kernel(spread_ref, gradient_ref, out_ref):
    out_ref[...] = (
        ADAPTER_SCALE
        * lax.dot_general(
            spread_ref[...],
            gradient_ref[...],
            (((0,), (0,)), ((), ())),
            preferred_element_type=jnp.float32,
        )
    ).astype(out_ref.dtype)


def grad_up(spread, gradient):
    tokens, ranks = spread.shape
    width = gradient.shape[1]
    block = 512
    return pl.pallas_call(
        grad_up_kernel,
        grid=(width // block,),
        in_specs=[
            pl.BlockSpec((tokens, ranks), lambda i: (0, 0)),
            pl.BlockSpec((tokens, block), lambda i: (0, i)),
        ],
        out_specs=pl.BlockSpec((ranks, block), lambda i: (0, i)),
        out_shape=jax.ShapeDtypeStruct((ranks, width), jnp.bfloat16),
        compiler_params=params(),
        name="grad_up",
    )(spread, gradient)


def grad_down_kernel(p0, p1, p2, p3, mask_ref, tokens_ref, out_ref, spread_ref):
    half = p0.shape[0]

    @pl.when(pl.program_id(0) == 0)
    def _():
        total = (p0[...].astype(jnp.float32) + p1[...].astype(jnp.float32)) + (
            p2[...].astype(jnp.float32) + p3[...].astype(jnp.float32)
        )
        low_grad = (ADAPTER_SCALE * total).astype(jnp.bfloat16).astype(jnp.float32)
        spread_ref[:half] = spread_of(low_grad, mask_ref[:half], True)
        spread_ref[half:] = spread_of(low_grad, mask_ref[half:], False)

    out_ref[...] = lax.dot_general(
        spread_ref[...],
        tokens_ref[...],
        (((0,), (0,)), ((), ())),
        preferred_element_type=jnp.float32,
    ).astype(out_ref.dtype)


def grad_down(parts, mask, x):
    half = parts[0].shape[0]
    ranks = mask.shape[1]
    tokens, width = x.shape
    block = 512
    return pl.pallas_call(
        grad_down_kernel,
        grid=(width // block,),
        in_specs=[pl.BlockSpec((half, 128), lambda i: (0, 0))] * 4
        + [
            pl.BlockSpec((tokens, ranks), lambda i: (0, 0)),
            pl.BlockSpec((tokens, block), lambda i: (0, i)),
        ],
        out_specs=pl.BlockSpec((ranks, block), lambda i: (0, i)),
        out_shape=jax.ShapeDtypeStruct((ranks, width), jnp.bfloat16),
        scratch_shapes=[pltpu.VMEM((tokens, ranks), jnp.bfloat16)],
        compiler_params=params(),
        name="grad_down",
    )(*parts, mask, x)


def heads_first(x, head_group):
    return jnp.concatenate(
        [x[:, h * HEAD_WIDTH : (h + 1) * HEAD_WIDTH] for h in range(head_group)], axis=0
    )


def by_rows(a, b):
    return lax.dot_general(a, b, (((1,), (1,)), ((), ())), preferred_element_type=jnp.float32)


def times(a, b):
    return jnp.dot(a, b, preferred_element_type=jnp.float32)


def attend_group(query, base, own_keys, own_values, keys, values, shared_seen, own_seen, weight):
    tokens = own_keys.shape[0]
    head_group = query.shape[1] // HEAD_WIDTH
    inv_root = 1.0 / math.sqrt(HEAD_WIDTH)
    query = heads_first(query, head_group).astype(jnp.bfloat16)
    base = heads_first(base, head_group)

    def group(x):
        return x.reshape(head_group, tokens, x.shape[-1])

    def flat(x):
        return x.reshape(head_group * tokens, x.shape[-1])

    shared = jnp.where(shared_seen[None], group(by_rows(query, keys)), -1e30)
    own = jnp.where(own_seen[None], group(by_rows(query, own_keys)), -1e30)
    top = jnp.maximum(
        jnp.max(shared, axis=-1, keepdims=True), jnp.max(own, axis=-1, keepdims=True)
    )
    shared = flat(jnp.exp2((shared - top) * (inv_root * LOG2_E)))
    own = flat(jnp.exp2((own - top) * (inv_root * LOG2_E)))
    total = jnp.sum(shared, axis=-1, keepdims=True) + jnp.sum(own, axis=-1, keepdims=True)
    scale = 1.0 / total
    attn_out = scale * (
        times(shared.astype(jnp.bfloat16), values) + times(own.astype(jnp.bfloat16), own_values)
    )
    grad_out = flat(group(attn_out - base) * weight[None]).astype(jnp.bfloat16)
    inner = jnp.sum(grad_out.astype(jnp.float32) * attn_out, axis=-1, keepdims=True)
    shared_gs = (shared * (by_rows(grad_out, values) - inner)).astype(jnp.bfloat16)
    own_gs = (own * (by_rows(grad_out, own_values) - inner)).astype(jnp.bfloat16)
    return (scale * inv_root) * (times(shared_gs, keys) + times(own_gs, own_keys))


def attend_block(b, load, delta_ref, grad_ref, key_ref, value_ref, vectors):
    row_len_ref, row_prompt_ref, row_weight_ref, key_prompt_ref, key_place_ref = vectors
    length = QUERY_LENGTH
    head_group = QUERY_HEADS // KEY_HEADS
    group_width = head_group * HEAD_WIDTH
    block_tokens = ROW_BLOCK * length
    block = pl.ds(b * ROW_BLOCK, ROW_BLOCK)
    tokens = pl.ds(b * block_tokens, block_tokens)
    shared_seen = (row_prompt_ref[tokens, :] == key_prompt_ref[...]) & (
        key_place_ref[...] < row_len_ref[tokens, :]
    )
    own_shape = (block_tokens, block_tokens)
    q_at = lax.broadcasted_iota(jnp.int32, own_shape, 0)
    k_at = lax.broadcasted_iota(jnp.int32, own_shape, 1)
    own_seen = (q_at // length == k_at // length) & (k_at <= q_at)
    weight = row_weight_ref[tokens, :]

    def two_d(x):
        return x.astype(jnp.float32).reshape(block_tokens, x.shape[-1])

    for g in range(key_ref.shape[1] // HEAD_WIDTH):
        columns = slice(g * group_width, (g + 1) * group_width)
        keys_at = slice(g * HEAD_WIDTH, (g + 1) * HEAD_WIDTH)
        gradient = attend_group(
            two_d(load("query", block, columns)) + two_d(delta_ref[block, :, columns]),
            two_d(load("base", block, columns)),
            two_d(load("key", block, keys_at)).astype(jnp.bfloat16),
            two_d(load("value", block, keys_at)).astype(jnp.bfloat16),
            key_ref[:, keys_at],
            value_ref[:, keys_at],
            shared_seen,
            own_seen,
            weight,
        )
        for h in range(head_group):
            piece = gradient[h * block_tokens : (h + 1) * block_tokens]
            at = g * group_width + h * HEAD_WIDTH
            grad_ref[block, :, at : at + HEAD_WIDTH] = piece.reshape(
                ROW_BLOCK, length, HEAD_WIDTH
            ).astype(jnp.bfloat16)


def attend_home_kernel(
    target_ref,
    query_ref,
    base_ref,
    own_key_ref,
    own_value_ref,
    key_ref,
    value_ref,
    row_len_ref,
    row_prompt_ref,
    row_weight_ref,
    key_prompt_ref,
    key_place_ref,
    delta_hbm,
    out_hbm,
    delta_ref,
    grad_ref,
    in_sem,
    out_sem,
):
    rows = query_ref.shape[0]
    refs = {"query": query_ref, "base": base_ref, "key": own_key_ref, "value": own_value_ref}
    vectors = (row_len_ref, row_prompt_ref, row_weight_ref, key_prompt_ref, key_place_ref)

    def fetch(r):
        return pltpu.make_async_copy(delta_hbm.at[target_ref[r]], delta_ref.at[r], in_sem.at[r])

    def send(r):
        return pltpu.make_async_copy(grad_ref.at[r], out_hbm.at[target_ref[r]], out_sem.at[r])

    for r in range(rows):
        fetch(r).start()
    for r in range(rows):
        fetch(r).wait()

    def load(name, block, columns):
        return refs[name][block, :, columns]

    def one_block(b, carry):
        attend_block(b, load, delta_ref, grad_ref, key_ref, value_ref, vectors)
        return carry

    lax.fori_loop(0, rows // ROW_BLOCK, one_block, 0)
    for r in range(rows):
        send(r).start()
    for r in range(rows):
        send(r).wait()


def attend_home(target, query, base, own_key, own_value, keys, values, per_token, per_key, delta):
    rows, length, width = query.shape
    return pl.pallas_call(
        attend_home_kernel,
        in_specs=[_SMEM] + [_VMEM] * 11 + [_ANY],
        out_specs=_ANY,
        out_shape=jax.ShapeDtypeStruct(delta.shape, delta.dtype),
        scratch_shapes=[
            pltpu.VMEM((rows, length, width), jnp.bfloat16),
            pltpu.VMEM((rows, length, width), jnp.bfloat16),
            pltpu.SemaphoreType.DMA((rows,)),
            pltpu.SemaphoreType.DMA((rows,)),
        ],
        input_output_aliases={12: 0},
        compiler_params=params(),
        name="attend_home",
    )(
        target,
        query,
        base,
        own_key,
        own_value,
        keys,
        values,
        *per_token,
        *per_key,
        delta,
    )


def part_starts(parts):
    starts = [0]
    for x in parts:
        starts.append(starts[-1] + x.shape[0])
    return starts


def attend_middle_kernel(*refs, hops):
    place_ref, seat_ref, count_ref = refs[:3]
    payload_hbm = refs[3 : 3 + hops]
    key_ref, value_ref = refs[3 + hops : 5 + hops]
    vectors = refs[5 + hops : 10 + hops]
    delta_hbm, out_hbm, payload_ref, delta_ref, grad_ref = refs[10 + hops : 15 + hops]
    in_sem, delta_sem, out_sem = refs[15 + hops :]
    width = delta_ref.shape[-1]
    kv_width = key_ref.shape[1]
    starts = {"query": 0, "base": width, "key": 2 * width, "value": 2 * width + kv_width}
    count = count_ref[0]
    blocks = (count + ROW_BLOCK - 1) // ROW_BLOCK

    part_start = part_starts(payload_hbm)

    def fetch(k, j, do):
        at = part_start[k] + j
        row = place_ref[at]

        @pl.when(row >= 0)
        def _():
            do(pltpu.make_async_copy(payload_hbm[k].at[j], payload_ref.at[row], in_sem.at[at]))

    def fetch_delta(i):
        return pltpu.make_async_copy(delta_hbm.at[seat_ref[i]], delta_ref.at[i], delta_sem.at[i])

    def send(i):
        return pltpu.make_async_copy(grad_ref.at[i], out_hbm.at[seat_ref[i]], out_sem.at[i])

    def each(first, last, do):
        def step(i, carry):
            do(i)
            return carry

        lax.fori_loop(first, last, step, 0)

    for k in range(hops):
        each(0, payload_hbm[k].shape[0], lambda j, k=k: fetch(k, j, lambda copy: copy.start()))
    each(0, count, lambda i: fetch_delta(i).start())

    def clear(i):
        payload_ref[i] = jnp.zeros_like(payload_ref[i])
        delta_ref[i] = jnp.zeros_like(delta_ref[i])

    each(count, blocks * ROW_BLOCK, clear)
    for k in range(hops):
        each(0, payload_hbm[k].shape[0], lambda j, k=k: fetch(k, j, lambda copy: copy.wait()))
    each(0, count, lambda i: fetch_delta(i).wait())

    def load(name, block, columns):
        start = starts[name]
        return payload_ref[block, :, start + columns.start : start + columns.stop]

    each(
        0,
        blocks,
        lambda b: attend_block(b, load, delta_ref, grad_ref, key_ref, value_ref, vectors),
    )
    each(0, count, lambda i: send(i).start())
    each(0, count, lambda i: send(i).wait())


def attend_middle(place, seat, count, payload, keys, values, per_token, per_key, delta):
    hops = len(payload)
    length, payload_width = payload[0].shape[1:]
    most = part_starts(payload)[-1]
    width = delta.shape[-1]
    return pl.pallas_call(
        functools.partial(attend_middle_kernel, hops=hops),
        in_specs=[_SMEM] * 3 + [_ANY] * hops + [_VMEM] * 7 + [_ANY],
        out_specs=_ANY,
        out_shape=jax.ShapeDtypeStruct(delta.shape, delta.dtype),
        scratch_shapes=[
            pltpu.VMEM((most, length, payload_width), jnp.bfloat16),
            pltpu.VMEM((most, length, width), jnp.bfloat16),
            pltpu.VMEM((most, length, width), jnp.bfloat16),
            pltpu.SemaphoreType.DMA((most,)),
            pltpu.SemaphoreType.DMA((most,)),
            pltpu.SemaphoreType.DMA((most,)),
        ],
        input_output_aliases={10 + hops: 0},
        compiler_params=params(),
        name="attend_middle",
    )(place, seat, count, *payload, keys, values, *per_token, *per_key, delta)


def deal_kernel(source_ref, *refs, count):
    inputs, outs, sem = refs[:count], refs[count:-1], refs[-1]
    part_start = part_starts(outs)

    def each(do):
        for k, out in enumerate(outs):

            def step(j, carry, k=k, out=out):
                slot = part_start[k] + j
                row = source_ref[slot]

                @pl.when(row >= 0)
                def _():
                    at = 0
                    for n, x in enumerate(inputs):
                        width = x.shape[-1]
                        do(
                            pltpu.make_async_copy(
                                x.at[row], out.at[j, :, pl.ds(at, width)], sem.at[slot, n]
                            )
                        )
                        at += width

                return carry

            lax.fori_loop(0, out.shape[0], step, 0)

    each(lambda copy: copy.start())
    each(lambda copy: copy.wait())


def deal(source, arrays, sizes):
    length = arrays[0].shape[1]
    width = sum(x.shape[2] for x in arrays)
    return pl.pallas_call(
        functools.partial(deal_kernel, count=len(arrays)),
        in_specs=[_SMEM] + [_ANY] * len(arrays),
        out_specs=[_ANY] * len(sizes),
        out_shape=[jax.ShapeDtypeStruct((n, length, width), arrays[0].dtype) for n in sizes],
        scratch_shapes=[pltpu.SemaphoreType.DMA((sum(sizes), len(arrays)))],
        compiler_params=params(),
        name="deal",
    )(source, *arrays)


def seat_kernel(seat_ref, empty_ref, *refs, hops):
    parts, out, zero_ref, sem, zero_sem = (
        refs[:hops],
        refs[hops],
        refs[hops + 1],
        refs[hops + 2],
        refs[hops + 3],
    )
    zero_ref[...] = jnp.zeros_like(zero_ref)

    def clear(do, slot, carry):
        @pl.when(empty_ref[slot] > 0)
        def _():
            do(pltpu.make_async_copy(zero_ref, out.at[slot], zero_sem.at[slot]))

        return carry

    part_start = part_starts(parts)

    def each(do):
        for k in range(hops):

            def step(j, carry, k=k):
                at = part_start[k] + j
                slot = seat_ref[at]

                @pl.when(slot >= 0)
                def _():
                    do(pltpu.make_async_copy(parts[k].at[j], out.at[slot], sem.at[at]))

                return carry

            lax.fori_loop(0, parts[k].shape[0], step, 0)
        lax.fori_loop(0, out.shape[0], functools.partial(clear, do), 0)

    each(lambda copy: copy.start())
    each(lambda copy: copy.wait())


def seat_rows(seat, empty, parts, slots):
    hops = len(parts)
    length, width = parts[0].shape[1:]
    return pl.pallas_call(
        functools.partial(seat_kernel, hops=hops),
        in_specs=[_SMEM] * 2 + [_ANY] * hops,
        out_specs=_ANY,
        out_shape=jax.ShapeDtypeStruct((slots, length, width), parts[0].dtype),
        scratch_shapes=[
            pltpu.VMEM((length, width), jnp.bfloat16),
            pltpu.SemaphoreType.DMA((part_starts(parts)[-1],)),
            pltpu.SemaphoreType.DMA((slots,)),
        ],
        compiler_params=params(),
        name="seat_rows",
    )(seat, empty, *parts)


def shifted(block_for, count):
    return [
        lax.ppermute(block_for(k), "kv", [(i, (i + k) % count) for i in range(count)])
        for k in range(1, count)
    ]


def before(same):
    at = jnp.arange(same.shape[-1], dtype=jnp.int32)
    return jnp.sum((same & (at[:, None] > at[None, :])).astype(jnp.int32), axis=-1)


def look_up(keys, wanted, values):
    return jnp.sum(jnp.where(keys[None, :] == wanted[:, None], values[None, :] + 1, 0), axis=1)


def adapter_mask(slot_adapter, adapters):
    slots = slot_adapter.shape[0]
    lane_adapter = jnp.arange(adapters * ADAPTER_RANK, dtype=jnp.int32) // ADAPTER_RANK + 1
    return jnp.broadcast_to(
        (slot_adapter[:, None] == lane_adapter[None, :]).astype(jnp.bfloat16)[:, None, :],
        (slots, QUERY_LENGTH, lane_adapter.shape[0]),
    ).reshape(slots * QUERY_LENGTH, lane_adapter.shape[0])


def gather_caches(prompt_key_cache, prompt_value_cache):
    kv_count = lax.axis_size("kv")
    kv = lax.axis_index("kv")
    prompts, place_local = prompt_key_cache.shape[:2]
    head_columns = prompt_key_cache.shape[2] // kv_count
    both = jnp.stack([prompt_key_cache, prompt_value_cache]).reshape(
        2 * prompts * place_local, kv_count, head_columns
    )

    def cache_block(k):
        return lax.dynamic_index_in_dim(both, (kv + k) % kv_count, 1, keepdims=False)

    cache = jnp.stack([cache_block(0)] + shifted(cache_block, kv_count)).reshape(
        kv_count, 2, prompts * place_local, head_columns
    )
    key_at = jnp.arange(kv_count * prompts * place_local, dtype=jnp.int32)
    key_from = (kv - key_at // (prompts * place_local) + kv_count) % kv_count
    key_prompt = key_at // place_local % prompts
    key_place = key_from * place_local + key_at % place_local
    return (
        cache[:, 0].reshape(-1, head_columns),
        cache[:, 1].reshape(-1, head_columns),
        (key_prompt.reshape(1, -1), key_place.reshape(1, -1)),
    )


def per_token(x):
    return jnp.repeat(x, QUERY_LENGTH).reshape(-1, 1)


def as_rows(x):
    return x.reshape(x.shape[0] // QUERY_LENGTH, QUERY_LENGTH, x.shape[1])


def owner_forward(flat_tokens, mask, down_flat, up_flat):
    kv_count = lax.axis_size("kv")
    part = project(flat_tokens, mask, down_flat, jnp.float32)
    return make_delta([part] + shifted(lambda k: part, kv_count), mask, up_flat)


def owner_backward(gradient, flat_tokens, mask, spread, up_flat):
    kv_count = lax.axis_size("kv")
    part = project(gradient, mask, up_flat, jnp.bfloat16)
    parts = [part] + shifted(lambda k: part, kv_count)
    return grad_down(parts, mask, flat_tokens), grad_up(spread, gradient)


def one_hop(
    tokens,
    frozen_query,
    trained_keys,
    trained_values,
    frozen_output,
    prompt_key_cache,
    prompt_value_cache,
    adapter_down,
    adapter_up,
    row_adapter_index,
    row_forget_flag,
    row_prompt_index,
    row_prompt_length,
):
    tok_count = lax.axis_size(TOK)
    me = lax.axis_index(TOK)
    rows = tokens.shape[0] // QUERY_LENGTH
    width = tokens.shape[1]
    adapters = adapter_down.shape[0]
    slots = tok_count * CAP
    down_flat = adapter_down.reshape(adapters * ADAPTER_RANK, width)
    up_flat = adapter_up.reshape(adapters * ADAPTER_RANK, width)

    mine = lax.dynamic_slice_in_dim(row_adapter_index, me * rows, rows) // adapters
    target = mine * CAP + before(mine[:, None] == mine[None, :])
    source = (
        look_up(
            target, jnp.arange(slots, dtype=jnp.int32), jnp.arange(rows, dtype=jnp.int32)
        )
        - 1
    )

    def exchange(x):
        return lax.all_to_all(x, TOK, split_axis=0, concat_axis=0, tiled=True)

    flat_tokens = exchange(route_rows(source, as_rows(tokens), slots)).reshape(-1, width)

    hit = (row_adapter_index // adapters).reshape(tok_count, rows) == me
    rank = before(jnp.broadcast_to(hit[:, None, :], (tok_count, rows, rows)))
    local_adapter = (row_adapter_index % adapters).reshape(tok_count, rows)
    slot_adapter = jnp.sum(
        jnp.where(
            hit[:, None, :]
            & (rank[:, None, :] == jnp.arange(CAP, dtype=jnp.int32)[None, :, None]),
            local_adapter[:, None, :] + 1,
            0,
        ),
        axis=2,
    ).reshape(slots)
    mask = adapter_mask(slot_adapter, adapters)
    keys, values, per_key = gather_caches(prompt_key_cache, prompt_value_cache)

    def of_mine(x):
        return lax.dynamic_slice_in_dim(x, me * rows, rows)

    delta, spread = owner_forward(flat_tokens, mask, down_flat, up_flat)
    gradient = attend_home(
        target,
        as_rows(frozen_query),
        as_rows(frozen_output),
        as_rows(trained_keys),
        as_rows(trained_values),
        keys,
        values,
        (
            per_token(of_mine(row_prompt_length)),
            per_token(of_mine(row_prompt_index)),
            per_token(1.0 - 2.0 * of_mine(row_forget_flag).astype(jnp.float32)),
        ),
        per_key,
        exchange(delta.reshape(slots, QUERY_LENGTH, width)),
    )
    down, up = owner_backward(
        exchange(gradient).reshape(-1, width), flat_tokens, mask, spread, up_flat
    )
    return down.reshape(adapter_down.shape), up.reshape(adapter_up.shape)


def two_hops(
    tokens,
    frozen_query,
    trained_keys,
    trained_values,
    frozen_output,
    prompt_key_cache,
    prompt_value_cache,
    adapter_down,
    adapter_up,
    row_adapter_index,
    row_forget_flag,
    row_prompt_index,
    row_prompt_length,
    *,
    cap,
):
    planes = lax.axis_size("z")
    places = lax.axis_size("p")
    z = lax.axis_index("z")
    p = lax.axis_index("p")
    rows = tokens.shape[0] // QUERY_LENGTH
    width = tokens.shape[1]
    adapters = adapter_down.shape[0]
    slots = planes * places * CAP
    most = planes * cap
    down_flat = adapter_down.reshape(adapters * ADAPTER_RANK, width)
    up_flat = adapter_up.reshape(adapters * ADAPTER_RANK, width)
    row_at = jnp.arange(rows, dtype=jnp.int32)
    plane_at = jnp.arange(planes, dtype=jnp.int32)

    mine = lax.dynamic_slice_in_dim(row_adapter_index, (z * places + p) * rows, rows) // adapters
    my_plane = mine // places
    my_slot = (my_plane - z + planes) % planes * cap + before(
        my_plane[:, None] == my_plane[None, :]
    )
    source = look_up(my_slot, jnp.arange(most, dtype=jnp.int32), row_at) - 1

    half = cap // 2
    sizes = (cap,) * 4 + (half, cap - half) + (cap,) * 3

    def along_z(part, k):
        return lax.ppermute(part, "z", [(i, (i + k) % planes) for i in range(planes)])

    def far(part):
        return along_z(along_z(part, 7), 5)

    sent = deal(source, [as_rows(tokens)], sizes)
    token_parts = [sent[0]] + [along_z(sent[k], k) for k in (1, 2, 3, 4)]
    token_parts += [far(sent[5])] + [along_z(sent[k + 1], k) for k in (5, 6, 7)]

    def of_column(x):
        return lax.dynamic_index_in_dim(x.reshape(planes, places, rows), p, 1, keepdims=False)

    owner = of_column(row_adapter_index) // adapters
    hit = owner // places == z
    hop_slot = ((z - plane_at + planes) % planes * cap)[:, None] + before(
        jnp.broadcast_to(hit[:, None, :], (planes, rows, rows))
    )
    seat = (
        owner % places * (planes * CAP)
        + plane_at[:, None] * CAP
        + before(owner[:, :, None] == owner[:, None, :])
    )
    hop_slot = jnp.where(hit, hop_slot, -1).reshape(-1)
    seat = jnp.where(hit, seat, -1).reshape(-1)
    flat_hit = hit.reshape(-1)
    packed = jnp.where(
        flat_hit, before(jnp.broadcast_to(flat_hit[None, :], (planes * rows,) * 2)), -1
    )
    count = jnp.sum(flat_hit.astype(jnp.int32)).reshape(1)
    most_at = jnp.arange(most, dtype=jnp.int32)
    slot_seat = look_up(hop_slot, most_at, seat) - 1
    slot_row = look_up(hop_slot, most_at, packed) - 1
    row_seat = look_up(packed, most_at, seat) - 1
    seat_empty = (
        look_up(seat, jnp.arange(slots, dtype=jnp.int32), jnp.zeros_like(seat)) == 0
    ).astype(jnp.int32)

    def of_rows(x):
        return look_up(packed, most_at, of_column(x).reshape(-1)) - 1

    row_weight = 1.0 - 2.0 * of_rows(row_forget_flag).astype(jnp.float32)

    def in_plane(x):
        return lax.all_to_all(x, "p", split_axis=0, concat_axis=0, tiled=True)

    rest = (frozen_query, frozen_output, trained_keys, trained_values)
    gated = lax.optimization_barrier((source, token_parts[3], token_parts[6]))
    sent = deal(gated[0], [as_rows(x) for x in rest], sizes)
    ahead = [along_z(sent[k], k) for k in (1, 3)] + [along_z(sent[k + 1], k) for k in (5, 7)]
    relay = along_z(sent[5], 7)
    flat_tokens = in_plane(seat_rows(slot_seat, seat_empty, token_parts, slots)).reshape(-1, width)
    flat_tokens, relay, *ahead = lax.optimization_barrier((flat_tokens, relay, *ahead))
    payload = [sent[0], ahead[0], along_z(sent[2], 2), ahead[1], along_z(sent[4], 4)]
    payload += [along_z(relay, 5), ahead[2], along_z(sent[7], 6), ahead[3]]

    mine_all = (row_adapter_index // adapters).reshape(planes, places, rows) == z * places + p
    mine_all = jnp.swapaxes(mine_all, 0, 1).reshape(planes * places, rows)
    local = jnp.swapaxes(
        (row_adapter_index % adapters).reshape(planes, places, rows), 0, 1
    ).reshape(planes * places, rows)
    rank = before(jnp.broadcast_to(mine_all[:, None, :], (planes * places, rows, rows)))
    slot_adapter = jnp.sum(
        jnp.where(
            mine_all[:, None, :]
            & (rank[:, None, :] == jnp.arange(CAP, dtype=jnp.int32)[None, :, None]),
            local[:, None, :] + 1,
            0,
        ),
        axis=2,
    ).reshape(slots)
    mask = adapter_mask(slot_adapter, adapters)
    keys, values, per_key = gather_caches(prompt_key_cache, prompt_value_cache)

    delta, spread = owner_forward(flat_tokens, mask, down_flat, up_flat)
    gradient = attend_middle(
        slot_row,
        row_seat,
        count,
        payload,
        keys,
        values,
        (per_token(of_rows(row_prompt_length)), per_token(of_rows(row_prompt_index)))
        + (per_token(row_weight),),
        per_key,
        in_plane(delta.reshape(slots, QUERY_LENGTH, width)),
    )
    down, up = owner_backward(
        in_plane(gradient).reshape(-1, width), flat_tokens, mask, spread, up_flat
    )
    return down.reshape(adapter_down.shape), up.reshape(adapter_up.shape)


def per_device(*arrays):
    row_adapter_index = arrays[9]
    adapters = arrays[7].shape[0]
    planes = lax.axis_size("z")
    places = lax.axis_size("p")
    plane = (row_adapter_index // (adapters * places)).reshape(planes * places, -1)
    load = jnp.sum(
        (plane[:, None, :] == jnp.arange(planes, dtype=jnp.int32)[None, :, None]).astype(
            jnp.int32
        ),
        axis=2,
    )
    return lax.cond(
        jnp.max(load) <= HOP_CAP,
        functools.partial(two_hops, cap=HOP_CAP),
        one_hop,
        *arrays,
    )


def solution(mesh):
    tok_count, kv_count = mesh.devices.shape
    grid = Mesh(mesh.devices.reshape(PLANES, tok_count // PLANES, kv_count), ("z", "p", "kv"))
    return jax.shard_map(
        per_device,
        mesh=grid,
        in_specs=(
            P(TOK, "kv"),
            P(TOK, "kv"),
            P(TOK, "kv"),
            P(TOK, "kv"),
            P(TOK, "kv"),
            P(None, "kv", None),
            P(None, "kv", None),
            P(TOK, None, "kv"),
            P(TOK, None, "kv"),
            P(),
            P(),
            P(),
            P(),
        ),
        out_specs=(P(TOK, None, "kv"), P(TOK, None, "kv")),
        check_vma=False,
    )
```

```python
import functools
import math

import jax
import jax.numpy as jnp
from jax import lax
from jax.experimental import pallas as pl
from jax.experimental.pallas import tpu as pltpu
from jax.sharding import Mesh
from jax.sharding import PartitionSpec as P

QUERY_HEADS = 64
KEY_HEADS = 8
HEAD_WIDTH = 128
ADAPTER_RANK = 64
QUERY_LENGTH = 8
ADAPTER_SCALE = 0.5
CAP = 2
PLANES = 8
HOP_CAP = 10
TOK = ("z", "p")
ROW_BLOCK = 16
LOG2_E = math.log2(math.e)
VMEM_LIMIT = 56 * 1024 * 1024

_VMEM = pl.BlockSpec(memory_space=pltpu.VMEM)
_SMEM = pl.BlockSpec(memory_space=pltpu.SMEM)
_ANY = pl.BlockSpec(memory_space=pl.ANY)


def params():
    return pltpu.CompilerParams(vmem_limit_bytes=VMEM_LIMIT)


def fold(products, mask):
    kept = products * mask.astype(jnp.float32)
    half = kept[:, :128] + kept[:, 128:]
    return half + pltpu.roll(half, 64, 1)


def low_half(shape):
    return lax.broadcasted_iota(jnp.int32, shape, 1) < 64


def all_rows(refs):
    parts = [r[...] for r in refs]
    return parts[0] if len(parts) == 1 else jnp.concatenate(parts, axis=0)


def project_kernel(weight_ref, mask_ref, *refs):
    x_refs, out_ref, total_ref = refs[:-2], refs[-2], refs[-1]
    step = pl.program_id(0)
    product = lax.dot_general(
        all_rows(x_refs),
        weight_ref[...],
        (((1,), (1,)), ((), ())),
        preferred_element_type=jnp.float32,
    )

    @pl.when(step == 0)
    def _():
        total_ref[...] = product

    @pl.when(step > 0)
    def _():
        total_ref[...] += product

    @pl.when(step == pl.num_programs(0) - 1)
    def _():
        half = out_ref.shape[0]
        both = jnp.where(
            low_half(out_ref.shape),
            fold(total_ref[:half], mask_ref[:half]),
            fold(total_ref[half:], mask_ref[half:]),
        )
        out_ref[...] = both.astype(out_ref.dtype)


def column_blocks(parts, block):
    return [pl.BlockSpec((x.shape[0], block), lambda i: (0, i)) for x in parts]


def project(parts, mask, weight, out_type):
    tokens = sum(x.shape[0] for x in parts)
    ranks, width = weight.shape
    block = 512
    return pl.pallas_call(
        project_kernel,
        grid=(width // block,),
        in_specs=[
            pl.BlockSpec((ranks, block), lambda i: (0, i)),
            pl.BlockSpec((tokens, ranks), lambda i: (0, 0)),
        ]
        + column_blocks(parts, block),
        out_specs=pl.BlockSpec((tokens // 2, 128), lambda i: (0, 0)),
        out_shape=jax.ShapeDtypeStruct((tokens // 2, 128), out_type),
        scratch_shapes=[pltpu.VMEM((tokens, ranks), jnp.float32)],
        compiler_params=params(),
        name="project",
    )(weight, mask, *parts)


def spread_of(packed, mask, is_low):
    low = low_half(packed.shape)
    turned = pltpu.roll(packed, 64, 1)
    twice = jnp.where(low, packed, turned) if is_low else jnp.where(low, turned, packed)
    return (jnp.concatenate([twice, twice], axis=1) * mask.astype(jnp.float32)).astype(
        jnp.bfloat16
    )


def delta_kernel(p0, p1, p2, p3, mask_ref, weight_ref, *refs):
    out_refs, spread_ref = refs[:-1], refs[-1]
    half = p0.shape[0]

    @pl.when(pl.program_id(0) == 0)
    def _():
        total = (p0[...] + p1[...]) + (p2[...] + p3[...])
        low_rank = total.astype(jnp.bfloat16).astype(jnp.float32)
        spread_ref[:half] = spread_of(low_rank, mask_ref[:half], True)
        spread_ref[half:] = spread_of(low_rank, mask_ref[half:], False)

    delta = (
        ADAPTER_SCALE
        * jnp.dot(spread_ref[...], weight_ref[...], preferred_element_type=jnp.float32)
    ).astype(jnp.bfloat16)
    at = 0
    for out_ref in out_refs:
        out_ref[...] = delta[at : at + out_ref.shape[0]]
        at += out_ref.shape[0]


def make_delta(sums, mask, weight, count):
    half = sums[0].shape[0]
    tokens = 2 * half
    ranks, width = weight.shape
    block = 512
    outs = [jax.ShapeDtypeStruct((tokens // count, width), jnp.bfloat16)] * count
    *parts, spread = pl.pallas_call(
        delta_kernel,
        grid=(width // block,),
        in_specs=[pl.BlockSpec((half, 128), lambda i: (0, 0))] * 4
        + [
            pl.BlockSpec((tokens, ranks), lambda i: (0, 0)),
            pl.BlockSpec((ranks, block), lambda i: (0, i)),
        ],
        out_specs=column_blocks(outs, block)
        + [pl.BlockSpec((tokens, ranks), lambda i: (0, 0))],
        out_shape=outs + [jax.ShapeDtypeStruct((tokens, ranks), jnp.bfloat16)],
        compiler_params=params(),
        name="make_delta",
    )(*sums, mask, weight)
    return parts, spread


def grad_up_kernel(spread_ref, *refs):
    out_ref = refs[-1]
    out_ref[...] = (
        ADAPTER_SCALE
        * lax.dot_general(
            spread_ref[...],
            all_rows(refs[:-1]),
            (((0,), (0,)), ((), ())),
            preferred_element_type=jnp.float32,
        )
    ).astype(out_ref.dtype)


def grad_up(spread, parts):
    tokens, ranks = spread.shape
    width = parts[0].shape[1]
    block = 512
    return pl.pallas_call(
        grad_up_kernel,
        grid=(width // block,),
        in_specs=[pl.BlockSpec((tokens, ranks), lambda i: (0, 0))] + column_blocks(parts, block),
        out_specs=pl.BlockSpec((ranks, block), lambda i: (0, i)),
        out_shape=jax.ShapeDtypeStruct((ranks, width), jnp.bfloat16),
        compiler_params=params(),
        name="grad_up",
    )(spread, *parts)


def grad_down_kernel(p0, p1, p2, p3, mask_ref, *refs):
    x_refs, out_ref, spread_ref = refs[:-2], refs[-2], refs[-1]
    half = p0.shape[0]

    @pl.when(pl.program_id(0) == 0)
    def _():
        total = (p0[...].astype(jnp.float32) + p1[...].astype(jnp.float32)) + (
            p2[...].astype(jnp.float32) + p3[...].astype(jnp.float32)
        )
        low_grad = (ADAPTER_SCALE * total).astype(jnp.bfloat16).astype(jnp.float32)
        spread_ref[:half] = spread_of(low_grad, mask_ref[:half], True)
        spread_ref[half:] = spread_of(low_grad, mask_ref[half:], False)

    out_ref[...] = lax.dot_general(
        spread_ref[...],
        all_rows(x_refs),
        (((0,), (0,)), ((), ())),
        preferred_element_type=jnp.float32,
    ).astype(out_ref.dtype)


def grad_down(sums, mask, parts):
    half = sums[0].shape[0]
    tokens, ranks = mask.shape
    width = parts[0].shape[1]
    block = 512
    return pl.pallas_call(
        grad_down_kernel,
        grid=(width // block,),
        in_specs=[pl.BlockSpec((half, 128), lambda i: (0, 0))] * 4
        + [pl.BlockSpec((tokens, ranks), lambda i: (0, 0))]
        + column_blocks(parts, block),
        out_specs=pl.BlockSpec((ranks, block), lambda i: (0, i)),
        out_shape=jax.ShapeDtypeStruct((ranks, width), jnp.bfloat16),
        scratch_shapes=[pltpu.VMEM((tokens, ranks), jnp.bfloat16)],
        compiler_params=params(),
        name="grad_down",
    )(*sums, mask, *parts)


def heads_first(x, head_group):
    return jnp.concatenate(
        [x[:, h * HEAD_WIDTH : (h + 1) * HEAD_WIDTH] for h in range(head_group)], axis=0
    )


def by_rows(a, b):
    return lax.dot_general(a, b, (((1,), (1,)), ((), ())), preferred_element_type=jnp.float32)


def times(a, b):
    return jnp.dot(a, b, preferred_element_type=jnp.float32)


def attend_group(query, base, own_keys, own_values, keys, values, shared_seen, own_seen, weight):
    tokens = own_keys.shape[0]
    head_group = query.shape[1] // HEAD_WIDTH
    inv_root = 1.0 / math.sqrt(HEAD_WIDTH)
    query = heads_first(query, head_group).astype(jnp.bfloat16)
    base = heads_first(base, head_group)

    def group(x):
        return x.reshape(head_group, tokens, x.shape[-1])

    def flat(x):
        return x.reshape(head_group * tokens, x.shape[-1])

    shared = jnp.where(shared_seen[None], group(by_rows(query, keys)), -1e30)
    own = jnp.where(own_seen[None], group(by_rows(query, own_keys)), -1e30)
    top = jnp.maximum(
        jnp.max(shared, axis=-1, keepdims=True), jnp.max(own, axis=-1, keepdims=True)
    )
    shared = flat(jnp.exp2((shared - top) * (inv_root * LOG2_E)))
    own = flat(jnp.exp2((own - top) * (inv_root * LOG2_E)))
    total = jnp.sum(shared, axis=-1, keepdims=True) + jnp.sum(own, axis=-1, keepdims=True)
    scale = 1.0 / total
    attn_out = scale * (
        times(shared.astype(jnp.bfloat16), values) + times(own.astype(jnp.bfloat16), own_values)
    )
    grad_out = flat(group(attn_out - base) * weight[None]).astype(jnp.bfloat16)
    inner = jnp.sum(grad_out.astype(jnp.float32) * attn_out, axis=-1, keepdims=True)
    shared_gs = (shared * (by_rows(grad_out, values) - inner)).astype(jnp.bfloat16)
    own_gs = (own * (by_rows(grad_out, own_values) - inner)).astype(jnp.bfloat16)
    return (scale * inv_root) * (times(shared_gs, keys) + times(own_gs, own_keys))


def attend_block(b, load, delta_ref, grad_ref, key_ref, value_ref, vectors):
    row_len_ref, row_prompt_ref, row_weight_ref, key_prompt_ref, key_place_ref = vectors
    length = QUERY_LENGTH
    head_group = QUERY_HEADS // KEY_HEADS
    group_width = head_group * HEAD_WIDTH
    block_tokens = ROW_BLOCK * length
    block = pl.ds(b * ROW_BLOCK, ROW_BLOCK)
    tokens = pl.ds(b * block_tokens, block_tokens)
    shared_seen = (row_prompt_ref[tokens, :] == key_prompt_ref[...]) & (
        key_place_ref[...] < row_len_ref[tokens, :]
    )
    own_shape = (block_tokens, block_tokens)
    q_at = lax.broadcasted_iota(jnp.int32, own_shape, 0)
    k_at = lax.broadcasted_iota(jnp.int32, own_shape, 1)
    own_seen = (q_at // length == k_at // length) & (k_at <= q_at)
    weight = row_weight_ref[tokens, :]

    def two_d(x):
        return x.astype(jnp.float32).reshape(block_tokens, x.shape[-1])

    for g in range(key_ref.shape[1] // HEAD_WIDTH):
        columns = slice(g * group_width, (g + 1) * group_width)
        keys_at = slice(g * HEAD_WIDTH, (g + 1) * HEAD_WIDTH)
        gradient = attend_group(
            two_d(load("query", block, columns)) + two_d(delta_ref[block, :, columns]),
            two_d(load("base", block, columns)),
            two_d(load("key", block, keys_at)).astype(jnp.bfloat16),
            two_d(load("value", block, keys_at)).astype(jnp.bfloat16),
            key_ref[:, keys_at],
            value_ref[:, keys_at],
            shared_seen,
            own_seen,
            weight,
        )
        for h in range(head_group):
            piece = gradient[h * block_tokens : (h + 1) * block_tokens]
            at = g * group_width + h * HEAD_WIDTH
            grad_ref[block, :, at : at + HEAD_WIDTH] = piece.reshape(
                ROW_BLOCK, length, HEAD_WIDTH
            ).astype(jnp.bfloat16)


def attend_home_kernel(
    target_ref,
    query_ref,
    base_ref,
    own_key_ref,
    own_value_ref,
    key_ref,
    value_ref,
    row_len_ref,
    row_prompt_ref,
    row_weight_ref,
    key_prompt_ref,
    key_place_ref,
    delta_hbm,
    out_hbm,
    delta_ref,
    grad_ref,
    in_sem,
    out_sem,
):
    rows = query_ref.shape[0]
    refs = {"query": query_ref, "base": base_ref, "key": own_key_ref, "value": own_value_ref}
    vectors = (row_len_ref, row_prompt_ref, row_weight_ref, key_prompt_ref, key_place_ref)

    def fetch(r):
        return pltpu.make_async_copy(delta_hbm.at[target_ref[r]], delta_ref.at[r], in_sem.at[r])

    def send(r):
        return pltpu.make_async_copy(grad_ref.at[r], out_hbm.at[target_ref[r]], out_sem.at[r])

    for r in range(rows):
        fetch(r).start()
    for r in range(rows):
        fetch(r).wait()

    def load(name, block, columns):
        return refs[name][block, :, columns]

    def one_block(b, carry):
        attend_block(b, load, delta_ref, grad_ref, key_ref, value_ref, vectors)
        return carry

    lax.fori_loop(0, rows // ROW_BLOCK, one_block, 0)
    for r in range(rows):
        send(r).start()
    for r in range(rows):
        send(r).wait()


def attend_home(target, query, base, own_key, own_value, keys, values, per_token, per_key, delta):
    rows, length, width = query.shape
    return pl.pallas_call(
        attend_home_kernel,
        in_specs=[_SMEM] + [_VMEM] * 11 + [_ANY],
        out_specs=_ANY,
        out_shape=jax.ShapeDtypeStruct(delta.shape, delta.dtype),
        scratch_shapes=[
            pltpu.VMEM((rows, length, width), jnp.bfloat16),
            pltpu.VMEM((rows, length, width), jnp.bfloat16),
            pltpu.SemaphoreType.DMA((rows,)),
            pltpu.SemaphoreType.DMA((rows,)),
        ],
        input_output_aliases={12: 0},
        compiler_params=params(),
        name="attend_home",
    )(
        target,
        query,
        base,
        own_key,
        own_value,
        keys,
        values,
        *per_token,
        *per_key,
        delta,
    )


def each(first, last, do):
    def step(i, carry):
        do(i)
        return carry

    lax.fori_loop(first, last, step, 0)


def attend_middle_kernel(*refs, count, names):
    place_ref, seated_ref, total_ref = refs[:3]
    refs = refs[3:]
    payload_hbm, refs = refs[: len(names)], refs[len(names) :]
    key_ref, value_ref = refs[:2]
    vectors, refs = refs[2:7], refs[7:]
    delta_hbm, out_hbm, refs = refs[:count], refs[count : 2 * count], refs[2 * count :]
    payload_refs, refs = refs[: len(names)], refs[len(names) :]
    delta_ref, grad_ref, in_sem, delta_sem, out_sem = refs
    slots = payload_hbm[0].shape[0]
    seats = delta_hbm[0].shape[0]
    total = total_ref[0]
    blocks = (total + ROW_BLOCK - 1) // ROW_BLOCK
    where = {name: (n, at) for n, held in enumerate(names) for name, at in held}

    def fetch(do):
        def step(h):
            row = place_ref[h]

            @pl.when(row >= 0)
            def _():
                for n in range(len(names)):
                    do(
                        pltpu.make_async_copy(
                            payload_hbm[n].at[h], payload_refs[n].at[row], in_sem.at[h, n]
                        )
                    )

        each(0, slots, step)

    def seat(copy, do):
        for k in range(count):

            def step(j, k=k):
                row = seated_ref[k * seats + j]

                @pl.when(row >= 0)
                def _():
                    do(copy(k, j, row))

            each(0, seats, step)

    def fetch_delta(k, j, row):
        return pltpu.make_async_copy(
            delta_hbm[k].at[j], delta_ref.at[row], delta_sem.at[k * seats + j]
        )

    def send(k, j, row):
        return pltpu.make_async_copy(
            grad_ref.at[row], out_hbm[k].at[j], out_sem.at[k * seats + j]
        )

    def start(copy):
        copy.start()

    def wait(copy):
        copy.wait()

    fetch(start)
    seat(fetch_delta, start)

    def clear(i):
        for ref in payload_refs + (delta_ref,):
            ref[i] = jnp.zeros_like(ref[i])

    each(total, blocks * ROW_BLOCK, clear)
    fetch(wait)
    seat(fetch_delta, wait)

    def load(name, block, columns):
        n, at = where[name]
        return payload_refs[n][block, :, at + columns.start : at + columns.stop]

    each(
        0,
        blocks,
        lambda b: attend_block(b, load, delta_ref, grad_ref, key_ref, value_ref, vectors),
    )
    seat(send, start)
    seat(send, wait)


def attend_middle(place, seated, total, payload, names, keys, values, per_row, per_key, delta):
    slots, length = payload[0].shape[:2]
    seats, _, width = delta[0].shape
    count = len(delta)
    rows = slots + (-slots) % ROW_BLOCK
    first_delta = 3 + len(payload) + 7
    return pl.pallas_call(
        functools.partial(attend_middle_kernel, count=count, names=names),
        in_specs=[_SMEM] * 3 + [_ANY] * len(payload) + [_VMEM] * 7 + [_ANY] * count,
        out_specs=[_ANY] * count,
        out_shape=[jax.ShapeDtypeStruct(x.shape, x.dtype) for x in delta],
        scratch_shapes=[pltpu.VMEM((rows, length, x.shape[2]), x.dtype) for x in payload]
        + [
            pltpu.VMEM((rows, length, width), jnp.bfloat16),
            pltpu.VMEM((rows, length, width), jnp.bfloat16),
            pltpu.SemaphoreType.DMA((slots, len(payload))),
            pltpu.SemaphoreType.DMA((count * seats,)),
            pltpu.SemaphoreType.DMA((count * seats,)),
        ],
        input_output_aliases={first_delta + k: k for k in range(count)},
        compiler_params=params(),
        name="attend_middle",
    )(place, seated, total, *payload, keys, values, *per_row, *per_key, *delta)


def deal_kernel(source_ref, *refs, count, parts, fill):
    inputs, outs, zero_ref, sem = refs[:count], refs[count : count + parts], refs[-2], refs[-1]
    size = outs[0].shape[0]
    if fill:
        zero_ref[...] = jnp.zeros_like(zero_ref)

    def copies(do):
        for k, out in enumerate(outs):

            def step(j, k=k, out=out):
                slot = k * size + j
                row = source_ref[slot]

                @pl.when(row >= 0)
                def _():
                    at = 0
                    for n, x in enumerate(inputs):
                        width = x.shape[-1]
                        to = out.at[j] if count == 1 else out.at[j, :, pl.ds(at, width)]
                        do(pltpu.make_async_copy(x.at[row], to, sem.at[slot, n]))
                        at += width

                if fill:

                    @pl.when(row < 0)
                    def _():
                        do(pltpu.make_async_copy(zero_ref, out.at[j], sem.at[slot, 0]))

            each(0, size, step)

    copies(lambda copy: copy.start())
    copies(lambda copy: copy.wait())


def deal(source, arrays, parts, fill):
    length = arrays[0].shape[1]
    width = sum(x.shape[2] for x in arrays)
    slots = source.shape[0]
    return pl.pallas_call(
        functools.partial(deal_kernel, count=len(arrays), parts=parts, fill=fill),
        in_specs=[_SMEM] + [_VMEM] * len(arrays),
        out_specs=[_ANY] * parts,
        out_shape=[jax.ShapeDtypeStruct((slots // parts, length, width), arrays[0].dtype)] * parts,
        scratch_shapes=[
            pltpu.VMEM((length, width), jnp.bfloat16),
            pltpu.SemaphoreType.DMA((slots, len(arrays))),
        ],
        compiler_params=params(),
        name="deal",
    )(source, *arrays)


def shifted(block_for, count):
    return [
        lax.ppermute(block_for(k), "kv", [(i, (i + k) % count) for i in range(count)])
        for k in range(1, count)
    ]


def before(same):
    at = jnp.arange(same.shape[-1], dtype=jnp.int32)
    return jnp.sum((same & (at[:, None] > at[None, :])).astype(jnp.int32), axis=-1)


def look_up(keys, wanted, values):
    return jnp.sum(jnp.where(keys[None, :] == wanted[:, None], values[None, :] + 1, 0), axis=1)


def adapter_mask(slot_adapter, adapters):
    slots = slot_adapter.shape[0]
    lane_adapter = jnp.arange(adapters * ADAPTER_RANK, dtype=jnp.int32) // ADAPTER_RANK + 1
    return jnp.broadcast_to(
        (slot_adapter[:, None] == lane_adapter[None, :]).astype(jnp.bfloat16)[:, None, :],
        (slots, QUERY_LENGTH, lane_adapter.shape[0]),
    ).reshape(slots * QUERY_LENGTH, lane_adapter.shape[0])


def gather_caches(prompt_key_cache, prompt_value_cache):
    kv_count = lax.axis_size("kv")
    kv = lax.axis_index("kv")
    prompts, place_local = prompt_key_cache.shape[:2]
    head_columns = prompt_key_cache.shape[2] // kv_count
    both = jnp.stack([prompt_key_cache, prompt_value_cache]).reshape(
        2 * prompts * place_local, kv_count, head_columns
    )

    def cache_block(k):
        return lax.dynamic_index_in_dim(both, (kv + k) % kv_count, 1, keepdims=False)

    cache = jnp.stack([cache_block(0)] + shifted(cache_block, kv_count)).reshape(
        kv_count, 2, prompts * place_local, head_columns
    )
    key_at = jnp.arange(kv_count * prompts * place_local, dtype=jnp.int32)
    key_from = (kv - key_at // (prompts * place_local) + kv_count) % kv_count
    key_prompt = key_at // place_local % prompts
    key_place = key_from * place_local + key_at % place_local
    return (
        cache[:, 0].reshape(-1, head_columns),
        cache[:, 1].reshape(-1, head_columns),
        (key_prompt.reshape(1, -1), key_place.reshape(1, -1)),
    )


def per_token(x):
    return jnp.repeat(x, QUERY_LENGTH).reshape(-1, 1)


def as_rows(x):
    return x.reshape(x.shape[0] // QUERY_LENGTH, QUERY_LENGTH, x.shape[1])


def owner_forward(token_parts, mask, down_flat, up_flat):
    part = project(token_parts, mask, down_flat, jnp.float32)
    sums = [part] + shifted(lambda k: part, lax.axis_size("kv"))
    return make_delta(sums, mask, up_flat, len(token_parts))


def owner_backward(gradient_parts, token_parts, mask, spread, up_flat):
    part = project(gradient_parts, mask, up_flat, jnp.bfloat16)
    sums = [part] + shifted(lambda k: part, lax.axis_size("kv"))
    return grad_down(sums, mask, token_parts), grad_up(spread, gradient_parts)


def one_hop(
    tokens,
    frozen_query,
    trained_keys,
    trained_values,
    frozen_output,
    prompt_key_cache,
    prompt_value_cache,
    adapter_down,
    adapter_up,
    row_adapter_index,
    row_forget_flag,
    row_prompt_index,
    row_prompt_length,
):
    tok_count = lax.axis_size(TOK)
    me = lax.axis_index(TOK)
    rows = tokens.shape[0] // QUERY_LENGTH
    width = tokens.shape[1]
    adapters = adapter_down.shape[0]
    slots = tok_count * CAP
    down_flat = adapter_down.reshape(adapters * ADAPTER_RANK, width)
    up_flat = adapter_up.reshape(adapters * ADAPTER_RANK, width)

    mine = lax.dynamic_slice_in_dim(row_adapter_index, me * rows, rows) // adapters
    target = mine * CAP + before(mine[:, None] == mine[None, :])
    source = (
        look_up(
            target, jnp.arange(slots, dtype=jnp.int32), jnp.arange(rows, dtype=jnp.int32)
        )
        - 1
    )

    def exchange(x):
        return lax.all_to_all(x, TOK, split_axis=0, concat_axis=0, tiled=True)

    token_parts = [
        exchange(deal(source, [as_rows(tokens)], 1, True)[0]).reshape(-1, width)
    ]

    hit = (row_adapter_index // adapters).reshape(tok_count, rows) == me
    rank = before(jnp.broadcast_to(hit[:, None, :], (tok_count, rows, rows)))
    local_adapter = (row_adapter_index % adapters).reshape(tok_count, rows)
    slot_adapter = jnp.sum(
        jnp.where(
            hit[:, None, :]
            & (rank[:, None, :] == jnp.arange(CAP, dtype=jnp.int32)[None, :, None]),
            local_adapter[:, None, :] + 1,
            0,
        ),
        axis=2,
    ).reshape(slots)
    mask = adapter_mask(slot_adapter, adapters)
    keys, values, per_key = gather_caches(prompt_key_cache, prompt_value_cache)

    def of_mine(x):
        return lax.dynamic_slice_in_dim(x, me * rows, rows)

    (delta,), spread = owner_forward(token_parts, mask, down_flat, up_flat)
    gradient = attend_home(
        target,
        as_rows(frozen_query),
        as_rows(frozen_output),
        as_rows(trained_keys),
        as_rows(trained_values),
        keys,
        values,
        (
            per_token(of_mine(row_prompt_length)),
            per_token(of_mine(row_prompt_index)),
            per_token(1.0 - 2.0 * of_mine(row_forget_flag).astype(jnp.float32)),
        ),
        per_key,
        exchange(delta.reshape(slots, QUERY_LENGTH, width)),
    )
    down, up = owner_backward(
        [exchange(gradient).reshape(-1, width)], token_parts, mask, spread, up_flat
    )
    return down.reshape(adapter_down.shape), up.reshape(adapter_up.shape)


def two_hops(
    tokens,
    frozen_query,
    trained_keys,
    trained_values,
    frozen_output,
    prompt_key_cache,
    prompt_value_cache,
    adapter_down,
    adapter_up,
    row_adapter_index,
    row_forget_flag,
    row_prompt_index,
    row_prompt_length,
    *,
    cap,
):
    planes = lax.axis_size("z")
    places = lax.axis_size("p")
    z = lax.axis_index("z")
    p = lax.axis_index("p")
    rows = tokens.shape[0] // QUERY_LENGTH
    width = tokens.shape[1]
    adapters = adapter_down.shape[0]
    seats = planes * CAP
    most = planes * cap
    down_flat = adapter_down.reshape(adapters * ADAPTER_RANK, width)
    up_flat = adapter_up.reshape(adapters * ADAPTER_RANK, width)
    row_at = jnp.arange(rows, dtype=jnp.int32)
    plane_at = jnp.arange(planes, dtype=jnp.int32)
    place_at = jnp.arange(places, dtype=jnp.int32)
    most_at = jnp.arange(most, dtype=jnp.int32)

    mine = lax.dynamic_slice_in_dim(row_adapter_index, (z * places + p) * rows, rows) // adapters
    my_plane = mine // places
    my_slot = my_plane * cap + before(my_plane[:, None] == my_plane[None, :])
    source = look_up(my_slot, most_at, row_at) - 1

    def dealt(*arrays):
        return deal(source, [as_rows(x) for x in arrays], 1, False)[0]

    def along_z(x):
        return lax.all_to_all(x, "z", split_axis=0, concat_axis=0, tiled=True)

    def partner(place, k):
        return (place // 2 + k // 2) % (places // 2) * 2 + (place + k) % 2

    def in_plane(parts, back=False):
        out = [parts[0]]
        for k in range(1, places):
            pairs = [(i, partner(i, k)) for i in range(places)]
            out.append(lax.ppermute(parts[k], "p", [(j, i) if back else (i, j) for i, j in pairs]))
        return out

    def part_of(place):
        return (place // 2 - p // 2 + places // 2) % (places // 2) * 2 + (place + p) % 2

    sent = dealt(tokens)
    moved_tokens = along_z(sent)

    def of_column(x):
        return lax.dynamic_index_in_dim(x.reshape(planes, places, rows), p, 1, keepdims=False)

    owner = of_column(row_adapter_index) // adapters
    hit = owner // places == z
    hop_slot = (plane_at * cap)[:, None] + before(
        jnp.broadcast_to(hit[:, None, :], (planes, rows, rows))
    )
    seat = (
        part_of(owner % places) * seats
        + plane_at[:, None] * CAP
        + before(owner[:, :, None] == owner[:, None, :])
    )
    hop_slot = jnp.where(hit, hop_slot, -1).reshape(-1)
    seat = jnp.where(hit, seat, -1).reshape(-1)
    flat_hit = hit.reshape(-1)
    packed = jnp.where(
        flat_hit, before(jnp.broadcast_to(flat_hit[None, :], (planes * rows,) * 2)), -1
    )
    total = jnp.sum(flat_hit.astype(jnp.int32)).reshape(1)
    seat_at = jnp.arange(places * seats, dtype=jnp.int32)
    seat_slot = look_up(seat, seat_at, hop_slot) - 1
    seat_row = look_up(seat, seat_at, packed) - 1
    slot_row = look_up(hop_slot, most_at, packed) - 1
    row_key = jnp.arange(most + (-most) % ROW_BLOCK, dtype=jnp.int32)

    def of_rows(x):
        return look_up(packed, row_key, of_column(x).reshape(-1)) - 1

    per_row = (
        per_token(of_rows(row_prompt_length)),
        per_token(of_rows(row_prompt_index)),
        per_token(1.0 - 2.0 * of_rows(row_forget_flag).astype(jnp.float32)),
    )

    def by_seat(x):
        homes = x.reshape(planes, places, rows)
        from_place = (p // 2 - place_at // 2 + places // 2) % (places // 2) * 2 + (
            p + place_at
        ) % 2
        pick = from_place[:, None] == place_at[None, :]
        return jnp.sum(
            jnp.where(pick[:, None, :, None], homes[None], 0), axis=2
        ).reshape(planes * places, rows)

    adapter_by_seat = by_seat(row_adapter_index)
    here = adapter_by_seat // adapters == z * places + p
    rank = before(jnp.broadcast_to(here[:, None, :], (planes * places, rows, rows)))
    slot_adapter = jnp.sum(
        jnp.where(
            here[:, None, :]
            & (rank[:, None, :] == jnp.arange(CAP, dtype=jnp.int32)[None, :, None]),
            (adapter_by_seat % adapters)[:, None, :] + 1,
            0,
        ),
        axis=2,
    ).reshape(places * seats)
    base = dealt(frozen_output)
    query = dealt(frozen_query, trained_keys, trained_values)
    kv_width = trained_keys.shape[1]
    names = (("query", 0), ("key", width), ("value", width + kv_width)), (("base", 0),)
    mask = adapter_mask(slot_adapter, adapters)
    caches = gather_caches(
        *lax.optimization_barrier((prompt_key_cache, prompt_value_cache, sent))[:2]
    )
    moved_tokens, base, query, mask, caches, per_row, seat_slot, seat_row, slot_row, total = (
        lax.optimization_barrier(
            (
                moved_tokens,
                base,
                query,
                mask,
                caches,
                per_row,
                seat_slot,
                seat_row,
                slot_row,
                total,
            )
        )
    )
    keys, values, per_key = caches

    base = along_z(base)
    token_parts = [
        x.reshape(-1, width) for x in in_plane(deal(seat_slot, [moved_tokens], places, True))
    ]
    base, query, *token_parts = lax.optimization_barrier((base, query, *token_parts))
    query = along_z(query)

    delta, spread = owner_forward(token_parts, mask, down_flat, up_flat)
    delta = in_plane([x.reshape(seats, QUERY_LENGTH, width) for x in delta], back=True)
    gradient = attend_middle(
        slot_row, seat_row, total, (query, base), names, keys, values, per_row, per_key, delta
    )
    gradient = [x.reshape(-1, width) for x in in_plane(gradient)]
    down, up = owner_backward(gradient, token_parts, mask, spread, up_flat)
    return down.reshape(adapter_down.shape), up.reshape(adapter_up.shape)


def per_device(*arrays):
    row_adapter_index = arrays[9]
    adapters = arrays[7].shape[0]
    planes = lax.axis_size("z")
    places = lax.axis_size("p")
    plane = (row_adapter_index // (adapters * places)).reshape(planes * places, -1)
    load = jnp.sum(
        (plane[:, None, :] == jnp.arange(planes, dtype=jnp.int32)[None, :, None]).astype(
            jnp.int32
        ),
        axis=2,
    )
    return lax.cond(
        jnp.max(load) <= HOP_CAP,
        functools.partial(two_hops, cap=HOP_CAP),
        one_hop,
        *arrays,
    )


def solution(mesh):
    tok_count, kv_count = mesh.devices.shape
    grid = Mesh(mesh.devices.reshape(PLANES, tok_count // PLANES, kv_count), ("z", "p", "kv"))
    return jax.shard_map(
        per_device,
        mesh=grid,
        in_specs=(
            P(TOK, "kv"),
            P(TOK, "kv"),
            P(TOK, "kv"),
            P(TOK, "kv"),
            P(TOK, "kv"),
            P(None, "kv", None),
            P(None, "kv", None),
            P(TOK, None, "kv"),
            P(TOK, None, "kv"),
            P(),
            P(),
            P(),
            P(),
        ),
        out_specs=(P(TOK, None, "kv"), P(TOK, None, "kv")),
        check_vma=False,
    )
```

```python
import functools
import math

import jax
import jax.numpy as jnp
from jax import lax
from jax.experimental import pallas as pl
from jax.experimental.pallas import tpu as pltpu
from jax.sharding import Mesh
from jax.sharding import PartitionSpec as P

QUERY_HEADS = 64
KEY_HEADS = 8
HEAD_WIDTH = 128
ADAPTER_RANK = 64
QUERY_LENGTH = 8
ADAPTER_SCALE = 0.5
CAP = 2
PLANES = 8
HOP_CAP = 10
TOK = ("z", "p")
ROW_BLOCK = 16
LOG2_E = math.log2(math.e)
VMEM_LIMIT = 56 * 1024 * 1024

_VMEM = pl.BlockSpec(memory_space=pltpu.VMEM)
_SMEM = pl.BlockSpec(memory_space=pltpu.SMEM)
_ANY = pl.BlockSpec(memory_space=pl.ANY)


def params():
    return pltpu.CompilerParams(vmem_limit_bytes=VMEM_LIMIT)


def fold(products, mask):
    kept = products * mask.astype(jnp.float32)
    half = kept[:, :128] + kept[:, 128:]
    return half + pltpu.roll(half, 64, 1)


def low_half(shape):
    return lax.broadcasted_iota(jnp.int32, shape, 1) < 64


def all_rows(refs):
    parts = [r[...] for r in refs]
    return parts[0] if len(parts) == 1 else jnp.concatenate(parts, axis=0)


def project_kernel(weight_ref, mask_ref, *refs, started):
    x_refs, out_ref, total_ref = refs[:-2], refs[-2], refs[-1]
    start_ref = None
    if started:
        start_ref, x_refs = x_refs[0], x_refs[1:]
    step = pl.program_id(0)
    product = lax.dot_general(
        all_rows(x_refs),
        weight_ref[...],
        (((1,), (1,)), ((), ())),
        preferred_element_type=jnp.float32,
    )

    @pl.when(step == 0)
    def _():
        total_ref[...] = product

    @pl.when(step > 0)
    def _():
        total_ref[...] += product

    @pl.when(step == pl.num_programs(0) - 1)
    def _():
        half = out_ref.shape[0]
        both = jnp.where(
            low_half(out_ref.shape),
            fold(total_ref[:half], mask_ref[:half]),
            fold(total_ref[half:], mask_ref[half:]),
        )
        if started:
            both = both + start_ref[...]
        out_ref[...] = both.astype(out_ref.dtype)


def column_blocks(parts, block):
    return [pl.BlockSpec((x.shape[0], block), lambda i: (0, i)) for x in parts]


def project(parts, mask, weight, out_type, piece=0, first=0, start=None):
    tokens = sum(x.shape[0] for x in parts)
    ranks = weight.shape[0]
    width = parts[0].shape[1]
    block = 512
    packed = pl.BlockSpec((tokens // 2, 128), lambda i: (0, 0))
    return pl.pallas_call(
        functools.partial(project_kernel, started=start is not None),
        grid=(width // block,),
        in_specs=[
            pl.BlockSpec((ranks, block), lambda i: (0, i + first // block)),
            pl.BlockSpec((tokens, ranks), lambda i: (piece, 0)),
        ]
        + [packed] * (start is not None)
        + column_blocks(parts, block),
        out_specs=packed,
        out_shape=jax.ShapeDtypeStruct((tokens // 2, 128), out_type),
        scratch_shapes=[pltpu.VMEM((tokens, ranks), jnp.float32)],
        compiler_params=params(),
        name="project",
    )(weight, mask, *([] if start is None else [start]), *parts)


def spread_of(packed, mask, is_low):
    low = low_half(packed.shape)
    turned = pltpu.roll(packed, 64, 1)
    twice = jnp.where(low, packed, turned) if is_low else jnp.where(low, turned, packed)
    return (jnp.concatenate([twice, twice], axis=1) * mask.astype(jnp.float32)).astype(
        jnp.bfloat16
    )


def delta_kernel(p0, p1, p2, p3, mask_ref, weight_ref, *refs):
    out_refs, spread_ref = refs[:-1], refs[-1]
    half = p0.shape[0]

    @pl.when(pl.program_id(0) == 0)
    def _():
        total = (p0[...] + p1[...]) + (p2[...] + p3[...])
        low_rank = total.astype(jnp.bfloat16).astype(jnp.float32)
        spread_ref[:half] = spread_of(low_rank, mask_ref[:half], True)
        spread_ref[half:] = spread_of(low_rank, mask_ref[half:], False)

    delta = (
        ADAPTER_SCALE
        * jnp.dot(spread_ref[...], weight_ref[...], preferred_element_type=jnp.float32)
    ).astype(jnp.bfloat16)
    at = 0
    for out_ref in out_refs:
        out_ref[...] = delta[at : at + out_ref.shape[0]]
        at += out_ref.shape[0]


def make_delta(sums, mask, weight, count, piece=0):
    half = sums[0].shape[0]
    tokens = 2 * half
    ranks, width = weight.shape
    block = 512
    outs = [jax.ShapeDtypeStruct((tokens // count, width), jnp.bfloat16)] * count
    *parts, spread = pl.pallas_call(
        delta_kernel,
        grid=(width // block,),
        in_specs=[pl.BlockSpec((half, 128), lambda i: (0, 0))] * 4
        + [
            pl.BlockSpec((tokens, ranks), lambda i: (piece, 0)),
            pl.BlockSpec((ranks, block), lambda i: (0, i)),
        ],
        out_specs=column_blocks(outs, block)
        + [pl.BlockSpec((tokens, ranks), lambda i: (0, 0))],
        out_shape=outs + [jax.ShapeDtypeStruct((tokens, ranks), jnp.bfloat16)],
        compiler_params=params(),
        name="make_delta",
    )(*sums, mask, weight)
    return parts, spread


def grad_up_kernel(*refs, spreads, given):
    out_ref = refs[-1]
    out_ref[...] = (
        ADAPTER_SCALE
        * lax.dot_general(
            all_rows(refs[:spreads]),
            all_rows(refs[spreads + given : -1]),
            (((0,), (0,)), ((), ())),
            preferred_element_type=jnp.float32,
        )
    ).astype(out_ref.dtype)


def grad_up(spreads, parts, width, first=0, given=()):
    ranks = spreads[0].shape[1]
    block = 512
    return pl.pallas_call(
        functools.partial(grad_up_kernel, spreads=len(spreads), given=len(given)),
        grid=(parts[0].shape[1] // block,),
        in_specs=[pl.BlockSpec(x.shape, lambda i: (0, 0)) for x in spreads]
        + [_ANY] * len(given)
        + column_blocks(parts, block),
        out_specs=pl.BlockSpec((ranks, block), lambda i: (0, i + first // block)),
        out_shape=jax.ShapeDtypeStruct((ranks, width), jnp.bfloat16),
        input_output_aliases={len(spreads): 0} if given else {},
        compiler_params=params(),
        name="grad_up",
    )(*spreads, *given, *parts)


def grad_down_kernel(p0, p1, p2, p3, mask_ref, *refs):
    x_refs, out_ref, spread_ref = refs[:-2], refs[-2], refs[-1]
    half = p0.shape[0]

    @pl.when(pl.program_id(0) == 0)
    def _():
        total = (p0[...].astype(jnp.float32) + p1[...].astype(jnp.float32)) + (
            p2[...].astype(jnp.float32) + p3[...].astype(jnp.float32)
        )
        low_grad = (ADAPTER_SCALE * total).astype(jnp.bfloat16).astype(jnp.float32)
        spread_ref[:half] = spread_of(low_grad, mask_ref[:half], True)
        spread_ref[half:] = spread_of(low_grad, mask_ref[half:], False)

    out_ref[...] = lax.dot_general(
        spread_ref[...],
        all_rows(x_refs),
        (((0,), (0,)), ((), ())),
        preferred_element_type=jnp.float32,
    ).astype(out_ref.dtype)


def grad_down(sums, mask, parts):
    half = sums[0].shape[0]
    tokens, ranks = mask.shape
    width = parts[0].shape[1]
    block = 512
    return pl.pallas_call(
        grad_down_kernel,
        grid=(width // block,),
        in_specs=[pl.BlockSpec((half, 128), lambda i: (0, 0))] * 4
        + [pl.BlockSpec((tokens, ranks), lambda i: (0, 0))]
        + column_blocks(parts, block),
        out_specs=pl.BlockSpec((ranks, block), lambda i: (0, i)),
        out_shape=jax.ShapeDtypeStruct((ranks, width), jnp.bfloat16),
        scratch_shapes=[pltpu.VMEM((tokens, ranks), jnp.bfloat16)],
        compiler_params=params(),
        name="grad_down",
    )(*sums, mask, *parts)


def heads_first(x, head_group):
    return jnp.concatenate(
        [x[:, h * HEAD_WIDTH : (h + 1) * HEAD_WIDTH] for h in range(head_group)], axis=0
    )


def by_rows(a, b):
    return lax.dot_general(a, b, (((1,), (1,)), ((), ())), preferred_element_type=jnp.float32)


def times(a, b):
    return jnp.dot(a, b, preferred_element_type=jnp.float32)


def attend_group(query, base, own_keys, own_values, keys, values, shared_seen, own_seen, weight):
    tokens = own_keys.shape[0]
    head_group = query.shape[1] // HEAD_WIDTH
    inv_root = 1.0 / math.sqrt(HEAD_WIDTH)
    query = heads_first(query, head_group).astype(jnp.bfloat16)
    base = heads_first(base, head_group)

    def group(x):
        return x.reshape(head_group, tokens, x.shape[-1])

    def flat(x):
        return x.reshape(head_group * tokens, x.shape[-1])

    shared = jnp.where(shared_seen[None], group(by_rows(query, keys)), -1e30)
    own = jnp.where(own_seen[None], group(by_rows(query, own_keys)), -1e30)
    top = jnp.maximum(
        jnp.max(shared, axis=-1, keepdims=True), jnp.max(own, axis=-1, keepdims=True)
    )
    shared = flat(jnp.exp2((shared - top) * (inv_root * LOG2_E)))
    own = flat(jnp.exp2((own - top) * (inv_root * LOG2_E)))
    total = jnp.sum(shared, axis=-1, keepdims=True) + jnp.sum(own, axis=-1, keepdims=True)
    scale = 1.0 / total
    attn_out = scale * (
        times(shared.astype(jnp.bfloat16), values) + times(own.astype(jnp.bfloat16), own_values)
    )
    grad_out = flat(group(attn_out - base) * weight[None]).astype(jnp.bfloat16)
    inner = jnp.sum(grad_out.astype(jnp.float32) * attn_out, axis=-1, keepdims=True)
    shared_gs = (shared * (by_rows(grad_out, values) - inner)).astype(jnp.bfloat16)
    own_gs = (own * (by_rows(grad_out, own_values) - inner)).astype(jnp.bfloat16)
    return (scale * inv_root) * (times(shared_gs, keys) + times(own_gs, own_keys))


def attend_block(b, load, delta_ref, grad_ref, key_ref, value_ref, vectors):
    row_len_ref, row_prompt_ref, row_weight_ref, key_prompt_ref, key_place_ref = vectors
    length = QUERY_LENGTH
    head_group = QUERY_HEADS // KEY_HEADS
    group_width = head_group * HEAD_WIDTH
    block_tokens = ROW_BLOCK * length
    block = pl.ds(b * ROW_BLOCK, ROW_BLOCK)
    tokens = pl.ds(b * block_tokens, block_tokens)
    shared_seen = (row_prompt_ref[tokens, :] == key_prompt_ref[...]) & (
        key_place_ref[...] < row_len_ref[tokens, :]
    )
    own_shape = (block_tokens, block_tokens)
    q_at = lax.broadcasted_iota(jnp.int32, own_shape, 0)
    k_at = lax.broadcasted_iota(jnp.int32, own_shape, 1)
    own_seen = (q_at // length == k_at // length) & (k_at <= q_at)
    weight = row_weight_ref[tokens, :]

    def two_d(x):
        return x.astype(jnp.float32).reshape(block_tokens, x.shape[-1])

    for g in range(key_ref.shape[1] // HEAD_WIDTH):
        columns = slice(g * group_width, (g + 1) * group_width)
        keys_at = slice(g * HEAD_WIDTH, (g + 1) * HEAD_WIDTH)
        gradient = attend_group(
            two_d(load("query", block, columns)) + two_d(delta_ref[block, :, columns]),
            two_d(load("base", block, columns)),
            two_d(load("key", block, keys_at)).astype(jnp.bfloat16),
            two_d(load("value", block, keys_at)).astype(jnp.bfloat16),
            key_ref[:, keys_at],
            value_ref[:, keys_at],
            shared_seen,
            own_seen,
            weight,
        )
        for h in range(head_group):
            piece = gradient[h * block_tokens : (h + 1) * block_tokens]
            at = g * group_width + h * HEAD_WIDTH
            grad_ref[block, :, at : at + HEAD_WIDTH] = piece.reshape(
                ROW_BLOCK, length, HEAD_WIDTH
            ).astype(jnp.bfloat16)


def attend_home_kernel(
    target_ref,
    query_ref,
    base_ref,
    own_key_ref,
    own_value_ref,
    key_ref,
    value_ref,
    row_len_ref,
    row_prompt_ref,
    row_weight_ref,
    key_prompt_ref,
    key_place_ref,
    delta_hbm,
    out_hbm,
    delta_ref,
    grad_ref,
    in_sem,
    out_sem,
):
    rows = query_ref.shape[0]
    refs = {"query": query_ref, "base": base_ref, "key": own_key_ref, "value": own_value_ref}
    vectors = (row_len_ref, row_prompt_ref, row_weight_ref, key_prompt_ref, key_place_ref)

    def fetch(r):
        return pltpu.make_async_copy(delta_hbm.at[target_ref[r]], delta_ref.at[r], in_sem.at[r])

    def send(r):
        return pltpu.make_async_copy(grad_ref.at[r], out_hbm.at[target_ref[r]], out_sem.at[r])

    for r in range(rows):
        fetch(r).start()
    for r in range(rows):
        fetch(r).wait()

    def load(name, block, columns):
        return refs[name][block, :, columns]

    def one_block(b, carry):
        attend_block(b, load, delta_ref, grad_ref, key_ref, value_ref, vectors)
        return carry

    lax.fori_loop(0, rows // ROW_BLOCK, one_block, 0)
    for r in range(rows):
        send(r).start()
    for r in range(rows):
        send(r).wait()


def attend_home(target, query, base, own_key, own_value, keys, values, per_token, per_key, delta):
    rows, length, width = query.shape
    return pl.pallas_call(
        attend_home_kernel,
        in_specs=[_SMEM] + [_VMEM] * 11 + [_ANY],
        out_specs=_ANY,
        out_shape=jax.ShapeDtypeStruct(delta.shape, delta.dtype),
        scratch_shapes=[
            pltpu.VMEM((rows, length, width), jnp.bfloat16),
            pltpu.VMEM((rows, length, width), jnp.bfloat16),
            pltpu.SemaphoreType.DMA((rows,)),
            pltpu.SemaphoreType.DMA((rows,)),
        ],
        input_output_aliases={12: 0},
        compiler_params=params(),
        name="attend_home",
    )(
        target,
        query,
        base,
        own_key,
        own_value,
        keys,
        values,
        *per_token,
        *per_key,
        delta,
    )


def each(first, last, do):
    def step(i, carry):
        do(i)
        return carry

    lax.fori_loop(first, last, step, 0)


def attend_middle_kernel(*refs, count, names, first):
    place_ref, seated_ref, total_ref = refs[:3]
    refs = refs[3:]
    payload_hbm, refs = refs[: len(names)], refs[len(names) :]
    key_ref, value_ref = refs[:2]
    vectors, refs = refs[2:7], refs[7:]
    delta_hbm, out_hbm, refs = refs[:count], refs[count : 2 * count], refs[2 * count :]
    payload_refs, refs = refs[: len(names)], refs[len(names) :]
    delta_ref, grad_ref, zero_ref, in_sem, delta_sem, out_sem = refs
    slots = payload_hbm[0].shape[0]
    seats, _, width = out_hbm[0].shape
    total = total_ref[0]
    blocks = (total + ROW_BLOCK - 1) // ROW_BLOCK
    where = {name: (n, at) for n, held in enumerate(names) for name, at in held}

    def start(copy):
        copy.start()

    def wait(copy):
        copy.wait()

    def fetch(do):
        def step(h):
            row = place_ref[h]

            @pl.when(row >= 0)
            def _():
                for n in range(len(names)):
                    do(
                        pltpu.make_async_copy(
                            payload_hbm[n].at[h], payload_refs[n].at[row], in_sem.at[h, n]
                        )
                    )

        each(0, slots, step)

    def seat(do, copy, empty=None):
        for k in range(count):

            def step(j, k=k):
                row = seated_ref[k * seats + j]

                @pl.when(row >= 0)
                def _():
                    do(copy(k, j, row))

                if empty is not None:

                    @pl.when(row < 0)
                    def _():
                        do(empty(k, j))

            each(0, seats, step)

    def fetch_delta(k, j, row):
        return pltpu.make_async_copy(
            delta_hbm[k].at[j, :, pl.ds(first, width)],
            delta_ref.at[row],
            delta_sem.at[k * seats + j],
        )

    def send(k, j, row):
        return pltpu.make_async_copy(
            grad_ref.at[row], out_hbm[k].at[j], out_sem.at[k * seats + j]
        )

    def send_zero(k, j):
        return pltpu.make_async_copy(zero_ref, out_hbm[k].at[j], out_sem.at[k * seats + j])

    fetch(start)
    seat(start, fetch_delta)
    zero_ref[...] = jnp.zeros_like(zero_ref)

    def clear(i):
        for ref in payload_refs + (delta_ref,):
            ref[i] = jnp.zeros_like(ref[i])

    each(total, blocks * ROW_BLOCK, clear)
    fetch(wait)
    seat(wait, fetch_delta)

    def load(name, block, columns):
        n, at = where[name]
        return payload_refs[n][block, :, at + columns.start : at + columns.stop]

    each(
        0,
        blocks,
        lambda b: attend_block(b, load, delta_ref, grad_ref, key_ref, value_ref, vectors),
    )
    seat(start, send, send_zero)
    seat(wait, send, send_zero)


def attend_middle(place, seated, total, payload, names, keys, values, per_row, per_key, delta, g):
    slots, length = payload[0].shape[:2]
    seats = delta[0].shape[0]
    count = len(delta)
    width = QUERY_HEADS // KEY_HEADS * HEAD_WIDTH
    rows = slots + (-slots) % ROW_BLOCK
    out = jax.ShapeDtypeStruct((seats, length, width), jnp.bfloat16)
    return pl.pallas_call(
        functools.partial(attend_middle_kernel, count=count, names=names, first=g * width),
        in_specs=[_SMEM] * 3 + [_ANY] * len(payload) + [_VMEM] * 7 + [_ANY] * count,
        out_specs=[_ANY] * count,
        out_shape=[out] * count,
        scratch_shapes=[pltpu.VMEM((rows, length, x.shape[2]), x.dtype) for x in payload]
        + [
            pltpu.VMEM((rows, length, width), jnp.bfloat16),
            pltpu.VMEM((rows, length, width), jnp.bfloat16),
            pltpu.VMEM((length, width), jnp.bfloat16),
            pltpu.SemaphoreType.DMA((slots, len(payload))),
            pltpu.SemaphoreType.DMA((count * seats,)),
            pltpu.SemaphoreType.DMA((count * seats,)),
        ],
        compiler_params=params(),
        name="attend_middle",
    )(place, seated, total, *payload, keys, values, *per_row, *per_key, *delta)


def deal_kernel(source_ref, *refs, count, parts, fill, windows):
    inputs, outs, zero_ref, sem = refs[:count], refs[count : count + parts], refs[-2], refs[-1]
    size = outs[0].shape[0]
    if fill:
        zero_ref[...] = jnp.zeros_like(zero_ref)

    def copies(do):
        for k, out in enumerate(outs):

            def step(j, k=k, out=out):
                slot = k * size + j
                row = source_ref[slot]

                @pl.when(row >= 0)
                def _():
                    at = 0
                    for n, (x, (first, width)) in enumerate(zip(inputs, windows)):
                        of = x.at[row] if width == x.shape[-1] else x.at[row, :, pl.ds(first, width)]
                        to = out.at[j] if count == 1 else out.at[j, :, pl.ds(at, width)]
                        do(pltpu.make_async_copy(of, to, sem.at[slot, n]))
                        at += width

                if fill:

                    @pl.when(row < 0)
                    def _():
                        do(pltpu.make_async_copy(zero_ref, out.at[j], sem.at[slot, 0]))

            each(0, size, step)

    copies(lambda copy: copy.start())
    copies(lambda copy: copy.wait())


def deal(source, arrays, parts, fill, windows=None):
    length = arrays[0].shape[1]
    windows = windows or [(0, x.shape[2]) for x in arrays]
    width = sum(w for _, w in windows)
    slots = source.shape[0]
    return pl.pallas_call(
        functools.partial(
            deal_kernel, count=len(arrays), parts=parts, fill=fill, windows=windows
        ),
        in_specs=[_SMEM] + [_VMEM] * len(arrays),
        out_specs=[_ANY] * parts,
        out_shape=[jax.ShapeDtypeStruct((slots // parts, length, width), arrays[0].dtype)] * parts,
        scratch_shapes=[
            pltpu.VMEM((length, width), jnp.bfloat16),
            pltpu.SemaphoreType.DMA((slots, len(arrays))),
        ],
        compiler_params=params(),
        name="deal",
    )(source, *arrays)


def shifted(block_for, count):
    return [
        lax.ppermute(block_for(k), "kv", [(i, (i + k) % count) for i in range(count)])
        for k in range(1, count)
    ]


def before(same):
    at = jnp.arange(same.shape[-1], dtype=jnp.int32)
    return jnp.sum((same & (at[:, None] > at[None, :])).astype(jnp.int32), axis=-1)


def look_up(keys, wanted, values):
    return jnp.sum(jnp.where(keys[None, :] == wanted[:, None], values[None, :] + 1, 0), axis=1)


def adapter_mask(slot_adapter, adapters):
    slots = slot_adapter.shape[0]
    lane_adapter = jnp.arange(adapters * ADAPTER_RANK, dtype=jnp.int32) // ADAPTER_RANK + 1
    return jnp.broadcast_to(
        (slot_adapter[:, None] == lane_adapter[None, :]).astype(jnp.bfloat16)[:, None, :],
        (slots, QUERY_LENGTH, lane_adapter.shape[0]),
    ).reshape(slots * QUERY_LENGTH, lane_adapter.shape[0])


def gather_caches(prompt_key_cache, prompt_value_cache):
    kv_count = lax.axis_size("kv")
    kv = lax.axis_index("kv")
    prompts, place_local = prompt_key_cache.shape[:2]
    head_columns = prompt_key_cache.shape[2] // kv_count
    both = jnp.stack([prompt_key_cache, prompt_value_cache]).reshape(
        2 * prompts * place_local, kv_count, head_columns
    )

    def cache_block(k):
        return lax.dynamic_index_in_dim(both, (kv + k) % kv_count, 1, keepdims=False)

    cache = jnp.stack([cache_block(0)] + shifted(cache_block, kv_count)).reshape(
        kv_count, 2, prompts * place_local, head_columns
    )
    key_at = jnp.arange(kv_count * prompts * place_local, dtype=jnp.int32)
    key_from = (kv - key_at // (prompts * place_local) + kv_count) % kv_count
    key_prompt = key_at // place_local % prompts
    key_place = key_from * place_local + key_at % place_local
    return (
        cache[:, 0].reshape(-1, head_columns),
        cache[:, 1].reshape(-1, head_columns),
        (key_prompt.reshape(1, -1), key_place.reshape(1, -1)),
    )


def per_token(x):
    return jnp.repeat(x, QUERY_LENGTH).reshape(-1, 1)


def as_rows(x):
    return x.reshape(x.shape[0] // QUERY_LENGTH, QUERY_LENGTH, x.shape[1])


def over_kv(part):
    return [part] + shifted(lambda k: part, lax.axis_size("kv"))


def one_hop(
    tokens,
    frozen_query,
    trained_keys,
    trained_values,
    frozen_output,
    prompt_key_cache,
    prompt_value_cache,
    adapter_down,
    adapter_up,
    row_adapter_index,
    row_forget_flag,
    row_prompt_index,
    row_prompt_length,
):
    tok_count = lax.axis_size(TOK)
    me = lax.axis_index(TOK)
    rows = tokens.shape[0] // QUERY_LENGTH
    width = tokens.shape[1]
    adapters = adapter_down.shape[0]
    slots = tok_count * CAP
    down_flat = adapter_down.reshape(adapters * ADAPTER_RANK, width)
    up_flat = adapter_up.reshape(adapters * ADAPTER_RANK, width)

    mine = lax.dynamic_slice_in_dim(row_adapter_index, me * rows, rows) // adapters
    target = mine * CAP + before(mine[:, None] == mine[None, :])
    source = (
        look_up(
            target, jnp.arange(slots, dtype=jnp.int32), jnp.arange(rows, dtype=jnp.int32)
        )
        - 1
    )

    def exchange(x):
        return lax.all_to_all(x, TOK, split_axis=0, concat_axis=0, tiled=True)

    token_parts = [
        exchange(deal(source, [as_rows(tokens)], 1, True)[0]).reshape(-1, width)
    ]

    hit = (row_adapter_index // adapters).reshape(tok_count, rows) == me
    rank = before(jnp.broadcast_to(hit[:, None, :], (tok_count, rows, rows)))
    local_adapter = (row_adapter_index % adapters).reshape(tok_count, rows)
    slot_adapter = jnp.sum(
        jnp.where(
            hit[:, None, :]
            & (rank[:, None, :] == jnp.arange(CAP, dtype=jnp.int32)[None, :, None]),
            local_adapter[:, None, :] + 1,
            0,
        ),
        axis=2,
    ).reshape(slots)
    mask = adapter_mask(slot_adapter, adapters)
    keys, values, per_key = gather_caches(prompt_key_cache, prompt_value_cache)

    def of_mine(x):
        return lax.dynamic_slice_in_dim(x, me * rows, rows)

    sums = over_kv(project(token_parts, mask, down_flat, jnp.float32))
    (delta,), spread = make_delta(sums, mask, up_flat, 1)
    gradient = attend_home(
        target,
        as_rows(frozen_query),
        as_rows(frozen_output),
        as_rows(trained_keys),
        as_rows(trained_values),
        keys,
        values,
        (
            per_token(of_mine(row_prompt_length)),
            per_token(of_mine(row_prompt_index)),
            per_token(1.0 - 2.0 * of_mine(row_forget_flag).astype(jnp.float32)),
        ),
        per_key,
        exchange(delta.reshape(slots, QUERY_LENGTH, width)),
    )
    gradient = [exchange(gradient).reshape(-1, width)]
    sums = over_kv(project(gradient, mask, up_flat, jnp.bfloat16))
    up = grad_up([spread], gradient, width)
    down = grad_down(sums, mask, token_parts)
    return down.reshape(adapter_down.shape), up.reshape(adapter_up.shape)


def two_hops(
    tokens,
    frozen_query,
    trained_keys,
    trained_values,
    frozen_output,
    prompt_key_cache,
    prompt_value_cache,
    adapter_down,
    adapter_up,
    row_adapter_index,
    row_forget_flag,
    row_prompt_index,
    row_prompt_length,
    *,
    cap,
):
    planes = lax.axis_size("z")
    places = lax.axis_size("p")
    z = lax.axis_index("z")
    p = lax.axis_index("p")
    rows = tokens.shape[0] // QUERY_LENGTH
    width = tokens.shape[1]
    adapters = adapter_down.shape[0]
    seats = planes * CAP
    most = planes * cap
    down_flat = adapter_down.reshape(adapters * ADAPTER_RANK, width)
    up_flat = adapter_up.reshape(adapters * ADAPTER_RANK, width)
    row_at = jnp.arange(rows, dtype=jnp.int32)
    plane_at = jnp.arange(planes, dtype=jnp.int32)
    place_at = jnp.arange(places, dtype=jnp.int32)
    most_at = jnp.arange(most, dtype=jnp.int32)

    mine = lax.dynamic_slice_in_dim(row_adapter_index, (z * places + p) * rows, rows) // adapters
    my_plane = mine // places
    my_slot = my_plane * cap + before(my_plane[:, None] == my_plane[None, :])
    source = look_up(my_slot, most_at, row_at) - 1

    def dealt(*arrays, windows=None):
        return deal(source, [as_rows(x) for x in arrays], 1, False, windows)[0]

    def along_z(x):
        return lax.all_to_all(x, "z", split_axis=0, concat_axis=0, tiled=True)

    def partner(place, k):
        return (place // 2 + k // 2) % (places // 2) * 2 + (place + k) % 2

    def in_plane(parts, first=0, back=False):
        out = []
        for k, part in enumerate(parts, first):
            pairs = [(i, partner(i, k)) for i in range(places)]
            if k:
                part = lax.ppermute(part, "p", [(j, i) if back else (i, j) for i, j in pairs])
            out.append(part)
        return out

    def part_of(place):
        return (place // 2 - p // 2 + places // 2) % (places // 2) * 2 + (place + p) % 2

    sent = dealt(tokens)
    moved_tokens = along_z(sent)

    def of_column(x):
        return lax.dynamic_index_in_dim(x.reshape(planes, places, rows), p, 1, keepdims=False)

    owner = of_column(row_adapter_index) // adapters
    hit = owner // places == z
    hop_slot = (plane_at * cap)[:, None] + before(
        jnp.broadcast_to(hit[:, None, :], (planes, rows, rows))
    )
    seat = (
        part_of(owner % places) * seats
        + plane_at[:, None] * CAP
        + before(owner[:, :, None] == owner[:, None, :])
    )
    hop_slot = jnp.where(hit, hop_slot, -1).reshape(-1)
    seat = jnp.where(hit, seat, -1).reshape(-1)
    flat_hit = hit.reshape(-1)
    packed = jnp.where(
        flat_hit, before(jnp.broadcast_to(flat_hit[None, :], (planes * rows,) * 2)), -1
    )
    total = jnp.sum(flat_hit.astype(jnp.int32)).reshape(1)
    seat_at = jnp.arange(places * seats, dtype=jnp.int32)
    seat_slot = look_up(seat, seat_at, hop_slot) - 1
    seat_row = look_up(seat, seat_at, packed) - 1
    slot_row = look_up(hop_slot, most_at, packed) - 1
    row_key = jnp.arange(most + (-most) % ROW_BLOCK, dtype=jnp.int32)

    def of_rows(x):
        return look_up(packed, row_key, of_column(x).reshape(-1)) - 1

    per_row = (
        per_token(of_rows(row_prompt_length)),
        per_token(of_rows(row_prompt_index)),
        per_token(1.0 - 2.0 * of_rows(row_forget_flag).astype(jnp.float32)),
    )

    def by_seat(x):
        homes = x.reshape(planes, places, rows)
        from_place = (p // 2 - place_at // 2 + places // 2) % (places // 2) * 2 + (
            p + place_at
        ) % 2
        pick = from_place[:, None] == place_at[None, :]
        return jnp.sum(
            jnp.where(pick[:, None, :, None], homes[None], 0), axis=2
        ).reshape(planes * places, rows)

    adapter_by_seat = by_seat(row_adapter_index)
    here = adapter_by_seat // adapters == z * places + p
    rank = before(jnp.broadcast_to(here[:, None, :], (planes * places, rows, rows)))
    slot_adapter = jnp.sum(
        jnp.where(
            here[:, None, :]
            & (rank[:, None, :] == jnp.arange(CAP, dtype=jnp.int32)[None, :, None]),
            (adapter_by_seat % adapters)[:, None, :] + 1,
            0,
        ),
        axis=2,
    ).reshape(places * seats)
    half = width // 2
    kv_width = trained_keys.shape[1]
    payload0 = dealt(
        frozen_query,
        frozen_output,
        trained_keys,
        trained_values,
        windows=[(0, half), (0, half), (0, kv_width), (0, kv_width)],
    )
    payload1 = dealt(frozen_query, frozen_output, windows=[(half, half), (half, half)])
    mask = adapter_mask(slot_adapter, adapters)
    keys, values, per_key = gather_caches(
        *lax.optimization_barrier((prompt_key_cache, prompt_value_cache, sent))[:2]
    )
    keys = [keys[:, :HEAD_WIDTH], keys[:, HEAD_WIDTH:]]
    values = [values[:, :HEAD_WIDTH], values[:, HEAD_WIDTH:]]
    moved_tokens, payload0, payload1, mask, keys, values, per_key, per_row, tables = (
        lax.optimization_barrier(
            (
                moved_tokens,
                payload0,
                payload1,
                mask,
                keys,
                values,
                per_key,
                per_row,
                (seat_slot, seat_row, slot_row, total),
            )
        )
    )
    seat_slot, seat_row, slot_row, total = tables

    payload0 = along_z(payload0)
    tokens_at = [x.reshape(-1, width) for x in deal(seat_slot, [moved_tokens], places, True)]
    cut = places // 2
    early = in_plane(tokens_at[:cut])
    late = in_plane(tokens_at[cut:], first=cut)

    def as_seats(x):
        return x.reshape(seats, QUERY_LENGTH, width)

    sums = over_kv(project(early, mask, down_flat, jnp.float32))
    made, early_spread = make_delta(sums, mask, up_flat, cut)
    delta = in_plane([as_seats(x) for x in made], back=True)
    late, _ = lax.optimization_barrier((late, made))
    sums = over_kv(project(late, mask, down_flat, jnp.float32, piece=1))
    sums, delta, payload0, payload1 = lax.optimization_barrier((sums, delta, payload0, payload1))
    payload1 = along_z(payload1)
    made, late_spread = make_delta(sums, mask, up_flat, places - cut, piece=1)
    delta = delta + in_plane([as_seats(x) for x in made], first=cut, back=True)

    def attend(payload, names, g):
        gradient = attend_middle(
            slot_row,
            seat_row,
            total,
            payload,
            names,
            keys[g],
            values[g],
            per_row,
            per_key,
            delta,
            g,
        )
        return [x.reshape(-1, half) for x in in_plane(gradient)]

    def own(g):
        key = 2 * half + g * HEAD_WIDTH
        return (("key", key), ("value", key + kv_width))

    shared = (("query", 0), ("base", half))
    gradient0 = attend([payload0], (shared + own(0),), 0)
    payload1, gradient0 = lax.optimization_barrier((payload1, gradient0))
    gradient1 = attend([payload1, payload0], (shared, own(1)), 1)

    spreads = [early_spread, late_spread]
    part = project(gradient0, mask, up_flat, jnp.float32)
    up = grad_up(spreads, gradient0, width)
    part = project(gradient1, mask, up_flat, jnp.bfloat16, first=half, start=part)
    sums = over_kv(part)
    up = grad_up(spreads, gradient1, width, first=half, given=[up])
    down = grad_down(sums, mask, early + late)
    return down.reshape(adapter_down.shape), up.reshape(adapter_up.shape)


def per_device(*arrays):
    row_adapter_index = arrays[9]
    adapters = arrays[7].shape[0]
    planes = lax.axis_size("z")
    places = lax.axis_size("p")
    plane = (row_adapter_index // (adapters * places)).reshape(planes * places, -1)
    load = jnp.sum(
        (plane[:, None, :] == jnp.arange(planes, dtype=jnp.int32)[None, :, None]).astype(
            jnp.int32
        ),
        axis=2,
    )
    return lax.cond(
        jnp.max(load) <= HOP_CAP,
        functools.partial(two_hops, cap=HOP_CAP),
        one_hop,
        *arrays,
    )


def solution(mesh):
    tok_count, kv_count = mesh.devices.shape
    grid = Mesh(mesh.devices.reshape(PLANES, tok_count // PLANES, kv_count), ("z", "p", "kv"))
    return jax.shard_map(
        per_device,
        mesh=grid,
        in_specs=(
            P(TOK, "kv"),
            P(TOK, "kv"),
            P(TOK, "kv"),
            P(TOK, "kv"),
            P(TOK, "kv"),
            P(None, "kv", None),
            P(None, "kv", None),
            P(TOK, None, "kv"),
            P(TOK, None, "kv"),
            P(),
            P(),
            P(),
            P(),
        ),
        out_specs=(P(TOK, None, "kv"), P(TOK, None, "kv")),
        check_vma=False,
    )
```

```python
import functools
import math

import jax
import jax.numpy as jnp
from jax import lax
from jax.experimental import pallas as pl
from jax.experimental.pallas import tpu as pltpu
from jax.sharding import Mesh
from jax.sharding import PartitionSpec as P

QUERY_HEADS = 64
KEY_HEADS = 8
HEAD_WIDTH = 128
ADAPTER_RANK = 64
QUERY_LENGTH = 8
ADAPTER_SCALE = 0.5
CAP = 2
PLANES = 8
HOP_CAP = 10
TOK = ("z", "p")
ROW_BLOCK = 16
LOG2_E = math.log2(math.e)
VMEM_LIMIT = 56 * 1024 * 1024

_VMEM = pl.BlockSpec(memory_space=pltpu.VMEM)
_SMEM = pl.BlockSpec(memory_space=pltpu.SMEM)
_ANY = pl.BlockSpec(memory_space=pl.ANY)


def params():
    return pltpu.CompilerParams(vmem_limit_bytes=VMEM_LIMIT)


def fold(products, mask):
    kept = products * mask.astype(jnp.float32)
    half = kept[:, :128] + kept[:, 128:]
    return half + pltpu.roll(half, 64, 1)


def low_half(shape):
    return lax.broadcasted_iota(jnp.int32, shape, 1) < 64


def all_rows(refs):
    parts = [r[...] for r in refs]
    return parts[0] if len(parts) == 1 else jnp.concatenate(parts, axis=0)


def project_kernel(weight_ref, mask_ref, *refs):
    x_refs, out_ref, total_ref = refs[:-2], refs[-2], refs[-1]
    step = pl.program_id(0)
    product = lax.dot_general(
        all_rows(x_refs),
        weight_ref[...],
        (((1,), (1,)), ((), ())),
        preferred_element_type=jnp.float32,
    )

    @pl.when(step == 0)
    def _():
        total_ref[...] = product

    @pl.when(step > 0)
    def _():
        total_ref[...] += product

    @pl.when(step == pl.num_programs(0) - 1)
    def _():
        half = out_ref.shape[0]
        both = jnp.where(
            low_half(out_ref.shape),
            fold(total_ref[:half], mask_ref[:half]),
            fold(total_ref[half:], mask_ref[half:]),
        )
        out_ref[...] = both.astype(out_ref.dtype)


def column_blocks(parts, block):
    return [pl.BlockSpec((x.shape[0], block), lambda i: (0, i)) for x in parts]


def project(parts, mask, weight, out_type):
    tokens = sum(x.shape[0] for x in parts)
    ranks, width = weight.shape
    block = 512
    return pl.pallas_call(
        project_kernel,
        grid=(width // block,),
        in_specs=[
            pl.BlockSpec((ranks, block), lambda i: (0, i)),
            pl.BlockSpec((tokens, ranks), lambda i: (0, 0)),
        ]
        + column_blocks(parts, block),
        out_specs=pl.BlockSpec((tokens // 2, 128), lambda i: (0, 0)),
        out_shape=jax.ShapeDtypeStruct((tokens // 2, 128), out_type),
        scratch_shapes=[pltpu.VMEM((tokens, ranks), jnp.float32)],
        compiler_params=params(),
        name="project",
    )(weight, mask, *parts)


def spread_of(packed, mask, is_low):
    low = low_half(packed.shape)
    turned = pltpu.roll(packed, 64, 1)
    twice = jnp.where(low, packed, turned) if is_low else jnp.where(low, turned, packed)
    return (jnp.concatenate([twice, twice], axis=1) * mask.astype(jnp.float32)).astype(
        jnp.bfloat16
    )


def delta_kernel(p0, p1, p2, p3, mask_ref, weight_ref, *refs):
    out_refs, spread_ref = refs[:-1], refs[-1]
    half = p0.shape[0]

    @pl.when(pl.program_id(0) == 0)
    def _():
        total = (p0[...].astype(jnp.float32) + p1[...].astype(jnp.float32)) + (
            p2[...].astype(jnp.float32) + p3[...].astype(jnp.float32)
        )
        low_rank = total.astype(jnp.bfloat16).astype(jnp.float32)
        spread_ref[:half] = spread_of(low_rank, mask_ref[:half], True)
        spread_ref[half:] = spread_of(low_rank, mask_ref[half:], False)

    delta = (
        ADAPTER_SCALE
        * jnp.dot(spread_ref[...], weight_ref[...], preferred_element_type=jnp.float32)
    ).astype(jnp.bfloat16)
    at = 0
    for out_ref in out_refs:
        out_ref[...] = delta[at : at + out_ref.shape[0]]
        at += out_ref.shape[0]


def make_delta(sums, mask, weight, count):
    half = sums[0].shape[0]
    tokens = 2 * half
    ranks, width = weight.shape
    block = 512
    outs = [jax.ShapeDtypeStruct((tokens // count, width), jnp.bfloat16)] * count
    *parts, spread = pl.pallas_call(
        delta_kernel,
        grid=(width // block,),
        in_specs=[pl.BlockSpec((half, 128), lambda i: (0, 0))] * 4
        + [
            pl.BlockSpec((tokens, ranks), lambda i: (0, 0)),
            pl.BlockSpec((ranks, block), lambda i: (0, i)),
        ],
        out_specs=column_blocks(outs, block)
        + [pl.BlockSpec((tokens, ranks), lambda i: (0, 0))],
        out_shape=outs + [jax.ShapeDtypeStruct((tokens, ranks), jnp.bfloat16)],
        compiler_params=params(),
        name="make_delta",
    )(*sums, mask, weight)
    return parts, spread


def grad_up_kernel(spread_ref, *refs):
    out_ref = refs[-1]
    out_ref[...] = (
        ADAPTER_SCALE
        * lax.dot_general(
            spread_ref[...],
            all_rows(refs[:-1]),
            (((0,), (0,)), ((), ())),
            preferred_element_type=jnp.float32,
        )
    ).astype(out_ref.dtype)


def grad_up(spread, parts):
    tokens, ranks = spread.shape
    width = parts[0].shape[1]
    block = 512
    return pl.pallas_call(
        grad_up_kernel,
        grid=(width // block,),
        in_specs=[pl.BlockSpec((tokens, ranks), lambda i: (0, 0))] + column_blocks(parts, block),
        out_specs=pl.BlockSpec((ranks, block), lambda i: (0, i)),
        out_shape=jax.ShapeDtypeStruct((ranks, width), jnp.bfloat16),
        compiler_params=params(),
        name="grad_up",
    )(spread, *parts)


def grad_down_kernel(p0, p1, p2, p3, mask_ref, *refs):
    x_refs, out_ref, spread_ref = refs[:-2], refs[-2], refs[-1]
    half = p0.shape[0]

    @pl.when(pl.program_id(0) == 0)
    def _():
        total = (p0[...].astype(jnp.float32) + p1[...].astype(jnp.float32)) + (
            p2[...].astype(jnp.float32) + p3[...].astype(jnp.float32)
        )
        low_grad = (ADAPTER_SCALE * total).astype(jnp.bfloat16).astype(jnp.float32)
        spread_ref[:half] = spread_of(low_grad, mask_ref[:half], True)
        spread_ref[half:] = spread_of(low_grad, mask_ref[half:], False)

    out_ref[...] = lax.dot_general(
        spread_ref[...],
        all_rows(x_refs),
        (((0,), (0,)), ((), ())),
        preferred_element_type=jnp.float32,
    ).astype(out_ref.dtype)


def grad_down(sums, mask, parts):
    half = sums[0].shape[0]
    tokens, ranks = mask.shape
    width = parts[0].shape[1]
    block = 512
    return pl.pallas_call(
        grad_down_kernel,
        grid=(width // block,),
        in_specs=[pl.BlockSpec((half, 128), lambda i: (0, 0))] * 4
        + [pl.BlockSpec((tokens, ranks), lambda i: (0, 0))]
        + column_blocks(parts, block),
        out_specs=pl.BlockSpec((ranks, block), lambda i: (0, i)),
        out_shape=jax.ShapeDtypeStruct((ranks, width), jnp.bfloat16),
        scratch_shapes=[pltpu.VMEM((tokens, ranks), jnp.bfloat16)],
        compiler_params=params(),
        name="grad_down",
    )(*sums, mask, *parts)


def heads_first(x, head_group):
    return jnp.concatenate(
        [x[:, h * HEAD_WIDTH : (h + 1) * HEAD_WIDTH] for h in range(head_group)], axis=0
    )


def by_rows(a, b):
    return lax.dot_general(a, b, (((1,), (1,)), ((), ())), preferred_element_type=jnp.float32)


def times(a, b):
    return jnp.dot(a, b, preferred_element_type=jnp.float32)


def attend_group(query, base, own_keys, own_values, keys, values, shared_seen, own_seen, weight):
    tokens = own_keys.shape[0]
    head_group = query.shape[1] // HEAD_WIDTH
    inv_root = 1.0 / math.sqrt(HEAD_WIDTH)
    query = heads_first(query, head_group).astype(jnp.bfloat16)
    base = heads_first(base, head_group)

    def group(x):
        return x.reshape(head_group, tokens, x.shape[-1])

    def flat(x):
        return x.reshape(head_group * tokens, x.shape[-1])

    shared = jnp.where(shared_seen[None], group(by_rows(query, keys)), -1e30)
    own = jnp.where(own_seen[None], group(by_rows(query, own_keys)), -1e30)
    top = jnp.maximum(
        jnp.max(shared, axis=-1, keepdims=True), jnp.max(own, axis=-1, keepdims=True)
    )
    shared = flat(jnp.exp2((shared - top) * (inv_root * LOG2_E)))
    own = flat(jnp.exp2((own - top) * (inv_root * LOG2_E)))
    total = jnp.sum(shared, axis=-1, keepdims=True) + jnp.sum(own, axis=-1, keepdims=True)
    scale = 1.0 / total
    attn_out = scale * (
        times(shared.astype(jnp.bfloat16), values) + times(own.astype(jnp.bfloat16), own_values)
    )
    grad_out = flat(group(attn_out - base) * weight[None]).astype(jnp.bfloat16)
    inner = jnp.sum(grad_out.astype(jnp.float32) * attn_out, axis=-1, keepdims=True)
    shared_gs = (shared * (by_rows(grad_out, values) - inner)).astype(jnp.bfloat16)
    own_gs = (own * (by_rows(grad_out, own_values) - inner)).astype(jnp.bfloat16)
    return (scale * inv_root) * (times(shared_gs, keys) + times(own_gs, own_keys))


def attend_block(b, load, delta_ref, grad_ref, key_ref, value_ref, vectors):
    row_len_ref, row_prompt_ref, row_weight_ref, key_prompt_ref, key_place_ref = vectors
    length = QUERY_LENGTH
    head_group = QUERY_HEADS // KEY_HEADS
    group_width = head_group * HEAD_WIDTH
    block_tokens = ROW_BLOCK * length
    block = pl.ds(b * ROW_BLOCK, ROW_BLOCK)
    tokens = pl.ds(b * block_tokens, block_tokens)
    shared_seen = (row_prompt_ref[tokens, :] == key_prompt_ref[...]) & (
        key_place_ref[...] < row_len_ref[tokens, :]
    )
    own_shape = (block_tokens, block_tokens)
    q_at = lax.broadcasted_iota(jnp.int32, own_shape, 0)
    k_at = lax.broadcasted_iota(jnp.int32, own_shape, 1)
    own_seen = (q_at // length == k_at // length) & (k_at <= q_at)
    weight = row_weight_ref[tokens, :]

    def two_d(x):
        return x.astype(jnp.float32).reshape(block_tokens, x.shape[-1])

    for g in range(key_ref.shape[1] // HEAD_WIDTH):
        columns = slice(g * group_width, (g + 1) * group_width)
        keys_at = slice(g * HEAD_WIDTH, (g + 1) * HEAD_WIDTH)
        gradient = attend_group(
            two_d(load("query", block, columns)) + two_d(delta_ref[block, :, columns]),
            two_d(load("base", block, columns)),
            two_d(load("key", block, keys_at)).astype(jnp.bfloat16),
            two_d(load("value", block, keys_at)).astype(jnp.bfloat16),
            key_ref[:, keys_at],
            value_ref[:, keys_at],
            shared_seen,
            own_seen,
            weight,
        )
        for h in range(head_group):
            piece = gradient[h * block_tokens : (h + 1) * block_tokens]
            at = g * group_width + h * HEAD_WIDTH
            grad_ref[block, :, at : at + HEAD_WIDTH] = piece.reshape(
                ROW_BLOCK, length, HEAD_WIDTH
            ).astype(jnp.bfloat16)


def attend_home_kernel(
    target_ref,
    query_ref,
    base_ref,
    own_key_ref,
    own_value_ref,
    key_ref,
    value_ref,
    row_len_ref,
    row_prompt_ref,
    row_weight_ref,
    key_prompt_ref,
    key_place_ref,
    delta_hbm,
    out_hbm,
    delta_ref,
    grad_ref,
    in_sem,
    out_sem,
):
    rows = query_ref.shape[0]
    refs = {"query": query_ref, "base": base_ref, "key": own_key_ref, "value": own_value_ref}
    vectors = (row_len_ref, row_prompt_ref, row_weight_ref, key_prompt_ref, key_place_ref)

    def fetch(r):
        return pltpu.make_async_copy(delta_hbm.at[target_ref[r]], delta_ref.at[r], in_sem.at[r])

    def send(r):
        return pltpu.make_async_copy(grad_ref.at[r], out_hbm.at[target_ref[r]], out_sem.at[r])

    for r in range(rows):
        fetch(r).start()
    for r in range(rows):
        fetch(r).wait()

    def load(name, block, columns):
        return refs[name][block, :, columns]

    def one_block(b, carry):
        attend_block(b, load, delta_ref, grad_ref, key_ref, value_ref, vectors)
        return carry

    lax.fori_loop(0, rows // ROW_BLOCK, one_block, 0)
    for r in range(rows):
        send(r).start()
    for r in range(rows):
        send(r).wait()


def attend_home(target, query, base, own_key, own_value, keys, values, per_token, per_key, delta):
    rows, length, width = query.shape
    return pl.pallas_call(
        attend_home_kernel,
        in_specs=[_SMEM] + [_VMEM] * 11 + [_ANY],
        out_specs=_ANY,
        out_shape=jax.ShapeDtypeStruct(delta.shape, delta.dtype),
        scratch_shapes=[
            pltpu.VMEM((rows, length, width), jnp.bfloat16),
            pltpu.VMEM((rows, length, width), jnp.bfloat16),
            pltpu.SemaphoreType.DMA((rows,)),
            pltpu.SemaphoreType.DMA((rows,)),
        ],
        input_output_aliases={12: 0},
        compiler_params=params(),
        name="attend_home",
    )(
        target,
        query,
        base,
        own_key,
        own_value,
        keys,
        values,
        *per_token,
        *per_key,
        delta,
    )


def each(first, last, do):
    def step(i, carry):
        do(i)
        return carry

    lax.fori_loop(first, last, step, 0)


def attend_middle_kernel(*refs, count, names):
    place_ref, seated_ref, total_ref = refs[:3]
    refs = refs[3:]
    payload_hbm, refs = refs[: len(names)], refs[len(names) :]
    key_ref, value_ref = refs[:2]
    vectors, refs = refs[2:7], refs[7:]
    delta_hbm, out_hbm, refs = refs[:count], refs[count : 2 * count], refs[2 * count :]
    payload_refs, refs = refs[: len(names)], refs[len(names) :]
    delta_ref, grad_ref, in_sem, delta_sem, out_sem = refs
    slots = payload_hbm[0].shape[0]
    seats = delta_hbm[0].shape[0]
    total = total_ref[0]
    blocks = (total + ROW_BLOCK - 1) // ROW_BLOCK
    where = {name: (n, at) for n, held in enumerate(names) for name, at in held}

    def fetch(do):
        def step(h):
            row = place_ref[h]

            @pl.when(row >= 0)
            def _():
                for n in range(len(names)):
                    do(
                        pltpu.make_async_copy(
                            payload_hbm[n].at[h], payload_refs[n].at[row], in_sem.at[h, n]
                        )
                    )

        each(0, slots, step)

    def seat(copy, do):
        for k in range(count):

            def step(j, k=k):
                row = seated_ref[k * seats + j]

                @pl.when(row >= 0)
                def _():
                    do(copy(k, j, row))

            each(0, seats, step)

    def fetch_delta(k, j, row):
        return pltpu.make_async_copy(
            delta_hbm[k].at[j], delta_ref.at[row], delta_sem.at[k * seats + j]
        )

    def send(k, j, row):
        return pltpu.make_async_copy(
            grad_ref.at[row], out_hbm[k].at[j], out_sem.at[k * seats + j]
        )

    def start(copy):
        copy.start()

    def wait(copy):
        copy.wait()

    fetch(start)
    seat(fetch_delta, start)

    def clear(i):
        for ref in payload_refs + (delta_ref,):
            ref[i] = jnp.zeros_like(ref[i])

    each(total, blocks * ROW_BLOCK, clear)
    fetch(wait)
    seat(fetch_delta, wait)

    def load(name, block, columns):
        n, at = where[name]
        return payload_refs[n][block, :, at + columns.start : at + columns.stop]

    each(
        0,
        blocks,
        lambda b: attend_block(b, load, delta_ref, grad_ref, key_ref, value_ref, vectors),
    )
    seat(send, start)
    seat(send, wait)


def attend_middle(place, seated, total, payload, names, keys, values, per_row, per_key, delta):
    slots, length = payload[0].shape[:2]
    seats, _, width = delta[0].shape
    count = len(delta)
    rows = slots + (-slots) % ROW_BLOCK
    first_delta = 3 + len(payload) + 7
    return pl.pallas_call(
        functools.partial(attend_middle_kernel, count=count, names=names),
        in_specs=[_SMEM] * 3 + [_ANY] * len(payload) + [_VMEM] * 7 + [_ANY] * count,
        out_specs=[_ANY] * count,
        out_shape=[jax.ShapeDtypeStruct(x.shape, x.dtype) for x in delta],
        scratch_shapes=[pltpu.VMEM((rows, length, x.shape[2]), x.dtype) for x in payload]
        + [
            pltpu.VMEM((rows, length, width), jnp.bfloat16),
            pltpu.VMEM((rows, length, width), jnp.bfloat16),
            pltpu.SemaphoreType.DMA((slots, len(payload))),
            pltpu.SemaphoreType.DMA((count * seats,)),
            pltpu.SemaphoreType.DMA((count * seats,)),
        ],
        input_output_aliases={first_delta + k: k for k in range(count)},
        compiler_params=params(),
        name="attend_middle",
    )(place, seated, total, *payload, keys, values, *per_row, *per_key, *delta)


def deal_kernel(source_ref, *refs, count, parts, fill):
    inputs, outs, zero_ref, sem = refs[:count], refs[count : count + parts], refs[-2], refs[-1]
    size = outs[0].shape[0]
    if fill:
        zero_ref[...] = jnp.zeros_like(zero_ref)

    def copies(do):
        for k, out in enumerate(outs):

            def step(j, k=k, out=out):
                slot = k * size + j
                row = source_ref[slot]

                @pl.when(row >= 0)
                def _():
                    at = 0
                    for n, x in enumerate(inputs):
                        width = x.shape[-1]
                        to = out.at[j] if count == 1 else out.at[j, :, pl.ds(at, width)]
                        do(pltpu.make_async_copy(x.at[row], to, sem.at[slot, n]))
                        at += width

                if fill:

                    @pl.when(row < 0)
                    def _():
                        do(pltpu.make_async_copy(zero_ref, out.at[j], sem.at[slot, 0]))

            each(0, size, step)

    copies(lambda copy: copy.start())
    copies(lambda copy: copy.wait())


def deal(source, arrays, parts, fill):
    length = arrays[0].shape[1]
    width = sum(x.shape[2] for x in arrays)
    slots = source.shape[0]
    return pl.pallas_call(
        functools.partial(deal_kernel, count=len(arrays), parts=parts, fill=fill),
        in_specs=[_SMEM] + [_VMEM] * len(arrays),
        out_specs=[_ANY] * parts,
        out_shape=[jax.ShapeDtypeStruct((slots // parts, length, width), arrays[0].dtype)] * parts,
        scratch_shapes=[
            pltpu.VMEM((length, width), jnp.bfloat16),
            pltpu.SemaphoreType.DMA((slots, len(arrays))),
        ],
        compiler_params=params(),
        name="deal",
    )(source, *arrays)


def shifted(block_for, count):
    return [
        lax.ppermute(block_for(k), "kv", [(i, (i + k) % count) for i in range(count)])
        for k in range(1, count)
    ]


def before(same):
    at = jnp.arange(same.shape[-1], dtype=jnp.int32)
    return jnp.sum((same & (at[:, None] > at[None, :])).astype(jnp.int32), axis=-1)


def look_up(keys, wanted, values):
    return jnp.sum(jnp.where(keys[None, :] == wanted[:, None], values[None, :] + 1, 0), axis=1)


def adapter_mask(slot_adapter, adapters):
    slots = slot_adapter.shape[0]
    lane_adapter = jnp.arange(adapters * ADAPTER_RANK, dtype=jnp.int32) // ADAPTER_RANK + 1
    return jnp.broadcast_to(
        (slot_adapter[:, None] == lane_adapter[None, :]).astype(jnp.bfloat16)[:, None, :],
        (slots, QUERY_LENGTH, lane_adapter.shape[0]),
    ).reshape(slots * QUERY_LENGTH, lane_adapter.shape[0])


def gather_caches(prompt_key_cache, prompt_value_cache):
    kv_count = lax.axis_size("kv")
    kv = lax.axis_index("kv")
    prompts, place_local = prompt_key_cache.shape[:2]
    head_columns = prompt_key_cache.shape[2] // kv_count
    both = jnp.stack([prompt_key_cache, prompt_value_cache]).reshape(
        2 * prompts * place_local, kv_count, head_columns
    )

    def cache_block(k):
        return lax.dynamic_index_in_dim(both, (kv + k) % kv_count, 1, keepdims=False)

    cache = jnp.stack([cache_block(0)] + shifted(cache_block, kv_count)).reshape(
        kv_count, 2, prompts * place_local, head_columns
    )
    key_at = jnp.arange(kv_count * prompts * place_local, dtype=jnp.int32)
    key_from = (kv - key_at // (prompts * place_local) + kv_count) % kv_count
    key_prompt = key_at // place_local % prompts
    key_place = key_from * place_local + key_at % place_local
    return (
        cache[:, 0].reshape(-1, head_columns),
        cache[:, 1].reshape(-1, head_columns),
        (key_prompt.reshape(1, -1), key_place.reshape(1, -1)),
    )


def per_token(x):
    return jnp.repeat(x, QUERY_LENGTH).reshape(-1, 1)


def as_rows(x):
    return x.reshape(x.shape[0] // QUERY_LENGTH, QUERY_LENGTH, x.shape[1])


def owner_forward(token_parts, mask, down_flat, up_flat):
    part = project(token_parts, mask, down_flat, jnp.bfloat16)
    sums = [part] + shifted(lambda k: part, lax.axis_size("kv"))
    return make_delta(sums, mask, up_flat, len(token_parts))


def owner_backward(gradient_parts, token_parts, mask, spread, up_flat):
    part = project(gradient_parts, mask, up_flat, jnp.bfloat16)
    sums = [part] + shifted(lambda k: part, lax.axis_size("kv"))
    return grad_down(sums, mask, token_parts), grad_up(spread, gradient_parts)


def one_hop(
    tokens,
    frozen_query,
    trained_keys,
    trained_values,
    frozen_output,
    prompt_key_cache,
    prompt_value_cache,
    adapter_down,
    adapter_up,
    row_adapter_index,
    row_forget_flag,
    row_prompt_index,
    row_prompt_length,
):
    tok_count = lax.axis_size(TOK)
    me = lax.axis_index(TOK)
    rows = tokens.shape[0] // QUERY_LENGTH
    width = tokens.shape[1]
    adapters = adapter_down.shape[0]
    slots = tok_count * CAP
    down_flat = adapter_down.reshape(adapters * ADAPTER_RANK, width)
    up_flat = adapter_up.reshape(adapters * ADAPTER_RANK, width)

    mine = lax.dynamic_slice_in_dim(row_adapter_index, me * rows, rows) // adapters
    target = mine * CAP + before(mine[:, None] == mine[None, :])
    source = (
        look_up(
            target, jnp.arange(slots, dtype=jnp.int32), jnp.arange(rows, dtype=jnp.int32)
        )
        - 1
    )

    def exchange(x):
        return lax.all_to_all(x, TOK, split_axis=0, concat_axis=0, tiled=True)

    token_parts = [
        exchange(deal(source, [as_rows(tokens)], 1, True)[0]).reshape(-1, width)
    ]

    hit = (row_adapter_index // adapters).reshape(tok_count, rows) == me
    rank = before(jnp.broadcast_to(hit[:, None, :], (tok_count, rows, rows)))
    local_adapter = (row_adapter_index % adapters).reshape(tok_count, rows)
    slot_adapter = jnp.sum(
        jnp.where(
            hit[:, None, :]
            & (rank[:, None, :] == jnp.arange(CAP, dtype=jnp.int32)[None, :, None]),
            local_adapter[:, None, :] + 1,
            0,
        ),
        axis=2,
    ).reshape(slots)
    mask = adapter_mask(slot_adapter, adapters)
    keys, values, per_key = gather_caches(prompt_key_cache, prompt_value_cache)

    def of_mine(x):
        return lax.dynamic_slice_in_dim(x, me * rows, rows)

    (delta,), spread = owner_forward(token_parts, mask, down_flat, up_flat)
    gradient = attend_home(
        target,
        as_rows(frozen_query),
        as_rows(frozen_output),
        as_rows(trained_keys),
        as_rows(trained_values),
        keys,
        values,
        (
            per_token(of_mine(row_prompt_length)),
            per_token(of_mine(row_prompt_index)),
            per_token(1.0 - 2.0 * of_mine(row_forget_flag).astype(jnp.float32)),
        ),
        per_key,
        exchange(delta.reshape(slots, QUERY_LENGTH, width)),
    )
    down, up = owner_backward(
        [exchange(gradient).reshape(-1, width)], token_parts, mask, spread, up_flat
    )
    return down.reshape(adapter_down.shape), up.reshape(adapter_up.shape)


def two_hops(
    tokens,
    frozen_query,
    trained_keys,
    trained_values,
    frozen_output,
    prompt_key_cache,
    prompt_value_cache,
    adapter_down,
    adapter_up,
    row_adapter_index,
    row_forget_flag,
    row_prompt_index,
    row_prompt_length,
    *,
    cap,
):
    planes = lax.axis_size("z")
    places = lax.axis_size("p")
    z = lax.axis_index("z")
    p = lax.axis_index("p")
    rows = tokens.shape[0] // QUERY_LENGTH
    width = tokens.shape[1]
    adapters = adapter_down.shape[0]
    seats = planes * CAP
    most = planes * cap
    down_flat = adapter_down.reshape(adapters * ADAPTER_RANK, width)
    up_flat = adapter_up.reshape(adapters * ADAPTER_RANK, width)
    row_at = jnp.arange(rows, dtype=jnp.int32)
    plane_at = jnp.arange(planes, dtype=jnp.int32)
    place_at = jnp.arange(places, dtype=jnp.int32)
    most_at = jnp.arange(most, dtype=jnp.int32)

    mine = lax.dynamic_slice_in_dim(row_adapter_index, (z * places + p) * rows, rows) // adapters
    my_plane = mine // places
    my_slot = my_plane * cap + before(my_plane[:, None] == my_plane[None, :])
    source = look_up(my_slot, most_at, row_at) - 1

    def dealt(*arrays):
        return deal(source, [as_rows(x) for x in arrays], 1, False)[0]

    def along_z(x):
        return lax.all_to_all(x, "z", split_axis=0, concat_axis=0, tiled=True)

    def partner(place, k):
        return (place // 2 + k // 2) % (places // 2) * 2 + (place + k) % 2

    def in_plane(parts, back=False):
        out = [parts[0]]
        for k in range(1, places):
            pairs = [(i, partner(i, k)) for i in range(places)]
            out.append(lax.ppermute(parts[k], "p", [(j, i) if back else (i, j) for i, j in pairs]))
        return out

    def part_of(place):
        return (place // 2 - p // 2 + places // 2) % (places // 2) * 2 + (place + p) % 2

    sent = dealt(tokens)
    moved_tokens = along_z(sent)

    def of_column(x):
        return lax.dynamic_index_in_dim(x.reshape(planes, places, rows), p, 1, keepdims=False)

    owner = of_column(row_adapter_index) // adapters
    hit = owner // places == z
    hop_slot = (plane_at * cap)[:, None] + before(
        jnp.broadcast_to(hit[:, None, :], (planes, rows, rows))
    )
    seat = (
        part_of(owner % places) * seats
        + plane_at[:, None] * CAP
        + before(owner[:, :, None] == owner[:, None, :])
    )
    hop_slot = jnp.where(hit, hop_slot, -1).reshape(-1)
    seat = jnp.where(hit, seat, -1).reshape(-1)
    flat_hit = hit.reshape(-1)
    packed = jnp.where(
        flat_hit, before(jnp.broadcast_to(flat_hit[None, :], (planes * rows,) * 2)), -1
    )
    total = jnp.sum(flat_hit.astype(jnp.int32)).reshape(1)
    seat_at = jnp.arange(places * seats, dtype=jnp.int32)
    seat_slot = look_up(seat, seat_at, hop_slot) - 1
    seat_row = look_up(seat, seat_at, packed) - 1
    slot_row = look_up(hop_slot, most_at, packed) - 1
    row_key = jnp.arange(most + (-most) % ROW_BLOCK, dtype=jnp.int32)

    def of_rows(x):
        return look_up(packed, row_key, of_column(x).reshape(-1)) - 1

    per_row = (
        per_token(of_rows(row_prompt_length)),
        per_token(of_rows(row_prompt_index)),
        per_token(1.0 - 2.0 * of_rows(row_forget_flag).astype(jnp.float32)),
    )

    def by_seat(x):
        homes = x.reshape(planes, places, rows)
        from_place = (p // 2 - place_at // 2 + places // 2) % (places // 2) * 2 + (
            p + place_at
        ) % 2
        pick = from_place[:, None] == place_at[None, :]
        return jnp.sum(
            jnp.where(pick[:, None, :, None], homes[None], 0), axis=2
        ).reshape(planes * places, rows)

    adapter_by_seat = by_seat(row_adapter_index)
    here = adapter_by_seat // adapters == z * places + p
    rank = before(jnp.broadcast_to(here[:, None, :], (planes * places, rows, rows)))
    slot_adapter = jnp.sum(
        jnp.where(
            here[:, None, :]
            & (rank[:, None, :] == jnp.arange(CAP, dtype=jnp.int32)[None, :, None]),
            (adapter_by_seat % adapters)[:, None, :] + 1,
            0,
        ),
        axis=2,
    ).reshape(places * seats)
    payload = dealt(frozen_query, frozen_output, trained_keys, trained_values)
    kv_width = trained_keys.shape[1]
    names = (
        ("query", 0),
        ("base", width),
        ("key", 2 * width),
        ("value", 2 * width + kv_width),
    )
    mask = adapter_mask(slot_adapter, adapters)
    caches = gather_caches(
        *lax.optimization_barrier((prompt_key_cache, prompt_value_cache, sent))[:2]
    )
    moved_tokens, payload, mask, caches, per_row, seat_slot, seat_row, slot_row, total = (
        lax.optimization_barrier(
            (
                moved_tokens,
                payload,
                mask,
                caches,
                per_row,
                seat_slot,
                seat_row,
                slot_row,
                total,
            )
        )
    )
    keys, values, per_key = caches

    payload = along_z(payload)
    token_parts = [
        x.reshape(-1, width) for x in in_plane(deal(seat_slot, [moved_tokens], places, True))
    ]

    delta, spread = owner_forward(token_parts, mask, down_flat, up_flat)
    delta = in_plane([x.reshape(seats, QUERY_LENGTH, width) for x in delta], back=True)
    gradient = attend_middle(
        slot_row, seat_row, total, (payload,), (names,), keys, values, per_row, per_key, delta
    )
    gradient = [x.reshape(-1, width) for x in in_plane(gradient)]
    down, up = owner_backward(gradient, token_parts, mask, spread, up_flat)
    return down.reshape(adapter_down.shape), up.reshape(adapter_up.shape)


def per_device(*arrays):
    row_adapter_index = arrays[9]
    adapters = arrays[7].shape[0]
    planes = lax.axis_size("z")
    places = lax.axis_size("p")
    plane = (row_adapter_index // (adapters * places)).reshape(planes * places, -1)
    load = jnp.sum(
        (plane[:, None, :] == jnp.arange(planes, dtype=jnp.int32)[None, :, None]).astype(
            jnp.int32
        ),
        axis=2,
    )
    return lax.cond(
        jnp.max(load) > HOP_CAP,
        one_hop,
        functools.partial(two_hops, cap=HOP_CAP),
        *arrays,
    )


def solution(mesh):
    tok_count, kv_count = mesh.devices.shape
    grid = Mesh(mesh.devices.reshape(PLANES, tok_count // PLANES, kv_count), ("z", "p", "kv"))
    return jax.shard_map(
        per_device,
        mesh=grid,
        in_specs=(
            P(TOK, "kv"),
            P(TOK, "kv"),
            P(TOK, "kv"),
            P(TOK, "kv"),
            P(TOK, "kv"),
            P(None, "kv", None),
            P(None, "kv", None),
            P(TOK, None, "kv"),
            P(TOK, None, "kv"),
            P(),
            P(),
            P(),
            P(),
        ),
        out_specs=(P(TOK, None, "kv"), P(TOK, None, "kv")),
        check_vma=False,
    )
```

```python
import functools
import math

import jax
import jax.numpy as jnp
from jax import lax
from jax.experimental import pallas as pl
from jax.experimental.pallas import tpu as pltpu
from jax.sharding import Mesh
from jax.sharding import PartitionSpec as P

QUERY_HEADS = 64
KEY_HEADS = 8
HEAD_WIDTH = 128
ADAPTER_RANK = 64
QUERY_LENGTH = 8
ADAPTER_SCALE = 0.5
CAP = 2
PLANES = 8
HOP_CAP = 10
TOK = ("z", "p")
ROW_BLOCK = 16
LOG2_E = math.log2(math.e)
VMEM_LIMIT = 56 * 1024 * 1024

_VMEM = pl.BlockSpec(memory_space=pltpu.VMEM)
_SMEM = pl.BlockSpec(memory_space=pltpu.SMEM)
_ANY = pl.BlockSpec(memory_space=pl.ANY)


def params():
    return pltpu.CompilerParams(vmem_limit_bytes=VMEM_LIMIT)


def fold(products, mask):
    kept = products * mask.astype(jnp.float32)
    half = kept[:, :128] + kept[:, 128:]
    return half + pltpu.roll(half, 64, 1)


def low_half(shape):
    return lax.broadcasted_iota(jnp.int32, shape, 1) < 64


def all_rows(refs):
    parts = [r[...] for r in refs]
    return parts[0] if len(parts) == 1 else jnp.concatenate(parts, axis=0)


def project_kernel(weight_ref, mask_ref, *refs):
    x_refs, out_ref, total_ref = refs[:-2], refs[-2], refs[-1]
    step = pl.program_id(0)
    product = lax.dot_general(
        all_rows(x_refs),
        weight_ref[...],
        (((1,), (1,)), ((), ())),
        preferred_element_type=jnp.float32,
    )

    @pl.when(step == 0)
    def _():
        total_ref[...] = product

    @pl.when(step > 0)
    def _():
        total_ref[...] += product

    @pl.when(step == pl.num_programs(0) - 1)
    def _():
        half = out_ref.shape[0]
        both = jnp.where(
            low_half(out_ref.shape),
            fold(total_ref[:half], mask_ref[:half]),
            fold(total_ref[half:], mask_ref[half:]),
        )
        out_ref[...] = both.astype(out_ref.dtype)


def column_blocks(parts, block):
    return [pl.BlockSpec((x.shape[0], block), lambda i: (0, i)) for x in parts]


def project(parts, mask, weight, out_type):
    tokens = sum(x.shape[0] for x in parts)
    ranks, width = weight.shape
    block = 1024
    return pl.pallas_call(
        project_kernel,
        grid=(width // block,),
        in_specs=[
            pl.BlockSpec((ranks, block), lambda i: (0, i)),
            pl.BlockSpec((tokens, ranks), lambda i: (0, 0)),
        ]
        + column_blocks(parts, block),
        out_specs=pl.BlockSpec((tokens // 2, 128), lambda i: (0, 0)),
        out_shape=jax.ShapeDtypeStruct((tokens // 2, 128), out_type),
        scratch_shapes=[pltpu.VMEM((tokens, ranks), jnp.float32)],
        compiler_params=params(),
        name="project",
    )(weight, mask, *parts)


def spread_of(packed, mask, is_low):
    low = low_half(packed.shape)
    turned = pltpu.roll(packed, 64, 1)
    twice = jnp.where(low, packed, turned) if is_low else jnp.where(low, turned, packed)
    return (jnp.concatenate([twice, twice], axis=1) * mask.astype(jnp.float32)).astype(
        jnp.bfloat16
    )


def delta_kernel(p0, p1, p2, p3, mask_ref, weight_ref, *refs):
    out_refs, spread_ref = refs[:-1], refs[-1]
    half = p0.shape[0]

    @pl.when(pl.program_id(0) == 0)
    def _():
        total = (p0[...].astype(jnp.float32) + p1[...].astype(jnp.float32)) + (
            p2[...].astype(jnp.float32) + p3[...].astype(jnp.float32)
        )
        low_rank = total.astype(jnp.bfloat16).astype(jnp.float32)
        spread_ref[:half] = spread_of(low_rank, mask_ref[:half], True)
        spread_ref[half:] = spread_of(low_rank, mask_ref[half:], False)

    delta = (
        ADAPTER_SCALE
        * jnp.dot(spread_ref[...], weight_ref[...], preferred_element_type=jnp.float32)
    ).astype(jnp.bfloat16)
    at = 0
    for out_ref in out_refs:
        out_ref[...] = delta[at : at + out_ref.shape[0]]
        at += out_ref.shape[0]


def make_delta(sums, mask, weight, count):
    half = sums[0].shape[0]
    tokens = 2 * half
    ranks, width = weight.shape
    block = 1024
    outs = [jax.ShapeDtypeStruct((tokens // count, width), jnp.bfloat16)] * count
    *parts, spread = pl.pallas_call(
        delta_kernel,
        grid=(width // block,),
        in_specs=[pl.BlockSpec((half, 128), lambda i: (0, 0))] * 4
        + [
            pl.BlockSpec((tokens, ranks), lambda i: (0, 0)),
            pl.BlockSpec((ranks, block), lambda i: (0, i)),
        ],
        out_specs=column_blocks(outs, block)
        + [pl.BlockSpec((tokens, ranks), lambda i: (0, 0))],
        out_shape=outs + [jax.ShapeDtypeStruct((tokens, ranks), jnp.bfloat16)],
        compiler_params=params(),
        name="make_delta",
    )(*sums, mask, weight)
    return parts, spread


def grad_up_kernel(spread_ref, *refs):
    out_ref = refs[-1]
    out_ref[...] = (
        ADAPTER_SCALE
        * lax.dot_general(
            spread_ref[...],
            all_rows(refs[:-1]),
            (((0,), (0,)), ((), ())),
            preferred_element_type=jnp.float32,
        )
    ).astype(out_ref.dtype)


def grad_up(spread, parts):
    tokens, ranks = spread.shape
    width = parts[0].shape[1]
    block = 1024
    return pl.pallas_call(
        grad_up_kernel,
        grid=(width // block,),
        in_specs=[pl.BlockSpec((tokens, ranks), lambda i: (0, 0))] + column_blocks(parts, block),
        out_specs=pl.BlockSpec((ranks, block), lambda i: (0, i)),
        out_shape=jax.ShapeDtypeStruct((ranks, width), jnp.bfloat16),
        compiler_params=params(),
        name="grad_up",
    )(spread, *parts)


def grad_down_kernel(p0, p1, p2, p3, mask_ref, *refs):
    x_refs, out_ref, spread_ref = refs[:-2], refs[-2], refs[-1]
    half = p0.shape[0]

    @pl.when(pl.program_id(0) == 0)
    def _():
        total = (p0[...].astype(jnp.float32) + p1[...].astype(jnp.float32)) + (
            p2[...].astype(jnp.float32) + p3[...].astype(jnp.float32)
        )
        low_grad = (ADAPTER_SCALE * total).astype(jnp.bfloat16).astype(jnp.float32)
        spread_ref[:half] = spread_of(low_grad, mask_ref[:half], True)
        spread_ref[half:] = spread_of(low_grad, mask_ref[half:], False)

    out_ref[...] = lax.dot_general(
        spread_ref[...],
        all_rows(x_refs),
        (((0,), (0,)), ((), ())),
        preferred_element_type=jnp.float32,
    ).astype(out_ref.dtype)


def grad_down(sums, mask, parts):
    half = sums[0].shape[0]
    tokens, ranks = mask.shape
    width = parts[0].shape[1]
    block = 1024
    return pl.pallas_call(
        grad_down_kernel,
        grid=(width // block,),
        in_specs=[pl.BlockSpec((half, 128), lambda i: (0, 0))] * 4
        + [pl.BlockSpec((tokens, ranks), lambda i: (0, 0))]
        + column_blocks(parts, block),
        out_specs=pl.BlockSpec((ranks, block), lambda i: (0, i)),
        out_shape=jax.ShapeDtypeStruct((ranks, width), jnp.bfloat16),
        scratch_shapes=[pltpu.VMEM((tokens, ranks), jnp.bfloat16)],
        compiler_params=params(),
        name="grad_down",
    )(*sums, mask, *parts)


def heads_first(x, head_group):
    return jnp.concatenate(
        [x[:, h * HEAD_WIDTH : (h + 1) * HEAD_WIDTH] for h in range(head_group)], axis=0
    )


def by_rows(a, b):
    return lax.dot_general(a, b, (((1,), (1,)), ((), ())), preferred_element_type=jnp.float32)


def times(a, b):
    return jnp.dot(a, b, preferred_element_type=jnp.float32)


def attend_group(query, base, own_keys, own_values, keys, values, shared_seen, own_seen, weight):
    tokens = own_keys.shape[0]
    head_group = query.shape[1] // HEAD_WIDTH
    inv_root = 1.0 / math.sqrt(HEAD_WIDTH)
    query = heads_first(query, head_group).astype(jnp.bfloat16)
    base = heads_first(base, head_group)

    def group(x):
        return x.reshape(head_group, tokens, x.shape[-1])

    def flat(x):
        return x.reshape(head_group * tokens, x.shape[-1])

    shared = jnp.where(shared_seen[None], group(by_rows(query, keys)), -1e30)
    own = jnp.where(own_seen[None], group(by_rows(query, own_keys)), -1e30)
    top = jnp.maximum(
        jnp.max(shared, axis=-1, keepdims=True), jnp.max(own, axis=-1, keepdims=True)
    )
    shared = flat(jnp.exp2((shared - top) * (inv_root * LOG2_E)))
    own = flat(jnp.exp2((own - top) * (inv_root * LOG2_E)))
    total = jnp.sum(shared, axis=-1, keepdims=True) + jnp.sum(own, axis=-1, keepdims=True)
    scale = 1.0 / total
    attn_out = scale * (
        times(shared.astype(jnp.bfloat16), values) + times(own.astype(jnp.bfloat16), own_values)
    )
    grad_out = flat(group(attn_out - base) * weight[None]).astype(jnp.bfloat16)
    inner = jnp.sum(grad_out.astype(jnp.float32) * attn_out, axis=-1, keepdims=True)
    shared_gs = (shared * (by_rows(grad_out, values) - inner)).astype(jnp.bfloat16)
    own_gs = (own * (by_rows(grad_out, own_values) - inner)).astype(jnp.bfloat16)
    return (scale * inv_root) * (times(shared_gs, keys) + times(own_gs, own_keys))


def attend_block(b, load, delta_ref, grad_ref, key_ref, value_ref, vectors):
    row_len_ref, row_prompt_ref, row_weight_ref, key_prompt_ref, key_place_ref = vectors
    length = QUERY_LENGTH
    head_group = QUERY_HEADS // KEY_HEADS
    group_width = head_group * HEAD_WIDTH
    block_tokens = ROW_BLOCK * length
    block = pl.ds(b * ROW_BLOCK, ROW_BLOCK)
    tokens = pl.ds(b * block_tokens, block_tokens)
    shared_seen = (row_prompt_ref[tokens, :] == key_prompt_ref[...]) & (
        key_place_ref[...] < row_len_ref[tokens, :]
    )
    own_shape = (block_tokens, block_tokens)
    q_at = lax.broadcasted_iota(jnp.int32, own_shape, 0)
    k_at = lax.broadcasted_iota(jnp.int32, own_shape, 1)
    own_seen = (q_at // length == k_at // length) & (k_at <= q_at)
    weight = row_weight_ref[tokens, :]

    def two_d(x):
        return x.astype(jnp.float32).reshape(block_tokens, x.shape[-1])

    for g in range(key_ref.shape[1] // HEAD_WIDTH):
        columns = slice(g * group_width, (g + 1) * group_width)
        keys_at = slice(g * HEAD_WIDTH, (g + 1) * HEAD_WIDTH)
        gradient = attend_group(
            two_d(load("query", block, columns)) + two_d(delta_ref[block, :, columns]),
            two_d(load("base", block, columns)),
            two_d(load("key", block, keys_at)).astype(jnp.bfloat16),
            two_d(load("value", block, keys_at)).astype(jnp.bfloat16),
            key_ref[:, keys_at],
            value_ref[:, keys_at],
            shared_seen,
            own_seen,
            weight,
        )
        for h in range(head_group):
            piece = gradient[h * block_tokens : (h + 1) * block_tokens]
            at = g * group_width + h * HEAD_WIDTH
            grad_ref[block, :, at : at + HEAD_WIDTH] = piece.reshape(
                ROW_BLOCK, length, HEAD_WIDTH
            ).astype(jnp.bfloat16)


def attend_home_kernel(
    target_ref,
    query_ref,
    base_ref,
    own_key_ref,
    own_value_ref,
    key_ref,
    value_ref,
    row_len_ref,
    row_prompt_ref,
    row_weight_ref,
    key_prompt_ref,
    key_place_ref,
    delta_hbm,
    out_hbm,
    delta_ref,
    grad_ref,
    in_sem,
    out_sem,
):
    rows = query_ref.shape[0]
    refs = {"query": query_ref, "base": base_ref, "key": own_key_ref, "value": own_value_ref}
    vectors = (row_len_ref, row_prompt_ref, row_weight_ref, key_prompt_ref, key_place_ref)

    def fetch(r):
        return pltpu.make_async_copy(delta_hbm.at[target_ref[r]], delta_ref.at[r], in_sem.at[r])

    def send(r):
        return pltpu.make_async_copy(grad_ref.at[r], out_hbm.at[target_ref[r]], out_sem.at[r])

    for r in range(rows):
        fetch(r).start()
    for r in range(rows):
        fetch(r).wait()

    def load(name, block, columns):
        return refs[name][block, :, columns]

    def one_block(b, carry):
        attend_block(b, load, delta_ref, grad_ref, key_ref, value_ref, vectors)
        return carry

    lax.fori_loop(0, rows // ROW_BLOCK, one_block, 0)
    for r in range(rows):
        send(r).start()
    for r in range(rows):
        send(r).wait()


def attend_home(target, query, base, own_key, own_value, keys, values, per_token, per_key, delta):
    rows, length, width = query.shape
    return pl.pallas_call(
        attend_home_kernel,
        in_specs=[_SMEM] + [_VMEM] * 11 + [_ANY],
        out_specs=_ANY,
        out_shape=jax.ShapeDtypeStruct(delta.shape, delta.dtype),
        scratch_shapes=[
            pltpu.VMEM((rows, length, width), jnp.bfloat16),
            pltpu.VMEM((rows, length, width), jnp.bfloat16),
            pltpu.SemaphoreType.DMA((rows,)),
            pltpu.SemaphoreType.DMA((rows,)),
        ],
        input_output_aliases={12: 0},
        compiler_params=params(),
        name="attend_home",
    )(
        target,
        query,
        base,
        own_key,
        own_value,
        keys,
        values,
        *per_token,
        *per_key,
        delta,
    )


def each(first, last, do):
    def step(i, carry):
        do(i)
        return carry

    lax.fori_loop(first, last, step, 0)


def attend_middle_kernel(*refs, count, names):
    place_ref, seated_ref, total_ref = refs[:3]
    refs = refs[3:]
    payload_hbm, refs = refs[: len(names)], refs[len(names) :]
    key_ref, value_ref = refs[:2]
    vectors, refs = refs[2:7], refs[7:]
    delta_hbm, out_hbm, refs = refs[:count], refs[count : 2 * count], refs[2 * count :]
    payload_refs, refs = refs[: len(names)], refs[len(names) :]
    delta_ref, grad_ref, in_sem, delta_sem, out_sem = refs
    slots = payload_hbm[0].shape[0]
    seats = delta_hbm[0].shape[0]
    total = total_ref[0]
    blocks = (total + ROW_BLOCK - 1) // ROW_BLOCK
    where = {name: (n, at) for n, held in enumerate(names) for name, at in held}

    def fetch(do):
        def step(h):
            row = place_ref[h]

            @pl.when(row >= 0)
            def _():
                for n in range(len(names)):
                    do(
                        pltpu.make_async_copy(
                            payload_hbm[n].at[h], payload_refs[n].at[row], in_sem.at[h, n]
                        )
                    )

        each(0, slots, step)

    def seat(copy, do):
        for k in range(count):

            def step(j, k=k):
                row = seated_ref[k * seats + j]

                @pl.when(row >= 0)
                def _():
                    do(copy(k, j, row))

            each(0, seats, step)

    def fetch_delta(k, j, row):
        return pltpu.make_async_copy(
            delta_hbm[k].at[j], delta_ref.at[row], delta_sem.at[k * seats + j]
        )

    def send(k, j, row):
        return pltpu.make_async_copy(
            grad_ref.at[row], out_hbm[k].at[j], out_sem.at[k * seats + j]
        )

    def start(copy):
        copy.start()

    def wait(copy):
        copy.wait()

    fetch(start)
    seat(fetch_delta, start)

    def clear(i):
        for ref in payload_refs + (delta_ref,):
            ref[i] = jnp.zeros_like(ref[i])

    each(total, blocks * ROW_BLOCK, clear)
    fetch(wait)
    seat(fetch_delta, wait)

    def load(name, block, columns):
        n, at = where[name]
        return payload_refs[n][block, :, at + columns.start : at + columns.stop]

    each(
        0,
        blocks,
        lambda b: attend_block(b, load, delta_ref, grad_ref, key_ref, value_ref, vectors),
    )
    seat(send, start)
    seat(send, wait)


def attend_middle(place, seated, total, payload, names, keys, values, per_row, per_key, delta):
    slots, length = payload[0].shape[:2]
    seats, _, width = delta[0].shape
    count = len(delta)
    rows = slots + (-slots) % ROW_BLOCK
    first_delta = 3 + len(payload) + 7
    return pl.pallas_call(
        functools.partial(attend_middle_kernel, count=count, names=names),
        in_specs=[_SMEM] * 3 + [_ANY] * len(payload) + [_VMEM] * 7 + [_ANY] * count,
        out_specs=[_ANY] * count,
        out_shape=[jax.ShapeDtypeStruct(x.shape, x.dtype) for x in delta],
        scratch_shapes=[pltpu.VMEM((rows, length, x.shape[2]), x.dtype) for x in payload]
        + [
            pltpu.VMEM((rows, length, width), jnp.bfloat16),
            pltpu.VMEM((rows, length, width), jnp.bfloat16),
            pltpu.SemaphoreType.DMA((slots, len(payload))),
            pltpu.SemaphoreType.DMA((count * seats,)),
            pltpu.SemaphoreType.DMA((count * seats,)),
        ],
        input_output_aliases={first_delta + k: k for k in range(count)},
        compiler_params=params(),
        name="attend_middle",
    )(place, seated, total, *payload, keys, values, *per_row, *per_key, *delta)


def deal_kernel(source_ref, *refs, count, parts, fill):
    inputs, outs, zero_ref, sem = refs[:count], refs[count : count + parts], refs[-2], refs[-1]
    size = outs[0].shape[0]
    if fill:
        zero_ref[...] = jnp.zeros_like(zero_ref)

    def copies(do):
        for k, out in enumerate(outs):

            def step(j, k=k, out=out):
                slot = k * size + j
                row = source_ref[slot]

                @pl.when(row >= 0)
                def _():
                    at = 0
                    for n, x in enumerate(inputs):
                        width = x.shape[-1]
                        to = out.at[j] if count == 1 else out.at[j, :, pl.ds(at, width)]
                        do(pltpu.make_async_copy(x.at[row], to, sem.at[slot, n]))
                        at += width

                if fill:

                    @pl.when(row < 0)
                    def _():
                        do(pltpu.make_async_copy(zero_ref, out.at[j], sem.at[slot, 0]))

            each(0, size, step)

    copies(lambda copy: copy.start())
    copies(lambda copy: copy.wait())


def deal(source, arrays, parts, fill):
    length = arrays[0].shape[1]
    width = sum(x.shape[2] for x in arrays)
    slots = source.shape[0]
    return pl.pallas_call(
        functools.partial(deal_kernel, count=len(arrays), parts=parts, fill=fill),
        in_specs=[_SMEM] + [_VMEM] * len(arrays),
        out_specs=[_ANY] * parts,
        out_shape=[jax.ShapeDtypeStruct((slots // parts, length, width), arrays[0].dtype)] * parts,
        scratch_shapes=[
            pltpu.VMEM((length, width), jnp.bfloat16),
            pltpu.SemaphoreType.DMA((slots, len(arrays))),
        ],
        compiler_params=params(),
        name="deal",
    )(source, *arrays)


def shifted(block_for, count):
    return [
        lax.ppermute(block_for(k), "kv", [(i, (i + k) % count) for i in range(count)])
        for k in range(1, count)
    ]


def before(same):
    at = jnp.arange(same.shape[-1], dtype=jnp.int32)
    return jnp.sum((same & (at[:, None] > at[None, :])).astype(jnp.int32), axis=-1)


def look_up(keys, wanted, values):
    return jnp.sum(jnp.where(keys[None, :] == wanted[:, None], values[None, :] + 1, 0), axis=1)


def adapter_mask(slot_adapter, adapters):
    slots = slot_adapter.shape[0]
    lane_adapter = jnp.arange(adapters * ADAPTER_RANK, dtype=jnp.int32) // ADAPTER_RANK + 1
    return jnp.broadcast_to(
        (slot_adapter[:, None] == lane_adapter[None, :]).astype(jnp.bfloat16)[:, None, :],
        (slots, QUERY_LENGTH, lane_adapter.shape[0]),
    ).reshape(slots * QUERY_LENGTH, lane_adapter.shape[0])


def gather_caches(prompt_key_cache, prompt_value_cache):
    kv_count = lax.axis_size("kv")
    kv = lax.axis_index("kv")
    prompts, place_local = prompt_key_cache.shape[:2]
    head_columns = prompt_key_cache.shape[2] // kv_count
    both = jnp.stack([prompt_key_cache, prompt_value_cache]).reshape(
        2 * prompts * place_local, kv_count, head_columns
    )

    def cache_block(k):
        return lax.dynamic_index_in_dim(both, (kv + k) % kv_count, 1, keepdims=False)

    cache = jnp.stack([cache_block(0)] + shifted(cache_block, kv_count)).reshape(
        kv_count, 2, prompts * place_local, head_columns
    )
    key_at = jnp.arange(kv_count * prompts * place_local, dtype=jnp.int32)
    key_from = (kv - key_at // (prompts * place_local) + kv_count) % kv_count
    key_prompt = key_at // place_local % prompts
    key_place = key_from * place_local + key_at % place_local
    return (
        cache[:, 0].reshape(-1, head_columns),
        cache[:, 1].reshape(-1, head_columns),
        (key_prompt.reshape(1, -1), key_place.reshape(1, -1)),
    )


def per_token(x):
    return jnp.repeat(x, QUERY_LENGTH).reshape(-1, 1)


def as_rows(x):
    return x.reshape(x.shape[0] // QUERY_LENGTH, QUERY_LENGTH, x.shape[1])


def owner_forward(token_parts, mask, down_flat, up_flat):
    part = project(token_parts, mask, down_flat, jnp.bfloat16)
    sums = [part] + shifted(lambda k: part, lax.axis_size("kv"))
    return make_delta(sums, mask, up_flat, len(token_parts))


def owner_backward(gradient_parts, token_parts, mask, spread, up_flat):
    part = project(gradient_parts, mask, up_flat, jnp.bfloat16)
    sums = [part] + shifted(lambda k: part, lax.axis_size("kv"))
    return grad_down(sums, mask, token_parts), grad_up(spread, gradient_parts)


def one_hop(
    tokens,
    frozen_query,
    trained_keys,
    trained_values,
    frozen_output,
    prompt_key_cache,
    prompt_value_cache,
    adapter_down,
    adapter_up,
    row_adapter_index,
    row_forget_flag,
    row_prompt_index,
    row_prompt_length,
):
    tok_count = lax.axis_size(TOK)
    me = lax.axis_index(TOK)
    rows = tokens.shape[0] // QUERY_LENGTH
    width = tokens.shape[1]
    adapters = adapter_down.shape[0]
    slots = tok_count * CAP
    down_flat = adapter_down.reshape(adapters * ADAPTER_RANK, width)
    up_flat = adapter_up.reshape(adapters * ADAPTER_RANK, width)

    mine = lax.dynamic_slice_in_dim(row_adapter_index, me * rows, rows) // adapters
    target = mine * CAP + before(mine[:, None] == mine[None, :])
    source = (
        look_up(
            target, jnp.arange(slots, dtype=jnp.int32), jnp.arange(rows, dtype=jnp.int32)
        )
        - 1
    )

    def exchange(x):
        return lax.all_to_all(x, TOK, split_axis=0, concat_axis=0, tiled=True)

    token_parts = [
        exchange(deal(source, [as_rows(tokens)], 1, True)[0]).reshape(-1, width)
    ]

    hit = (row_adapter_index // adapters).reshape(tok_count, rows) == me
    rank = before(jnp.broadcast_to(hit[:, None, :], (tok_count, rows, rows)))
    local_adapter = (row_adapter_index % adapters).reshape(tok_count, rows)
    slot_adapter = jnp.sum(
        jnp.where(
            hit[:, None, :]
            & (rank[:, None, :] == jnp.arange(CAP, dtype=jnp.int32)[None, :, None]),
            local_adapter[:, None, :] + 1,
            0,
        ),
        axis=2,
    ).reshape(slots)
    mask = adapter_mask(slot_adapter, adapters)
    keys, values, per_key = gather_caches(prompt_key_cache, prompt_value_cache)

    def of_mine(x):
        return lax.dynamic_slice_in_dim(x, me * rows, rows)

    (delta,), spread = owner_forward(token_parts, mask, down_flat, up_flat)
    gradient = attend_home(
        target,
        as_rows(frozen_query),
        as_rows(frozen_output),
        as_rows(trained_keys),
        as_rows(trained_values),
        keys,
        values,
        (
            per_token(of_mine(row_prompt_length)),
            per_token(of_mine(row_prompt_index)),
            per_token(1.0 - 2.0 * of_mine(row_forget_flag).astype(jnp.float32)),
        ),
        per_key,
        exchange(delta.reshape(slots, QUERY_LENGTH, width)),
    )
    down, up = owner_backward(
        [exchange(gradient).reshape(-1, width)], token_parts, mask, spread, up_flat
    )
    return down.reshape(adapter_down.shape), up.reshape(adapter_up.shape)


def two_hops(
    tokens,
    frozen_query,
    trained_keys,
    trained_values,
    frozen_output,
    prompt_key_cache,
    prompt_value_cache,
    adapter_down,
    adapter_up,
    row_adapter_index,
    row_forget_flag,
    row_prompt_index,
    row_prompt_length,
    *,
    cap,
):
    planes = lax.axis_size("z")
    places = lax.axis_size("p")
    z = lax.axis_index("z")
    p = lax.axis_index("p")
    rows = tokens.shape[0] // QUERY_LENGTH
    width = tokens.shape[1]
    adapters = adapter_down.shape[0]
    seats = planes * CAP
    most = planes * cap
    down_flat = adapter_down.reshape(adapters * ADAPTER_RANK, width)
    up_flat = adapter_up.reshape(adapters * ADAPTER_RANK, width)
    row_at = jnp.arange(rows, dtype=jnp.int32)
    plane_at = jnp.arange(planes, dtype=jnp.int32)
    place_at = jnp.arange(places, dtype=jnp.int32)
    most_at = jnp.arange(most, dtype=jnp.int32)

    mine = lax.dynamic_slice_in_dim(row_adapter_index, (z * places + p) * rows, rows) // adapters
    my_plane = mine // places
    my_slot = my_plane * cap + before(my_plane[:, None] == my_plane[None, :])
    source = look_up(my_slot, most_at, row_at) - 1

    def dealt(*arrays):
        return deal(source, [as_rows(x) for x in arrays], 1, False)[0]

    def along_z(x):
        return lax.all_to_all(x, "z", split_axis=0, concat_axis=0, tiled=True)

    assert places == 8

    def steps(n):
        return n % 2 * 2 + n // 2

    def partner(place, k):
        return (place // 2 + steps(k // 2)) % 4 * 2 + (place + k) % 2

    def in_plane(parts, first=0, back=False):
        out = []
        for k, part in enumerate(parts, first):
            pairs = [(i, partner(i, k)) for i in range(places)]
            if k:
                part = lax.ppermute(part, "p", [(j, i) if back else (i, j) for i, j in pairs])
            out.append(part)
        return out

    def part_of(place):
        return steps((place // 2 - p // 2 + 4) % 4) * 2 + (place + p) % 2

    sent = dealt(tokens)
    moved_tokens = along_z(sent)

    def of_column(x):
        return lax.dynamic_index_in_dim(x.reshape(planes, places, rows), p, 1, keepdims=False)

    owner = of_column(row_adapter_index) // adapters
    hit = owner // places == z
    hop_slot = (plane_at * cap)[:, None] + before(
        jnp.broadcast_to(hit[:, None, :], (planes, rows, rows))
    )
    seat = (
        part_of(owner % places) * seats
        + plane_at[:, None] * CAP
        + before(owner[:, :, None] == owner[:, None, :])
    )
    hop_slot = jnp.where(hit, hop_slot, -1).reshape(-1)
    seat = jnp.where(hit, seat, -1).reshape(-1)
    seat_slot = look_up(seat, jnp.arange(places * seats, dtype=jnp.int32), hop_slot) - 1
    cut = places // 2
    row_key = jnp.arange(most + (-most) % ROW_BLOCK, dtype=jnp.int32)

    def attend_tables(first, last):
        low, high = first * seats, last * seats
        here = (seat >= low) & (seat < high)
        packed = jnp.where(
            here, before(jnp.broadcast_to(here[None, :], (planes * rows,) * 2)), -1
        )

        def of_rows(x):
            return look_up(packed, row_key, of_column(x).reshape(-1)) - 1

        return (
            look_up(jnp.where(here, hop_slot, -1), most_at, packed) - 1,
            look_up(seat, jnp.arange(low, high, dtype=jnp.int32), packed) - 1,
            jnp.sum(here.astype(jnp.int32)).reshape(1),
            (
                per_token(of_rows(row_prompt_length)),
                per_token(of_rows(row_prompt_index)),
                per_token(1.0 - 2.0 * of_rows(row_forget_flag).astype(jnp.float32)),
            ),
        )

    tables = (attend_tables(0, cut), attend_tables(cut, places))

    def by_seat(x):
        homes = x.reshape(planes, places, rows)
        from_place = (p // 2 - steps(place_at // 2) + 4) % 4 * 2 + (p + place_at) % 2
        pick = from_place[:, None] == place_at[None, :]
        return jnp.sum(
            jnp.where(pick[:, None, :, None], homes[None], 0), axis=2
        ).reshape(planes * places, rows)

    adapter_by_seat = by_seat(row_adapter_index)
    here = adapter_by_seat // adapters == z * places + p
    rank = before(jnp.broadcast_to(here[:, None, :], (planes * places, rows, rows)))
    slot_adapter = jnp.sum(
        jnp.where(
            here[:, None, :]
            & (rank[:, None, :] == jnp.arange(CAP, dtype=jnp.int32)[None, :, None]),
            (adapter_by_seat % adapters)[:, None, :] + 1,
            0,
        ),
        axis=2,
    ).reshape(places * seats)
    payload = dealt(frozen_query, frozen_output, trained_keys, trained_values)
    kv_width = trained_keys.shape[1]
    names = (
        ("query", 0),
        ("base", width),
        ("key", 2 * width),
        ("value", 2 * width + kv_width),
    )
    mask = adapter_mask(slot_adapter, adapters)
    caches = gather_caches(
        *lax.optimization_barrier((prompt_key_cache, prompt_value_cache, sent))[:2]
    )
    moved_tokens, payload, mask, caches, seat_slot, tables = lax.optimization_barrier(
        (moved_tokens, payload, mask, caches, seat_slot, tables)
    )
    keys, values, per_key = caches

    payload = along_z(payload)
    token_parts = [
        x.reshape(-1, width) for x in in_plane(deal(seat_slot, [moved_tokens], places, True))
    ]

    delta, spread = owner_forward(token_parts, mask, down_flat, up_flat)
    delta = in_plane([x.reshape(seats, QUERY_LENGTH, width) for x in delta], back=True)

    def attend(part_delta, part_tables):
        slot_row, seat_row, total, per_row = part_tables
        return attend_middle(
            slot_row,
            seat_row,
            total,
            (payload,),
            (names,),
            keys,
            values,
            per_row,
            per_key,
            part_delta,
        )

    early = attend(delta[:cut], tables[0])
    late_delta, early = lax.optimization_barrier((delta[cut:], early))
    gradient = in_plane(early) + in_plane(attend(late_delta, tables[1]), first=cut)
    gradient = [x.reshape(-1, width) for x in gradient]
    down, up = owner_backward(gradient, token_parts, mask, spread, up_flat)
    return down.reshape(adapter_down.shape), up.reshape(adapter_up.shape)


def per_device(*arrays):
    row_adapter_index = arrays[9]
    adapters = arrays[7].shape[0]
    planes = lax.axis_size("z")
    places = lax.axis_size("p")
    plane = (row_adapter_index // (adapters * places)).reshape(planes * places, -1)
    load = jnp.sum(
        (plane[:, None, :] == jnp.arange(planes, dtype=jnp.int32)[None, :, None]).astype(
            jnp.int32
        ),
        axis=2,
    )
    return lax.cond(
        jnp.max(load) > HOP_CAP,
        one_hop,
        functools.partial(two_hops, cap=HOP_CAP),
        *arrays,
    )


def solution(mesh):
    tok_count, kv_count = mesh.devices.shape
    grid = Mesh(mesh.devices.reshape(PLANES, tok_count // PLANES, kv_count), ("z", "p", "kv"))
    return jax.shard_map(
        per_device,
        mesh=grid,
        in_specs=(
            P(TOK, "kv"),
            P(TOK, "kv"),
            P(TOK, "kv"),
            P(TOK, "kv"),
            P(TOK, "kv"),
            P(None, "kv", None),
            P(None, "kv", None),
            P(TOK, None, "kv"),
            P(TOK, None, "kv"),
            P(),
            P(),
            P(),
            P(),
        ),
        out_specs=(P(TOK, None, "kv"), P(TOK, None, "kv")),
        check_vma=False,
    )
```

```python
import functools
import math

import jax
import jax.numpy as jnp
from jax import lax
from jax.experimental import pallas as pl
from jax.experimental.pallas import tpu as pltpu
from jax.sharding import Mesh
from jax.sharding import PartitionSpec as P

QUERY_HEADS = 64
KEY_HEADS = 8
HEAD_WIDTH = 128
ADAPTER_RANK = 64
QUERY_LENGTH = 8
ADAPTER_SCALE = 0.5
CAP = 2
PLANES = 8
HOP_CAP = 10
TOK = ("z", "p")
ROW_BLOCK = 16
LOG2_E = math.log2(math.e)
VMEM_LIMIT = 56 * 1024 * 1024

_VMEM = pl.BlockSpec(memory_space=pltpu.VMEM)
_SMEM = pl.BlockSpec(memory_space=pltpu.SMEM)
_ANY = pl.BlockSpec(memory_space=pl.ANY)


def params():
    return pltpu.CompilerParams(vmem_limit_bytes=VMEM_LIMIT)


def fold(products, mask):
    kept = products * mask.astype(jnp.float32)
    half = kept[:, :128] + kept[:, 128:]
    return half + pltpu.roll(half, 64, 1)


def low_half(shape):
    return lax.broadcasted_iota(jnp.int32, shape, 1) < 64


def all_rows(refs):
    parts = [r[...] for r in refs]
    return parts[0] if len(parts) == 1 else jnp.concatenate(parts, axis=0)


def project_kernel(weight_ref, mask_ref, *refs):
    x_refs, out_ref, total_ref = refs[:-2], refs[-2], refs[-1]
    step = pl.program_id(0)
    product = lax.dot_general(
        all_rows(x_refs),
        weight_ref[...],
        (((1,), (1,)), ((), ())),
        preferred_element_type=jnp.float32,
    )

    @pl.when(step == 0)
    def _():
        total_ref[...] = product

    @pl.when(step > 0)
    def _():
        total_ref[...] += product

    @pl.when(step == pl.num_programs(0) - 1)
    def _():
        half = out_ref.shape[0]
        both = jnp.where(
            low_half(out_ref.shape),
            fold(total_ref[:half], mask_ref[:half]),
            fold(total_ref[half:], mask_ref[half:]),
        )
        out_ref[...] = both.astype(out_ref.dtype)


def column_blocks(parts, block):
    return [pl.BlockSpec((x.shape[0], block), lambda i: (0, i)) for x in parts]


def project(parts, mask, weight, out_type, piece=0):
    tokens = sum(x.shape[0] for x in parts)
    ranks, width = weight.shape
    block = 1024
    return pl.pallas_call(
        project_kernel,
        grid=(width // block,),
        in_specs=[
            pl.BlockSpec((ranks, block), lambda i: (0, i)),
            pl.BlockSpec((tokens, ranks), lambda i: (piece, 0)),
        ]
        + column_blocks(parts, block),
        out_specs=pl.BlockSpec((tokens // 2, 128), lambda i: (0, 0)),
        out_shape=jax.ShapeDtypeStruct((tokens // 2, 128), out_type),
        scratch_shapes=[pltpu.VMEM((tokens, ranks), jnp.float32)],
        compiler_params=params(),
        name="project",
    )(weight, mask, *parts)


def spread_of(packed, mask, is_low):
    low = low_half(packed.shape)
    turned = pltpu.roll(packed, 64, 1)
    twice = jnp.where(low, packed, turned) if is_low else jnp.where(low, turned, packed)
    return (jnp.concatenate([twice, twice], axis=1) * mask.astype(jnp.float32)).astype(
        jnp.bfloat16
    )


def delta_kernel(p0, p1, p2, p3, mask_ref, weight_ref, *refs):
    out_refs, spread_ref = refs[:-1], refs[-1]
    half = p0.shape[0]

    @pl.when(pl.program_id(0) == 0)
    def _():
        total = (p0[...].astype(jnp.float32) + p1[...].astype(jnp.float32)) + (
            p2[...].astype(jnp.float32) + p3[...].astype(jnp.float32)
        )
        low_rank = total.astype(jnp.bfloat16).astype(jnp.float32)
        spread_ref[:half] = spread_of(low_rank, mask_ref[:half], True)
        spread_ref[half:] = spread_of(low_rank, mask_ref[half:], False)

    delta = (
        ADAPTER_SCALE
        * jnp.dot(spread_ref[...], weight_ref[...], preferred_element_type=jnp.float32)
    ).astype(jnp.bfloat16)
    at = 0
    for out_ref in out_refs:
        out_ref[...] = delta[at : at + out_ref.shape[0]]
        at += out_ref.shape[0]


def make_delta(sums, mask, weight, count):
    half = sums[0].shape[0]
    tokens = 2 * half
    ranks, width = weight.shape
    block = 1024
    outs = [jax.ShapeDtypeStruct((tokens // count, width), jnp.bfloat16)] * count
    *parts, spread = pl.pallas_call(
        delta_kernel,
        grid=(width // block,),
        in_specs=[pl.BlockSpec((half, 128), lambda i: (0, 0))] * 4
        + [
            pl.BlockSpec((tokens, ranks), lambda i: (0, 0)),
            pl.BlockSpec((ranks, block), lambda i: (0, i)),
        ],
        out_specs=column_blocks(outs, block)
        + [pl.BlockSpec((tokens, ranks), lambda i: (0, 0))],
        out_shape=outs + [jax.ShapeDtypeStruct((tokens, ranks), jnp.bfloat16)],
        compiler_params=params(),
        name="make_delta",
    )(*sums, mask, weight)
    return parts, spread


def grad_up_kernel(spread_ref, *refs):
    out_ref = refs[-1]
    out_ref[...] = (
        ADAPTER_SCALE
        * lax.dot_general(
            spread_ref[...],
            all_rows(refs[:-1]),
            (((0,), (0,)), ((), ())),
            preferred_element_type=jnp.float32,
        )
    ).astype(out_ref.dtype)


def grad_up(spread, parts):
    tokens, ranks = spread.shape
    width = parts[0].shape[1]
    block = 1024
    return pl.pallas_call(
        grad_up_kernel,
        grid=(width // block,),
        in_specs=[pl.BlockSpec((tokens, ranks), lambda i: (0, 0))] + column_blocks(parts, block),
        out_specs=pl.BlockSpec((ranks, block), lambda i: (0, i)),
        out_shape=jax.ShapeDtypeStruct((ranks, width), jnp.bfloat16),
        compiler_params=params(),
        name="grad_up",
    )(spread, *parts)


def grad_down_kernel(mask_ref, *refs, pieces):
    sums, x_refs, out_ref, spread_ref = refs[: 4 * pieces], refs[4 * pieces : -2], refs[-2], refs[-1]

    @pl.when(pl.program_id(0) == 0)
    def _():
        at = 0
        for n in range(pieces):
            p0, p1, p2, p3 = (r[...].astype(jnp.float32) for r in sums[4 * n : 4 * n + 4])
            total = (p0 + p1) + (p2 + p3)
            low_grad = (ADAPTER_SCALE * total).astype(jnp.bfloat16).astype(jnp.float32)
            for is_low in (True, False):
                tokens = slice(at, at + total.shape[0])
                spread_ref[tokens] = spread_of(low_grad, mask_ref[tokens], is_low)
                at += total.shape[0]

    out_ref[...] = lax.dot_general(
        spread_ref[...],
        all_rows(x_refs),
        (((0,), (0,)), ((), ())),
        preferred_element_type=jnp.float32,
    ).astype(out_ref.dtype)


def grad_down(sums, mask, parts):
    tokens, ranks = mask.shape
    width = parts[0].shape[1]
    block = 1024
    return pl.pallas_call(
        functools.partial(grad_down_kernel, pieces=len(sums)),
        grid=(width // block,),
        in_specs=[pl.BlockSpec((tokens, ranks), lambda i: (0, 0))]
        + [pl.BlockSpec(x.shape, lambda i: (0, 0)) for piece in sums for x in piece]
        + column_blocks(parts, block),
        out_specs=pl.BlockSpec((ranks, block), lambda i: (0, i)),
        out_shape=jax.ShapeDtypeStruct((ranks, width), jnp.bfloat16),
        scratch_shapes=[pltpu.VMEM((tokens, ranks), jnp.bfloat16)],
        compiler_params=params(),
        name="grad_down",
    )(mask, *(x for piece in sums for x in piece), *parts)


def heads_first(x, head_group):
    return jnp.concatenate(
        [x[:, h * HEAD_WIDTH : (h + 1) * HEAD_WIDTH] for h in range(head_group)], axis=0
    )


def by_rows(a, b):
    return lax.dot_general(a, b, (((1,), (1,)), ((), ())), preferred_element_type=jnp.float32)


def times(a, b):
    return jnp.dot(a, b, preferred_element_type=jnp.float32)


def attend_group(query, base, own_keys, own_values, keys, values, shared_seen, own_seen, weight):
    tokens = own_keys.shape[0]
    head_group = query.shape[1] // HEAD_WIDTH
    inv_root = 1.0 / math.sqrt(HEAD_WIDTH)
    query = heads_first(query, head_group).astype(jnp.bfloat16)
    base = heads_first(base, head_group)

    def group(x):
        return x.reshape(head_group, tokens, x.shape[-1])

    def flat(x):
        return x.reshape(head_group * tokens, x.shape[-1])

    shared = jnp.where(shared_seen[None], group(by_rows(query, keys)), -1e30)
    own = jnp.where(own_seen[None], group(by_rows(query, own_keys)), -1e30)
    top = jnp.maximum(
        jnp.max(shared, axis=-1, keepdims=True), jnp.max(own, axis=-1, keepdims=True)
    )
    shared = flat(jnp.exp2((shared - top) * (inv_root * LOG2_E)))
    own = flat(jnp.exp2((own - top) * (inv_root * LOG2_E)))
    total = jnp.sum(shared, axis=-1, keepdims=True) + jnp.sum(own, axis=-1, keepdims=True)
    scale = 1.0 / total
    attn_out = scale * (
        times(shared.astype(jnp.bfloat16), values) + times(own.astype(jnp.bfloat16), own_values)
    )
    grad_out = flat(group(attn_out - base) * weight[None]).astype(jnp.bfloat16)
    inner = jnp.sum(grad_out.astype(jnp.float32) * attn_out, axis=-1, keepdims=True)
    shared_gs = (shared * (by_rows(grad_out, values) - inner)).astype(jnp.bfloat16)
    own_gs = (own * (by_rows(grad_out, own_values) - inner)).astype(jnp.bfloat16)
    return (scale * inv_root) * (times(shared_gs, keys) + times(own_gs, own_keys))


def attend_block(b, load, delta_ref, grad_ref, key_ref, value_ref, vectors):
    row_len_ref, row_prompt_ref, row_weight_ref, key_prompt_ref, key_place_ref = vectors
    length = QUERY_LENGTH
    head_group = QUERY_HEADS // KEY_HEADS
    group_width = head_group * HEAD_WIDTH
    block_tokens = ROW_BLOCK * length
    block = pl.ds(b * ROW_BLOCK, ROW_BLOCK)
    tokens = pl.ds(b * block_tokens, block_tokens)
    shared_seen = (row_prompt_ref[tokens, :] == key_prompt_ref[...]) & (
        key_place_ref[...] < row_len_ref[tokens, :]
    )
    own_shape = (block_tokens, block_tokens)
    q_at = lax.broadcasted_iota(jnp.int32, own_shape, 0)
    k_at = lax.broadcasted_iota(jnp.int32, own_shape, 1)
    own_seen = (q_at // length == k_at // length) & (k_at <= q_at)
    weight = row_weight_ref[tokens, :]

    def two_d(x):
        return x.astype(jnp.float32).reshape(block_tokens, x.shape[-1])

    for g in range(key_ref.shape[1] // HEAD_WIDTH):
        columns = slice(g * group_width, (g + 1) * group_width)
        keys_at = slice(g * HEAD_WIDTH, (g + 1) * HEAD_WIDTH)
        gradient = attend_group(
            two_d(load("query", block, columns)) + two_d(delta_ref[block, :, columns]),
            two_d(load("base", block, columns)),
            two_d(load("key", block, keys_at)).astype(jnp.bfloat16),
            two_d(load("value", block, keys_at)).astype(jnp.bfloat16),
            key_ref[:, keys_at],
            value_ref[:, keys_at],
            shared_seen,
            own_seen,
            weight,
        )
        for h in range(head_group):
            piece = gradient[h * block_tokens : (h + 1) * block_tokens]
            at = g * group_width + h * HEAD_WIDTH
            grad_ref[block, :, at : at + HEAD_WIDTH] = piece.reshape(
                ROW_BLOCK, length, HEAD_WIDTH
            ).astype(jnp.bfloat16)


def attend_home_kernel(
    target_ref,
    query_ref,
    base_ref,
    own_key_ref,
    own_value_ref,
    key_ref,
    value_ref,
    row_len_ref,
    row_prompt_ref,
    row_weight_ref,
    key_prompt_ref,
    key_place_ref,
    delta_hbm,
    out_hbm,
    delta_ref,
    grad_ref,
    in_sem,
    out_sem,
):
    rows = query_ref.shape[0]
    refs = {"query": query_ref, "base": base_ref, "key": own_key_ref, "value": own_value_ref}
    vectors = (row_len_ref, row_prompt_ref, row_weight_ref, key_prompt_ref, key_place_ref)

    def fetch(r):
        return pltpu.make_async_copy(delta_hbm.at[target_ref[r]], delta_ref.at[r], in_sem.at[r])

    def send(r):
        return pltpu.make_async_copy(grad_ref.at[r], out_hbm.at[target_ref[r]], out_sem.at[r])

    for r in range(rows):
        fetch(r).start()
    for r in range(rows):
        fetch(r).wait()

    def load(name, block, columns):
        return refs[name][block, :, columns]

    def one_block(b, carry):
        attend_block(b, load, delta_ref, grad_ref, key_ref, value_ref, vectors)
        return carry

    lax.fori_loop(0, rows // ROW_BLOCK, one_block, 0)
    for r in range(rows):
        send(r).start()
    for r in range(rows):
        send(r).wait()


def attend_home(target, query, base, own_key, own_value, keys, values, per_token, per_key, delta):
    rows, length, width = query.shape
    return pl.pallas_call(
        attend_home_kernel,
        in_specs=[_SMEM] + [_VMEM] * 11 + [_ANY],
        out_specs=_ANY,
        out_shape=jax.ShapeDtypeStruct(delta.shape, delta.dtype),
        scratch_shapes=[
            pltpu.VMEM((rows, length, width), jnp.bfloat16),
            pltpu.VMEM((rows, length, width), jnp.bfloat16),
            pltpu.SemaphoreType.DMA((rows,)),
            pltpu.SemaphoreType.DMA((rows,)),
        ],
        input_output_aliases={12: 0},
        compiler_params=params(),
        name="attend_home",
    )(
        target,
        query,
        base,
        own_key,
        own_value,
        keys,
        values,
        *per_token,
        *per_key,
        delta,
    )


def each(first, last, do):
    def step(i, carry):
        do(i)
        return carry

    lax.fori_loop(first, last, step, 0)


def attend_middle_kernel(*refs, count, names):
    place_ref, seated_ref, total_ref = refs[:3]
    refs = refs[3:]
    payload_hbm, refs = refs[: len(names)], refs[len(names) :]
    key_ref, value_ref = refs[:2]
    vectors, refs = refs[2:7], refs[7:]
    delta_hbm, out_hbm, refs = refs[:count], refs[count : 2 * count], refs[2 * count :]
    payload_refs, refs = refs[: len(names)], refs[len(names) :]
    delta_ref, grad_ref, in_sem, delta_sem, out_sem = refs
    slots = payload_hbm[0].shape[0]
    seats = delta_hbm[0].shape[0]
    total = total_ref[0]
    blocks = (total + ROW_BLOCK - 1) // ROW_BLOCK
    where = {name: (n, at) for n, held in enumerate(names) for name, at in held}

    def fetch(do):
        def step(h):
            row = place_ref[h]

            @pl.when(row >= 0)
            def _():
                for n in range(len(names)):
                    do(
                        pltpu.make_async_copy(
                            payload_hbm[n].at[h], payload_refs[n].at[row], in_sem.at[h, n]
                        )
                    )

        each(0, slots, step)

    def seat(copy, do):
        for k in range(count):

            def step(j, k=k):
                row = seated_ref[k * seats + j]

                @pl.when(row >= 0)
                def _():
                    do(copy(k, j, row))

            each(0, seats, step)

    def fetch_delta(k, j, row):
        return pltpu.make_async_copy(
            delta_hbm[k].at[j], delta_ref.at[row], delta_sem.at[k * seats + j]
        )

    def send(k, j, row):
        return pltpu.make_async_copy(
            grad_ref.at[row], out_hbm[k].at[j], out_sem.at[k * seats + j]
        )

    def start(copy):
        copy.start()

    def wait(copy):
        copy.wait()

    fetch(start)
    seat(fetch_delta, start)

    def clear(i):
        for ref in payload_refs + (delta_ref,):
            ref[i] = jnp.zeros_like(ref[i])

    each(total, blocks * ROW_BLOCK, clear)
    fetch(wait)
    seat(fetch_delta, wait)

    def load(name, block, columns):
        n, at = where[name]
        return payload_refs[n][block, :, at + columns.start : at + columns.stop]

    each(
        0,
        blocks,
        lambda b: attend_block(b, load, delta_ref, grad_ref, key_ref, value_ref, vectors),
    )
    seat(send, start)
    seat(send, wait)


def attend_middle(place, seated, total, payload, names, keys, values, per_row, per_key, delta):
    slots, length = payload[0].shape[:2]
    seats, _, width = delta[0].shape
    count = len(delta)
    rows = slots + (-slots) % ROW_BLOCK
    first_delta = 3 + len(payload) + 7
    return pl.pallas_call(
        functools.partial(attend_middle_kernel, count=count, names=names),
        in_specs=[_SMEM] * 3 + [_ANY] * len(payload) + [_VMEM] * 7 + [_ANY] * count,
        out_specs=[_ANY] * count,
        out_shape=[jax.ShapeDtypeStruct(x.shape, x.dtype) for x in delta],
        scratch_shapes=[pltpu.VMEM((rows, length, x.shape[2]), x.dtype) for x in payload]
        + [
            pltpu.VMEM((rows, length, width), jnp.bfloat16),
            pltpu.VMEM((rows, length, width), jnp.bfloat16),
            pltpu.SemaphoreType.DMA((slots, len(payload))),
            pltpu.SemaphoreType.DMA((count * seats,)),
            pltpu.SemaphoreType.DMA((count * seats,)),
        ],
        input_output_aliases={first_delta + k: k for k in range(count)},
        compiler_params=params(),
        name="attend_middle",
    )(place, seated, total, *payload, keys, values, *per_row, *per_key, *delta)


def deal_kernel(source_ref, *refs, count, parts, fill):
    inputs, outs, zero_ref, sem = refs[:count], refs[count : count + parts], refs[-2], refs[-1]
    size = outs[0].shape[0]
    if fill:
        zero_ref[...] = jnp.zeros_like(zero_ref)

    def copies(do):
        for k, out in enumerate(outs):

            def step(j, k=k, out=out):
                slot = k * size + j
                row = source_ref[slot]

                @pl.when(row >= 0)
                def _():
                    at = 0
                    for n, x in enumerate(inputs):
                        width = x.shape[-1]
                        to = out.at[j] if count == 1 else out.at[j, :, pl.ds(at, width)]
                        do(pltpu.make_async_copy(x.at[row], to, sem.at[slot, n]))
                        at += width

                if fill:

                    @pl.when(row < 0)
                    def _():
                        do(pltpu.make_async_copy(zero_ref, out.at[j], sem.at[slot, 0]))

            each(0, size, step)

    copies(lambda copy: copy.start())
    copies(lambda copy: copy.wait())


def deal(source, arrays, parts, fill):
    length = arrays[0].shape[1]
    width = sum(x.shape[2] for x in arrays)
    slots = source.shape[0]
    return pl.pallas_call(
        functools.partial(deal_kernel, count=len(arrays), parts=parts, fill=fill),
        in_specs=[_SMEM] + [_VMEM] * len(arrays),
        out_specs=[_ANY] * parts,
        out_shape=[jax.ShapeDtypeStruct((slots // parts, length, width), arrays[0].dtype)] * parts,
        scratch_shapes=[
            pltpu.VMEM((length, width), jnp.bfloat16),
            pltpu.SemaphoreType.DMA((slots, len(arrays))),
        ],
        compiler_params=params(),
        name="deal",
    )(source, *arrays)


def shifted(block_for, count):
    return [
        lax.ppermute(block_for(k), "kv", [(i, (i + k) % count) for i in range(count)])
        for k in range(1, count)
    ]


def before(same):
    at = jnp.arange(same.shape[-1], dtype=jnp.int32)
    return jnp.sum((same & (at[:, None] > at[None, :])).astype(jnp.int32), axis=-1)


def look_up(keys, wanted, values):
    return jnp.sum(jnp.where(keys[None, :] == wanted[:, None], values[None, :] + 1, 0), axis=1)


def adapter_mask(slot_adapter, adapters):
    slots = slot_adapter.shape[0]
    lane_adapter = jnp.arange(adapters * ADAPTER_RANK, dtype=jnp.int32) // ADAPTER_RANK + 1
    return jnp.broadcast_to(
        (slot_adapter[:, None] == lane_adapter[None, :]).astype(jnp.bfloat16)[:, None, :],
        (slots, QUERY_LENGTH, lane_adapter.shape[0]),
    ).reshape(slots * QUERY_LENGTH, lane_adapter.shape[0])


def gather_caches(prompt_key_cache, prompt_value_cache):
    kv_count = lax.axis_size("kv")
    kv = lax.axis_index("kv")
    prompts, place_local = prompt_key_cache.shape[:2]
    head_columns = prompt_key_cache.shape[2] // kv_count
    both = jnp.stack([prompt_key_cache, prompt_value_cache]).reshape(
        2 * prompts * place_local, kv_count, head_columns
    )

    def cache_block(k):
        return lax.dynamic_index_in_dim(both, (kv + k) % kv_count, 1, keepdims=False)

    cache = jnp.stack([cache_block(0)] + shifted(cache_block, kv_count)).reshape(
        kv_count, 2, prompts * place_local, head_columns
    )
    key_at = jnp.arange(kv_count * prompts * place_local, dtype=jnp.int32)
    key_from = (kv - key_at // (prompts * place_local) + kv_count) % kv_count
    key_prompt = key_at // place_local % prompts
    key_place = key_from * place_local + key_at % place_local
    return (
        cache[:, 0].reshape(-1, head_columns),
        cache[:, 1].reshape(-1, head_columns),
        (key_prompt.reshape(1, -1), key_place.reshape(1, -1)),
    )


def per_token(x):
    return jnp.repeat(x, QUERY_LENGTH).reshape(-1, 1)


def as_rows(x):
    return x.reshape(x.shape[0] // QUERY_LENGTH, QUERY_LENGTH, x.shape[1])


def owner_forward(token_parts, mask, down_flat, up_flat):
    part = project(token_parts, mask, down_flat, jnp.bfloat16)
    sums = [part] + shifted(lambda k: part, lax.axis_size("kv"))
    return make_delta(sums, mask, up_flat, len(token_parts))


def owner_backward(gradient_pieces, token_parts, mask, spread, up_flat):
    kv_count = lax.axis_size("kv")
    sums = []
    for n, parts in enumerate(gradient_pieces):
        part = project(parts, mask, up_flat, jnp.bfloat16, piece=n)
        sums.append([part] + shifted(lambda k, part=part: part, kv_count))
    gradient = [x for parts in gradient_pieces for x in parts]
    return grad_down(sums, mask, token_parts), grad_up(spread, gradient)


def one_hop(
    tokens,
    frozen_query,
    trained_keys,
    trained_values,
    frozen_output,
    prompt_key_cache,
    prompt_value_cache,
    adapter_down,
    adapter_up,
    row_adapter_index,
    row_forget_flag,
    row_prompt_index,
    row_prompt_length,
):
    tok_count = lax.axis_size(TOK)
    me = lax.axis_index(TOK)
    rows = tokens.shape[0] // QUERY_LENGTH
    width = tokens.shape[1]
    adapters = adapter_down.shape[0]
    slots = tok_count * CAP
    down_flat = adapter_down.reshape(adapters * ADAPTER_RANK, width)
    up_flat = adapter_up.reshape(adapters * ADAPTER_RANK, width)

    mine = lax.dynamic_slice_in_dim(row_adapter_index, me * rows, rows) // adapters
    target = mine * CAP + before(mine[:, None] == mine[None, :])
    source = (
        look_up(
            target, jnp.arange(slots, dtype=jnp.int32), jnp.arange(rows, dtype=jnp.int32)
        )
        - 1
    )

    def exchange(x):
        return lax.all_to_all(x, TOK, split_axis=0, concat_axis=0, tiled=True)

    token_parts = [
        exchange(deal(source, [as_rows(tokens)], 1, True)[0]).reshape(-1, width)
    ]

    hit = (row_adapter_index // adapters).reshape(tok_count, rows) == me
    rank = before(jnp.broadcast_to(hit[:, None, :], (tok_count, rows, rows)))
    local_adapter = (row_adapter_index % adapters).reshape(tok_count, rows)
    slot_adapter = jnp.sum(
        jnp.where(
            hit[:, None, :]
            & (rank[:, None, :] == jnp.arange(CAP, dtype=jnp.int32)[None, :, None]),
            local_adapter[:, None, :] + 1,
            0,
        ),
        axis=2,
    ).reshape(slots)
    mask = adapter_mask(slot_adapter, adapters)
    keys, values, per_key = gather_caches(prompt_key_cache, prompt_value_cache)

    def of_mine(x):
        return lax.dynamic_slice_in_dim(x, me * rows, rows)

    (delta,), spread = owner_forward(token_parts, mask, down_flat, up_flat)
    gradient = attend_home(
        target,
        as_rows(frozen_query),
        as_rows(frozen_output),
        as_rows(trained_keys),
        as_rows(trained_values),
        keys,
        values,
        (
            per_token(of_mine(row_prompt_length)),
            per_token(of_mine(row_prompt_index)),
            per_token(1.0 - 2.0 * of_mine(row_forget_flag).astype(jnp.float32)),
        ),
        per_key,
        exchange(delta.reshape(slots, QUERY_LENGTH, width)),
    )
    down, up = owner_backward(
        [[exchange(gradient).reshape(-1, width)]], token_parts, mask, spread, up_flat
    )
    return down.reshape(adapter_down.shape), up.reshape(adapter_up.shape)


def two_hops(
    tokens,
    frozen_query,
    trained_keys,
    trained_values,
    frozen_output,
    prompt_key_cache,
    prompt_value_cache,
    adapter_down,
    adapter_up,
    row_adapter_index,
    row_forget_flag,
    row_prompt_index,
    row_prompt_length,
    *,
    cap,
):
    planes = lax.axis_size("z")
    places = lax.axis_size("p")
    z = lax.axis_index("z")
    p = lax.axis_index("p")
    rows = tokens.shape[0] // QUERY_LENGTH
    width = tokens.shape[1]
    adapters = adapter_down.shape[0]
    seats = planes * CAP
    most = planes * cap
    down_flat = adapter_down.reshape(adapters * ADAPTER_RANK, width)
    up_flat = adapter_up.reshape(adapters * ADAPTER_RANK, width)
    row_at = jnp.arange(rows, dtype=jnp.int32)
    plane_at = jnp.arange(planes, dtype=jnp.int32)
    place_at = jnp.arange(places, dtype=jnp.int32)
    most_at = jnp.arange(most, dtype=jnp.int32)

    mine = lax.dynamic_slice_in_dim(row_adapter_index, (z * places + p) * rows, rows) // adapters
    my_plane = mine // places
    my_slot = my_plane * cap + before(my_plane[:, None] == my_plane[None, :])
    source = look_up(my_slot, most_at, row_at) - 1

    def dealt(*arrays):
        return deal(source, [as_rows(x) for x in arrays], 1, False)[0]

    def along_z(x):
        return lax.all_to_all(x, "z", split_axis=0, concat_axis=0, tiled=True)

    assert places == 8

    def steps(n):
        return n % 2 * 2 + n // 2

    def partner(place, k):
        return (place // 2 + steps(k // 2)) % 4 * 2 + (place + k) % 2

    def in_plane(parts, first=0, back=False):
        out = []
        for k, part in enumerate(parts, first):
            pairs = [(i, partner(i, k)) for i in range(places)]
            if k:
                part = lax.ppermute(part, "p", [(j, i) if back else (i, j) for i, j in pairs])
            out.append(part)
        return out

    def part_of(place):
        return steps((place // 2 - p // 2 + 4) % 4) * 2 + (place + p) % 2

    sent = dealt(tokens)
    moved_tokens = along_z(sent)

    def of_column(x):
        return lax.dynamic_index_in_dim(x.reshape(planes, places, rows), p, 1, keepdims=False)

    owner = of_column(row_adapter_index) // adapters
    hit = owner // places == z
    hop_slot = (plane_at * cap)[:, None] + before(
        jnp.broadcast_to(hit[:, None, :], (planes, rows, rows))
    )
    seat = (
        part_of(owner % places) * seats
        + plane_at[:, None] * CAP
        + before(owner[:, :, None] == owner[:, None, :])
    )
    hop_slot = jnp.where(hit, hop_slot, -1).reshape(-1)
    seat = jnp.where(hit, seat, -1).reshape(-1)
    seat_slot = look_up(seat, jnp.arange(places * seats, dtype=jnp.int32), hop_slot) - 1
    cut = places // 2
    row_key = jnp.arange(most + (-most) % ROW_BLOCK, dtype=jnp.int32)

    def attend_tables(first, last):
        low, high = first * seats, last * seats
        here = (seat >= low) & (seat < high)
        packed = jnp.where(
            here, before(jnp.broadcast_to(here[None, :], (planes * rows,) * 2)), -1
        )

        def of_rows(x):
            return look_up(packed, row_key, of_column(x).reshape(-1)) - 1

        return (
            look_up(jnp.where(here, hop_slot, -1), most_at, packed) - 1,
            look_up(seat, jnp.arange(low, high, dtype=jnp.int32), packed) - 1,
            jnp.sum(here.astype(jnp.int32)).reshape(1),
            (
                per_token(of_rows(row_prompt_length)),
                per_token(of_rows(row_prompt_index)),
                per_token(1.0 - 2.0 * of_rows(row_forget_flag).astype(jnp.float32)),
            ),
        )

    tables = (attend_tables(0, cut), attend_tables(cut, places))

    def by_seat(x):
        homes = x.reshape(planes, places, rows)
        from_place = (p // 2 - steps(place_at // 2) + 4) % 4 * 2 + (p + place_at) % 2
        pick = from_place[:, None] == place_at[None, :]
        return jnp.sum(
            jnp.where(pick[:, None, :, None], homes[None], 0), axis=2
        ).reshape(planes * places, rows)

    adapter_by_seat = by_seat(row_adapter_index)
    here = adapter_by_seat // adapters == z * places + p
    rank = before(jnp.broadcast_to(here[:, None, :], (planes * places, rows, rows)))
    slot_adapter = jnp.sum(
        jnp.where(
            here[:, None, :]
            & (rank[:, None, :] == jnp.arange(CAP, dtype=jnp.int32)[None, :, None]),
            (adapter_by_seat % adapters)[:, None, :] + 1,
            0,
        ),
        axis=2,
    ).reshape(places * seats)
    payload = dealt(frozen_query, frozen_output, trained_keys, trained_values)
    kv_width = trained_keys.shape[1]
    names = (
        ("query", 0),
        ("base", width),
        ("key", 2 * width),
        ("value", 2 * width + kv_width),
    )
    mask = adapter_mask(slot_adapter, adapters)
    caches = gather_caches(
        *lax.optimization_barrier((prompt_key_cache, prompt_value_cache, sent))[:2]
    )
    moved_tokens, payload, mask, caches, seat_slot, tables = lax.optimization_barrier(
        (moved_tokens, payload, mask, caches, seat_slot, tables)
    )
    keys, values, per_key = caches

    payload = along_z(payload)
    token_parts = [
        x.reshape(-1, width) for x in in_plane(deal(seat_slot, [moved_tokens], places, True))
    ]

    delta, spread = owner_forward(token_parts, mask, down_flat, up_flat)
    delta = in_plane([x.reshape(seats, QUERY_LENGTH, width) for x in delta], back=True)

    def attend(part_delta, part_tables):
        slot_row, seat_row, total, per_row = part_tables
        return attend_middle(
            slot_row,
            seat_row,
            total,
            (payload,),
            (names,),
            keys,
            values,
            per_row,
            per_key,
            part_delta,
        )

    early = attend(delta[:cut], tables[0])
    late_delta, early = lax.optimization_barrier((delta[cut:], early))
    gradient = in_plane(early) + in_plane(attend(late_delta, tables[1]), first=cut)
    gradient = [x.reshape(-1, width) for x in gradient]
    down, up = owner_backward(
        [gradient[:cut], gradient[cut:]], token_parts, mask, spread, up_flat
    )
    return down.reshape(adapter_down.shape), up.reshape(adapter_up.shape)


def per_device(*arrays):
    row_adapter_index = arrays[9]
    adapters = arrays[7].shape[0]
    planes = lax.axis_size("z")
    places = lax.axis_size("p")
    plane = (row_adapter_index // (adapters * places)).reshape(planes * places, -1)
    load = jnp.sum(
        (plane[:, None, :] == jnp.arange(planes, dtype=jnp.int32)[None, :, None]).astype(
            jnp.int32
        ),
        axis=2,
    )
    return lax.cond(
        jnp.max(load) > HOP_CAP,
        one_hop,
        functools.partial(two_hops, cap=HOP_CAP),
        *arrays,
    )


def solution(mesh):
    tok_count, kv_count = mesh.devices.shape
    grid = Mesh(mesh.devices.reshape(PLANES, tok_count // PLANES, kv_count), ("z", "p", "kv"))
    return jax.shard_map(
        per_device,
        mesh=grid,
        in_specs=(
            P(TOK, "kv"),
            P(TOK, "kv"),
            P(TOK, "kv"),
            P(TOK, "kv"),
            P(TOK, "kv"),
            P(None, "kv", None),
            P(None, "kv", None),
            P(TOK, None, "kv"),
            P(TOK, None, "kv"),
            P(),
            P(),
            P(),
            P(),
        ),
        out_specs=(P(TOK, None, "kv"), P(TOK, None, "kv")),
        check_vma=False,
    )
```
